128 devices in a mesh: req: 32 (over x, y, z_hi), rep: 4 (over z_lo, core).
Axes of the slice: x: 4, y: 4, z: 4 (z_hi: 2, z_lo: 2; z = z_hi * 2 + z_lo), core: 2. Of those that a mesh axis runs over, the one named last changes fastest.
Arguments:
- tokens: bfloat16 [128, 2, 2048], P('req'), may hold values from -6 to 6
- norm_gains: float32 [2, 2048], replicated, may hold values from 0.1 to 1.9
- w_kv: bfloat16 [2048, 2, 2048], P(None, None, 'rep'), may hold values from -0.125 to 0.125
- w_query: bfloat16 [32, 2048, 512], P('req', None, 'rep'), may hold values from -0.125 to 0.125
- w_out: bfloat16 [32, 512, 2048], P('req', 'rep'), may hold values from -0.5 to 0.5
- w_gate: bfloat16 [32, 2048, 1408], P('req', None, 'rep'), may hold values from -0.125 to 0.125
- w_up: bfloat16 [32, 2048, 1408], P('req', None, 'rep'), may hold values from -0.125 to 0.125
- w_down: bfloat16 [32, 1408, 2048], P('req', 'rep'), may hold values from -0.078125 to 0.078125
- kv_pages: bfloat16 [8192, 16, 2, 2048], P('req', None, None, 'rep'), may hold values from -80 to 80
- page_table: int32 [128, 64], P('req'), may hold values from 0 to 255, as said below
- cache_len: int32 [128], P('req'), may hold values from 1 to 1024
- route_ids: int32 [128, 2, 2, 2], P('req'), may hold values from 0 to 7, all different within a row
- route_gates: bfloat16 [128, 2, 2, 2], P('req'), may hold values from 0.19921875 to 1
- new_slot: int32 [128], P('req'), may hold values from 0 to 127, each once
Outputs:
- layer_out: bfloat16 [128, 2, 2048], P('req')
The draws below stay inside these ranges and needn't reach their ends.
Inputs may be any that keep to these rules, and one draw needn't show every extreme that they name: `page_table`: row i lists 64 distinct pages of the pool of the device that holds request i; two requests of one device share no page.
All inputs are finite; a program needn't handle non-finite values.
Results may differ from the reference program's by a relative error of at most 0.022.
Values may be sent and summed in bfloat16 or wider, within the bound.
No kernel may reach another device: no remote copies, remote signals or barrier semaphores. Data moves between devices by JAX's collectives and lax.ppermute only.
A program may use at most 128 MiB of HBM per device.

```python
import math
import jax
import jax.numpy as jnp
from jax import lax

D = 2048
H = 16
HD = 128
EXPERTS = 8
FFW = 5632
REQ_DEV = 4
PAGE = 16
MAXP = 64
PAGES_DEV = 256
HOLDERS = 4
REQUESTS = 128
POOL = 8192
N_REQ = 32
N_REP = 4


def draw_kv_pages(key, part):
    normal_key = jax.random.fold_in(key, 0)
    values = jnp.clip(jax.random.normal(normal_key, (POOL, PAGE, 2, H * HD), jnp.float32), -4.0, 4.0)
    return values.astype(jnp.bfloat16)


def draw_page_table(key, part):
    owners = REQUESTS // REQ_DEV
    orders = jax.vmap(lambda owner_key: jax.random.permutation(owner_key, PAGES_DEV))(jax.random.split(key, owners))
    return orders.reshape(REQUESTS, MAXP).astype(jnp.int32)


def draw_cache_len(key, part):
    subkeys = jax.random.split(key, 4)
    exponent = jax.random.randint(subkeys[0], (REQUESTS,), 4, 11)
    ceiling = jnp.left_shift(jnp.ones((REQUESTS,), jnp.int32), exponent)
    lengths = 1 + jax.random.randint(subkeys[1], (REQUESTS,), 0, ceiling)
    longest = jax.random.randint(subkeys[2], (), 0, REQUESTS)
    shortest = (longest + 1 + jax.random.randint(subkeys[3], (), 0, REQUESTS - 1)) % REQUESTS
    position = jnp.arange(REQUESTS, dtype=jnp.int32)
    lengths = jnp.minimum(lengths, MAXP * PAGE)
    lengths = jnp.where(position == longest, MAXP * PAGE, lengths)
    lengths = jnp.where(position == shortest, 1, lengths)
    return lengths.astype(jnp.int32)


def levels(rng, dims, shards, least, top_value):
    def one(dim, parts):
        draws = jax.random.uniform(jax.random.fold_in(jax.random.fold_in(rng, 6), dim), (parts,), jnp.float32, least / len(shards), top_value / len(shards))
        return jnp.repeat(jnp.exp(draws), dims[dim] // parts).reshape((-1,) + (1,) * (len(dims) - dim - 1))

    level = one(*shards[0])
    for cut in shards[1:]:
        level = level * one(*cut)
    return level


def different_ones(rng, rows, count, top, lift):
    ranking = jax.random.permutation(jax.random.fold_in(rng, 1), count)
    pull = ranking
    for power in range(3):
        pull = pull * pull // count
    pull = pull * lift // count
    lots = jax.random.randint(jax.random.fold_in(rng, 2), (rows, count), 0, 4096) + pull
    sure = jax.random.permutation(jax.random.fold_in(rng, 3), rows)[jnp.arange(count) % rows]
    lots = jnp.where(jnp.arange(rows)[:, None] == sure[None, :], 1 << 14, lots)
    score = lots * count + jnp.arange(count)
    return lax.top_k(score.astype(jnp.int32), top)[1].astype(jnp.int32)


def normal_values(own_key, extent, scale, bound, shards=(), kind=jnp.bfloat16):
    values = scale * jax.random.normal(own_key, extent, jnp.float32)
    if shards:
        values = values * levels(own_key, extent, shards, -0.22, 0.18)
    return jnp.clip(values, -bound, bound).astype(kind)


def setup_inputs(seed: int = 0) -> dict:
    key_of = jax.random.split(jax.random.key(seed), 15)
    tokens = normal_values(key_of[0], (REQUESTS, 2, D), 1.0, 6.0, ((0, 32),))
    norm_gains = jnp.clip(1.0 + 0.18 * jax.random.normal(key_of[1], (2, D), jnp.float32), 0.1, 1.9)
    w_kv = normal_values(key_of[2], (D, 2, H * HD), D ** -0.5, 0.125, ((2, 4),))
    w_query = normal_values(key_of[3], (EXPERTS * HOLDERS, D, H * HD // HOLDERS), D ** -0.5, 0.125, ((0, 32), (2, 4)))
    w_out = normal_values(key_of[4], (EXPERTS * HOLDERS, H * HD // HOLDERS, D), HD ** -0.5, 0.5, ((0, 32), (1, 4)))
    w_gate = normal_values(key_of[5], (EXPERTS * HOLDERS, D, FFW // HOLDERS), D ** -0.5, 0.125, ((0, 32), (2, 4)))
    w_up = normal_values(key_of[6], (EXPERTS * HOLDERS, D, FFW // HOLDERS), D ** -0.5, 0.125, ((0, 32), (2, 4)))
    w_down = normal_values(key_of[7], (EXPERTS * HOLDERS, FFW // HOLDERS, D), FFW ** -0.5, 0.078125, ((0, 32), (1, 4)))
    kv_pages = draw_kv_pages(jax.random.fold_in(key_of[14], 71), 0)
    page_table = draw_page_table(jax.random.fold_in(key_of[14], 71), 0)
    cache_len = draw_cache_len(jax.random.fold_in(key_of[14], 71), 0)
    route_ids = different_ones(key_of[11], REQUESTS * 2 * 2, EXPERTS, 2, 4096).reshape((REQUESTS, 2, 2, 2))
    route_gates = jnp.clip(0.19921875 + 0.80078125 * jax.random.uniform(key_of[12], (REQUESTS, 2, 2, 2), jnp.float32) ** levels(key_of[12], (REQUESTS, 2, 2, 2), ((0, 32),), -0.2, 0.2), 0.19921875, 1.0).astype(jnp.bfloat16)
    new_slot = jax.random.permutation(key_of[13], REQUESTS).astype(jnp.int32)
    return dict(tokens=tokens, norm_gains=norm_gains, w_kv=w_kv, w_query=w_query, w_out=w_out, w_gate=w_gate, w_up=w_up, w_down=w_down, kv_pages=kv_pages, page_table=page_table, cache_len=cache_len, route_ids=route_ids, route_gates=route_gates, new_slot=new_slot)


EPSILON = 1e-06
MASKED = -1e+30

def normalize(values, gain_row):
    scaling = lax.rsqrt(lax.optimization_barrier(jnp.mean(values * values, axis=-1, keepdims=True)) + EPSILON)
    return (values * scaling * gain_row).astype(jnp.bfloat16)

def attend(queries, cache_keys, cache_values, lengths, extra_keys, extra_values, extra_live):
    inv_scale = 1.0 / math.sqrt(queries.shape[-1])
    query_wide = queries.astype(jnp.float32)
    cache_scores = jnp.einsum('jskhc,jlhc->jskhl', query_wide, cache_keys.astype(jnp.float32)) * inv_scale
    alive_mask = jnp.arange(cache_keys.shape[1], dtype=jnp.int32)[None, :] < lengths[:, None]
    cache_scores = jnp.where(alive_mask[:, None, None, None, :], cache_scores, MASKED)
    extra_scores = jnp.einsum('jskhc,jxhc->jskhx', query_wide, extra_keys.astype(jnp.float32)) * inv_scale
    extra_scores = jnp.where(extra_live[None, :, None, None, :], extra_scores, MASKED)
    highest = jnp.maximum(lax.optimization_barrier(jnp.max(cache_scores, axis=-1)), lax.optimization_barrier(jnp.max(extra_scores, axis=-1)))[..., None]
    cache_exp = jnp.exp(cache_scores - highest)
    extra_exp = jnp.exp(extra_scores - highest)
    denominator = (lax.optimization_barrier(jnp.sum(cache_exp, axis=-1)) + lax.optimization_barrier(jnp.sum(extra_exp, axis=-1)))[..., None]
    cache_weight = (cache_exp / denominator).astype(jnp.bfloat16)
    extra_weight = (extra_exp / denominator).astype(jnp.bfloat16)
    mixture = jnp.einsum('jskhl,jlhc->jskhc', cache_weight.astype(jnp.float32), cache_values.astype(jnp.float32))
    mixture = mixture + jnp.einsum('jskhx,jxhc->jskhc', extra_weight.astype(jnp.float32), extra_values.astype(jnp.float32))
    return mixture.astype(jnp.bfloat16)

def reference(tokens, norm_gains, w_kv, w_query, w_out, w_gate, w_up, w_down, kv_pages, page_table, cache_len, route_ids, route_gates, new_slot):
    all_rows = tokens.shape[0]
    holders = N_REQ // EXPERTS
    heads_dev = H // (holders * N_REP)
    units_dev = FFW // (holders * N_REP)
    inner = H * HD
    query_full = w_query.reshape(EXPERTS, holders, D, N_REP, heads_dev * HD).transpose(0, 2, 3, 1, 4).reshape(EXPERTS, D, inner)
    out_full = w_out.reshape(EXPERTS, holders, N_REP, heads_dev * HD, D).transpose(0, 2, 1, 3, 4).reshape(EXPERTS, inner, D)
    gate_full = w_gate.reshape(EXPERTS, holders, D, N_REP, units_dev).transpose(0, 2, 1, 3, 4).reshape(EXPERTS, D, FFW)
    up_full = w_up.reshape(EXPERTS, holders, D, N_REP, units_dev).transpose(0, 2, 1, 3, 4).reshape(EXPERTS, D, FFW)
    down_full = w_down.reshape(EXPERTS, FFW, D)
    position = jnp.arange(all_rows, dtype=jnp.int32)
    inverse = jnp.zeros((all_rows,), jnp.int32).at[new_slot].set(position)
    inputs = tokens.astype(jnp.float32)
    normed = normalize(inputs, norm_gains[0])
    fresh = jnp.einsum('bsd,dtc->bstc', normed.astype(jnp.float32), w_kv.astype(jnp.float32)).astype(jnp.bfloat16)
    extra_kv = jnp.stack([fresh[:, 0], fresh[new_slot, 1]], axis=1)
    all_queries = jnp.einsum('bsd,edc->bsec', normed.astype(jnp.float32), query_full.astype(jnp.float32))
    experts_row = jnp.arange(EXPERTS, dtype=jnp.int32)
    attn_ids = route_ids[:, 0]
    chosen = (attn_ids[..., None] == experts_row).astype(jnp.float32)
    picked = jnp.einsum('bske,bsec->bskc', chosen, all_queries).astype(jnp.bfloat16)
    old_queries = jnp.stack([picked[:, 0], picked[new_slot, 1]], axis=1)
    tables = (position // REQ_DEV)[:, None] * PAGES_DEV + page_table
    extra_live = jnp.array([[True, False], [True, True]])

    def one_request(item):
        query_rows, table_row, length, extra_row = item
        block = kv_pages[table_row].reshape(-1, 2, H, HD)
        extra_row = extra_row.reshape(2, 2, H, HD)
        result = attend(query_rows.reshape(1, 2, 2, H, HD), block[None, :, 0], block[None, :, 1], length[None], extra_row[None, :, 0], extra_row[None, :, 1], extra_live)
        return result[0]
    outcome = lax.map(one_request, (old_queries, tables, cache_len, extra_kv))
    outcome = outcome.reshape(all_rows, 2, 2, inner)
    answers = jnp.stack([outcome[:, 0], outcome[inverse, 1]], axis=1)
    flat_answers = answers.reshape(-1, inner)
    attn_gates = route_gates[:, 0].astype(jnp.float32)
    mixture = jnp.zeros((all_rows, 2, D), jnp.float32)
    for expert in range(EXPERTS):
        projected = jnp.dot(flat_answers, out_full[expert], preferred_element_type=jnp.float32).reshape(all_rows, 2, 2, D)
        weight = jnp.where(attn_ids == expert, attn_gates, 0.0)
        mixture = mixture + lax.optimization_barrier(jnp.sum(projected * weight[..., None], axis=2))
    hidden = inputs + mixture
    hidden_normed = normalize(hidden, norm_gains[1]).reshape(-1, D)
    ffn_ids = route_ids[:, 1]
    ffn_gates = route_gates[:, 1].astype(jnp.float32)
    feed = jnp.zeros((all_rows, 2, D), jnp.float32)
    for expert in range(EXPERTS):
        gate_part = jnp.dot(hidden_normed, gate_full[expert], preferred_element_type=jnp.float32)
        up_part = jnp.dot(hidden_normed, up_full[expert], preferred_element_type=jnp.float32)
        active = (jax.nn.silu(gate_part) * up_part).astype(jnp.bfloat16)
        projected = jnp.dot(active, down_full[expert], preferred_element_type=jnp.float32).reshape(all_rows, 2, D)
        weight = lax.optimization_barrier(jnp.sum(jnp.where(ffn_ids == expert, ffn_gates, 0.0), axis=-1))
        feed = feed + projected * weight[..., None]
    return (hidden + feed).astype(jnp.bfloat16)
```

```python
import math

import jax
import jax.numpy as jnp
from jax import lax
from jax.sharding import PartitionSpec as P

HD = 128
EXPERTS = 8
EPSILON = 1e-06
MASKED = -1e30
F32 = jnp.float32
BF16 = jnp.bfloat16


def dot(a, b):
    return jnp.dot(a, b, preferred_element_type=F32)


def attend(queries, cache_keys, cache_values, lengths, extra_keys, extra_values, extra_live):
    inv_scale = 1.0 / math.sqrt(queries.shape[-1])
    cache_scores = (
        jnp.einsum("jskhc,jlhc->jskhl", queries, cache_keys, preferred_element_type=F32)
        * inv_scale
    )
    alive_mask = jnp.arange(cache_keys.shape[1], dtype=jnp.int32)[None, :] < lengths[:, None]
    cache_scores = jnp.where(alive_mask[:, None, None, None, :], cache_scores, MASKED)
    extra_scores = (
        jnp.einsum("jskhc,jxhc->jskhx", queries, extra_keys, preferred_element_type=F32)
        * inv_scale
    )
    extra_scores = jnp.where(extra_live[None, :, None, None, :], extra_scores, MASKED)
    highest = jnp.maximum(jnp.max(cache_scores, axis=-1), jnp.max(extra_scores, axis=-1))[..., None]
    cache_exp = jnp.exp(cache_scores - highest)
    extra_exp = jnp.exp(extra_scores - highest)
    denominator = (jnp.sum(cache_exp, axis=-1) + jnp.sum(extra_exp, axis=-1))[..., None]
    cache_weight = (cache_exp / denominator).astype(BF16)
    extra_weight = (extra_exp / denominator).astype(BF16)
    mixture = jnp.einsum("jskhl,jlhc->jskhc", cache_weight, cache_values, preferred_element_type=F32)
    mixture = mixture + jnp.einsum(
        "jskhx,jxhc->jskhc", extra_weight, extra_values, preferred_element_type=F32
    )
    return mixture.astype(BF16)


def shards(
    tokens,
    norm_gains,
    w_kv,
    w_query,
    w_out,
    w_gate,
    w_up,
    w_down,
    kv_pages,
    page_table,
    cache_len,
    route_ids,
    route_gates,
    new_slot,
):
    req_count = lax.axis_size("req")
    rep_count = lax.axis_size("rep")
    mine = tokens.shape[0]
    width = tokens.shape[-1]
    rows = 2 * mine
    total = rows * req_count
    holders = req_count // EXPERTS
    half = width // 2
    quarter = width // rep_count
    heads_rep = kv_pages.shape[-1] // HD
    rank = lax.axis_index("req")
    rep = lax.axis_index("rep")
    core = rep % 2
    swap = [(p, p ^ 1) for p in range(rep_count)]
    wide_groups = [
        [r * rep_count + 2 * z + c for r in range(req_count) for z in range(rep_count // 2)]
        for c in range(2)
    ]
    peers = req_count * rep_count // 2

    def spread_req(value):
        return lax.all_to_all(value, "req", split_axis=0, concat_axis=0, tiled=True)

    def spread_wide(value):
        return lax.all_to_all(
            value,
            ("req", "rep"),
            split_axis=0,
            concat_axis=0,
            tiled=True,
            axis_index_groups=wide_groups,
        )

    def other_core(value):
        return lax.ppermute(value, "rep", swap)

    def pick(value, index, axis):
        return lax.dynamic_index_in_dim(value, index, axis, keepdims=False)

    inputs = tokens.astype(F32).transpose(1, 0, 2).reshape(rows, width)
    scaling = lax.rsqrt(jnp.mean(inputs * inputs, axis=-1, keepdims=True) + EPSILON)
    normed = (inputs * scaling * norm_gains[0]).astype(BF16)
    own_pos = rank * rows + jnp.arange(mine, dtype=jnp.int32)
    moved_pos = (new_slot // mine) * rows + mine + new_slot % mine
    source = jnp.concatenate([own_pos, moved_pos])
    ids = route_ids.transpose(1, 2, 0, 3).reshape(2, rows, 2)
    gates = route_gates.astype(F32).transpose(1, 2, 0, 3).reshape(2, rows, 2)
    experts_row = jnp.arange(EXPERTS, dtype=jnp.int32)
    shares = jnp.sum(jnp.where(ids[..., None] == experts_row, gates[..., None], 0.0), axis=2)

    extras = jnp.concatenate([source[:, None], ids[0]], axis=1).astype(BF16)
    extras = jnp.pad(extras, ((0, 0), (0, HD - extras.shape[1])))
    message = jnp.concatenate(
        [lax.dynamic_slice_in_dim(normed, core * half, half, 1), extras], axis=1
    )
    gathered = spread_req(jnp.broadcast_to(message[None], (req_count,) + message.shape))
    gathered = gathered.reshape(total, half + HD)
    near, notes = gathered[:, :half], gathered[:, half:]
    far = other_core(near)

    wq = w_query[0].reshape(2, half, HD)
    queries = (dot(near, pick(wq, core, 0)) + dot(far, pick(wq, 1 - core, 0))).astype(BF16)
    order = (
        notes[:, :1].astype(jnp.int32) == jnp.arange(total, dtype=jnp.int32)[None, :]
    ).astype(BF16)
    ordered = dot(order, queries).astype(BF16)
    arrived = spread_req(ordered.reshape(req_count, rows, HD))

    own_order = lax.dynamic_slice_in_dim(order, rank * rows, rows, 0)
    own_ids = dot(own_order, notes)[:, 1:3].astype(jnp.int32)
    wkv = w_kv.reshape(2, half, 2 * heads_rep * HD)
    fresh = (
        dot(dot(own_order, near).astype(BF16), pick(wkv, core, 0))
        + dot(dot(own_order, far).astype(BF16), pick(wkv, 1 - core, 0))
    ).astype(BF16)
    extra = fresh.reshape(2, mine, 2, heads_rep, HD).transpose(1, 0, 2, 3, 4)

    chosen = (own_ids.reshape(2, mine, 2)[..., None] == experts_row).astype(BF16)
    arrived = arrived.reshape(EXPERTS, holders, 2, mine, HD)
    picked = jnp.einsum("sjke,ehsjc->jskhc", chosen, arrived, preferred_element_type=F32).astype(BF16)
    pages = kv_pages[page_table].reshape(mine, -1, 2, heads_rep, HD)
    extra_live = jnp.array([[True, False], [True, True]])
    result = attend(
        picked, pages[:, :, 0], pages[:, :, 1], cache_len, extra[:, :, 0], extra[:, :, 1], extra_live
    )
    back = jnp.einsum("sjke,jskhc->ehsjc", chosen, result, preferred_element_type=F32).astype(BF16)
    returned = spread_req(back.reshape(req_count, rows, HD)).reshape(total, HD)
    answers = lax.dot_general(
        order, returned, (((0,), (0,)), ((), ())), preferred_element_type=F32
    ).astype(BF16)

    def reduce_wide(partial, share):
        parts = partial.reshape(total, rep_count // 2, 2, quarter)
        theirs = other_core(pick(parts, 1 - core, 2).astype(BF16))
        summed = (pick(parts, core, 2) + theirs.astype(F32)).astype(BF16)
        summed = summed.reshape(req_count, rows, rep_count // 2, quarter).transpose(0, 2, 1, 3)
        got = spread_wide(summed.reshape(peers, rows, quarter))
        got = got.reshape(EXPERTS, peers // EXPERTS, rows, quarter).astype(F32)
        return jnp.sum(jnp.sum(got, axis=1) * share.T[:, :, None], axis=0)

    hidden = lax.dynamic_slice_in_dim(inputs, rep * quarter, quarter, 1) + reduce_wide(
        dot(answers, w_out[0]), shares[0]
    )
    block = spread_wide(jnp.broadcast_to(hidden.astype(BF16)[None], (peers, rows, quarter)))
    near = block.reshape(req_count, rep_count // 2, rows, quarter)
    far = other_core(near)
    near32, far32 = near.astype(F32), far.astype(F32)
    squares = jnp.sum(near32 * near32, axis=(1, 3)) + jnp.sum(far32 * far32, axis=(1, 3))
    scaling = lax.rsqrt(squares / width + EPSILON)[:, None, :, None]
    gain = norm_gains[1].reshape(rep_count // 2, 2, quarter)
    near_n = (near32 * scaling * pick(gain, core, 1)[None, :, None, :]).astype(BF16)
    far_n = (far32 * scaling * pick(gain, 1 - core, 1)[None, :, None, :]).astype(BF16)

    def project(weight):
        split = weight.reshape(rep_count // 2, 2, quarter, -1)
        return jnp.einsum(
            "rzbc,zcf->rbf", near_n, pick(split, core, 1), preferred_element_type=F32
        ) + jnp.einsum("rzbc,zcf->rbf", far_n, pick(split, 1 - core, 1), preferred_element_type=F32)

    units = (jax.nn.silu(project(w_gate[0])) * project(w_up[0])).astype(BF16)
    feed = reduce_wide(dot(units.reshape(total, -1), w_down[0]), shares[1])
    final = lax.all_gather((hidden + feed).astype(BF16), "rep", axis=1, tiled=True)
    return final.reshape(2, mine, width).transpose(1, 0, 2)


def solution(mesh):
    in_specs = (
        P("req", None, None),
        P(),
        P(None, None, "rep"),
        P("req", None, "rep"),
        P("req", "rep", None),
        P("req", None, "rep"),
        P("req", None, "rep"),
        P("req", "rep", None),
        P("req", None, None, "rep"),
        P("req", None),
        P("req"),
        P("req", None, None, None),
        P("req", None, None, None),
        P("req"),
    )
    out_specs = P("req", None, None)
    return jax.shard_map(shards, mesh=mesh, in_specs=in_specs, out_specs=out_specs, check_vma=False)
```

```python
import functools
import math

import jax
import jax.numpy as jnp
from jax import lax
from jax.experimental import pallas as pl
from jax.experimental.pallas import tpu as pltpu
from jax.sharding import PartitionSpec as P

HD = 128
EXPERTS = 8
SPAN = 256
EPSILON = 1e-06
MASKED = -1e30
F32 = jnp.float32
BF16 = jnp.bfloat16
VM = pl.BlockSpec(memory_space=pltpu.VMEM)
SM = pl.BlockSpec(memory_space=pltpu.SMEM)
ANY = pl.BlockSpec(memory_space=pl.ANY)
ROWS_BY_ROWS = (((1,), (1,)), ((), ()))


def dot(a, b):
    return jnp.dot(a, b, preferred_element_type=F32)


def dot_rows(a, b):
    return lax.dot_general(a, b, ROWS_BY_ROWS, preferred_element_type=F32)


def call(body, out, ins, scratch=(), limit=40):
    many = isinstance(out, (list, tuple))
    return pl.pallas_call(
        body,
        out_shape=out,
        in_specs=ins,
        out_specs=[VM] * len(out) if many else VM,
        scratch_shapes=scratch,
        compiler_params=pltpu.CompilerParams(vmem_limit_bytes=limit << 20),
    )


def shape_of(shape, dtype=BF16):
    return jax.ShapeDtypeStruct(shape, dtype)


def message_kernel(slots, ids, tokens, gains, out):
    count, _, width = tokens.shape
    rows = 2 * count
    half = width // 2
    rank, core = lax.axis_index("req"), lax.axis_index("rep") % 2
    x = tokens[...].reshape(rows, width).astype(F32)
    scaling = lax.rsqrt(jnp.mean(x * x, axis=1, keepdims=True) + EPSILON)
    normed = (x * scaling * gains[0:1]).astype(BF16)
    out[0, :, :half] = jnp.where(core == 0, normed[:, :half], normed[:, half:])
    row = lax.broadcasted_iota(jnp.int32, (rows, HD), 0)
    lane = lax.broadcasted_iota(jnp.int32, (rows, HD), 1)
    notes = jnp.zeros((rows, HD), jnp.int32)
    for j in range(count):
        for s in range(2):
            here = row == 2 * j + s
            source = 2 * (rank * count + j) if s == 0 else 2 * slots[j] + 1
            notes = jnp.where(here & (lane == 0), source, notes)
            for k in range(2):
                notes = jnp.where(here & (lane == 1 + k), ids[0, s, k, j], notes)
    out[0, :, half:] = notes.astype(F32).astype(BF16)
    message = out[0]
    for r in range(1, out.shape[0]):
        out[r] = message


def order_of(near):
    peers, rows, wide = near.shape
    source = near[:, :, wide - HD :].reshape(peers * rows, HD)[:, :1]
    column = lax.broadcasted_iota(jnp.int32, (peers * rows, peers * rows), 1)
    return (source.astype(jnp.int32) == column).astype(BF16)


def query_kernel(near, far, wq, out):
    peers, rows, wide = near.shape
    half = wide - HD
    core = lax.axis_index("rep") % 2
    a = near[:, :, :half].reshape(peers * rows, half)
    b = far[:, :, :half].reshape(peers * rows, half)
    q = dot(a, wq[0, pl.ds(pl.multiple_of(core * half, half), half)])
    q = q + dot(b, wq[0, pl.ds(pl.multiple_of((1 - core) * half, half), half)])
    out[...] = dot(order_of(near), q.astype(BF16)).astype(BF16).reshape(out.shape)


def own_kernel(near, far, sel, own):
    peers, rows, wide = near.shape
    half = wide - HD
    rank, core = lax.axis_index("req"), lax.axis_index("rep") % 2
    source = near[rank][:, half : half + 1]
    column = lax.broadcasted_iota(jnp.int32, (rows, peers * rows), 1)
    order = (source.astype(jnp.int32) == column).astype(BF16)
    a = dot(order, near[...].reshape(peers * rows, wide))
    b = dot(order, far[:, :, :half].reshape(peers * rows, half)).astype(BF16)
    sel[...] = a[:, half:]
    a = a[:, :half].astype(BF16)
    own[:, :half] = jnp.where(core == 0, a, b)
    own[:, half:] = jnp.where(core == 0, b, a)


def page_kernel(table, lens, pool, out, sems):
    count, length = out.shape[:2]
    page = pool.shape[1]
    chunks = length // SPAN

    def each(act):
        for j in range(count):
            for c in range(chunks):
                pl.when(c * SPAN < lens[j])(functools.partial(act, j, c))

    def start(j, c):
        for p in range(SPAN // page):
            pltpu.make_async_copy(
                pool.at[table[j, c * (SPAN // page) + p]],
                out.at[j, pl.ds(c * SPAN + p * page, page)],
                sems.at[j, c],
            ).start()

    def wait(j, c):
        block = out.at[j, pl.ds(c * SPAN, SPAN)]
        pltpu.make_async_copy(block, block, sems.at[j, c]).wait()

    each(start)
    each(wait)


def attention_kernel(lens, sel, arrived, fresh, cache, out, qs, os, sc, ef):
    peers, rows, _ = arrived.shape
    count, _, _, wide = cache.shape
    heads = wide // HD
    group = 2 * heads
    inv_scale = 1.0 / math.sqrt(HD)
    picks = sel[...]
    masks = [[picks[:, 1 + k : 2 + k] == float(e) for e in range(EXPERTS)] for k in range(2)]
    for h in range(heads):
        values = [arrived[e * heads + h].astype(F32) for e in range(EXPERTS)]
        for k in range(2):
            total = jnp.where(masks[k][0], values[0], 0.0)
            for e in range(1, EXPERTS):
                total = total + jnp.where(masks[k][e], values[e], 0.0)
            qs[k * heads + h] = total
    ef[...] = jnp.zeros_like(ef)
    ef[0 : 2 * rows] = fresh[...].reshape(2 * rows, wide)
    extra = ef[...]
    big = (2 * group, wide)
    block_row = lax.broadcasted_iota(jnp.int32, big, 0) % heads
    diagonal = block_row == lax.broadcasted_iota(jnp.int32, big, 1) // HD
    scores_shape = (2 * group, 2 * SPAN)
    column = lax.broadcasted_iota(jnp.int32, scores_shape, 1)
    keys = column % 2 == 0
    e_col = lax.broadcasted_iota(jnp.int32, (2 * group, HD), 1)
    e_row = lax.broadcasted_iota(jnp.int32, (2 * group, HD), 0)
    requests = range(count)

    def block(j, c):
        return cache[j, pl.ds(c * SPAN, SPAN)].reshape(2 * SPAN, wide)

    def masked_scores(q, j, c):
        s = dot_rows(q, block(j, c)) * inv_scale
        return jnp.where(keys & (column < 2 * (lens[j] - c * SPAN)), s, MASKED)

    def highest(s):
        return jnp.max(s, axis=1, keepdims=True)

    def added(p):
        return jnp.sum(p, axis=1, keepdims=True)

    def onto_values(p):
        return pltpu.roll(p, 1, 1).astype(BF16)

    chunks = [(lens[j] + SPAN - 1) // SPAN for j in requests]
    queries, extras, firsts, tops = [], [], [], []
    for j in requests:
        q = jnp.concatenate([qs[:, 2 * j, :], qs[:, 2 * j + 1, :]], axis=0)
        q = jnp.where(diagonal, jnp.concatenate([q] * heads, axis=1), 0.0).astype(BF16)
        live = (e_col == 4 * j) | ((e_col == 4 * j + 2) & (e_row >= group))
        e = jnp.where(live, dot_rows(q, extra) * inv_scale, MASKED)
        s = masked_scores(q, j, 0)
        queries.append(q)
        extras.append(e)
        firsts.append(s)
        tops.append(jnp.maximum(highest(e), highest(s)))

    for j in requests:

        def score(c, top, j=j):
            s = masked_scores(queries[j], j, c)
            sc[j, c] = s
            return jnp.maximum(top, highest(s))

        tops[j] = lax.fori_loop(1, chunks[j], score, tops[j])

    extras = [jnp.exp(extras[j] - tops[j]) for j in requests]
    firsts = [jnp.exp(firsts[j] - tops[j]) for j in requests]
    sums = [added(extras[j]) + added(firsts[j]) for j in requests]
    for j in requests:

        def weigh(c, total, j=j):
            p = jnp.exp(sc[j, c] - tops[j])
            sc[j, c] = p
            return total + added(p)

        sums[j] = lax.fori_loop(1, chunks[j], weigh, sums[j])

    inverses = [1.0 / sums[j] for j in requests]
    mixed = [
        dot(onto_values(extras[j] * inverses[j]), extra)
        + dot(onto_values(firsts[j] * inverses[j]), block(j, 0))
        for j in requests
    ]
    for j in requests:

        def gather(c, total, j=j):
            return total + dot(onto_values(sc[j, c] * inverses[j]), block(j, c))

        mixed[j] = lax.fori_loop(1, chunks[j], gather, mixed[j])

    for j in requests:
        kept = jnp.where(diagonal, mixed[j], 0.0)
        o = kept[:, :HD]
        for h in range(1, heads):
            o = o + kept[:, h * HD : (h + 1) * HD]
        os[:, 2 * j, :] = o[:group]
        os[:, 2 * j + 1, :] = o[group:]
    for h in range(heads):
        first, second = os[h], os[heads + h]
        for e in range(EXPERTS):
            value = jnp.where(masks[0][e], first, 0.0) + jnp.where(masks[1][e], second, 0.0)
            out[e * heads + h] = value.astype(BF16)


def columns_of(z, core, quarter):
    return pl.ds(pl.multiple_of((2 * z + core) * quarter, quarter), quarter)


def project_kernel(near, returned, wo, answers, theirs):
    peers, halves, rows, quarter = theirs.shape
    core = lax.axis_index("rep") % 2
    values = returned[...].reshape(peers * rows, returned.shape[2])
    a = lax.dot_general(
        order_of(near), values, (((0,), (0,)), ((), ())), preferred_element_type=F32
    ).astype(BF16)
    answers[...] = a
    for z in range(halves):
        part = dot(a, wo[0, :, columns_of(z, 1 - core, quarter)])
        theirs[:, z] = part.astype(BF16).reshape(peers, rows, quarter)


def add_kernel(left, theirs, weight, out):
    peers, halves, rows, quarter = theirs.shape
    core = lax.axis_index("rep") % 2
    a = left[...]
    for z in range(halves):
        part = dot(a, weight[0, :, columns_of(z, core, quarter)]).reshape(peers, rows, quarter)
        out[:, z] = (part + theirs[:, z].astype(F32)).astype(BF16)


def expert_kernel(near, far, gains, wg, wu, wd, units, theirs):
    peers, halves, rows, quarter = near.shape
    core = lax.axis_index("rep") % 2
    total = peers * rows
    squares = jnp.zeros((total, 1), F32)
    for block in (near, far):
        for z in range(halves):
            v = block[:, z].reshape(total, quarter).astype(F32)
            squares = squares + jnp.sum(v * v, axis=1, keepdims=True)
    scaling = lax.rsqrt(squares / (2 * halves * quarter) + EPSILON)
    gate = jnp.zeros((total, wg.shape[1]), F32)
    up = jnp.zeros((total, wg.shape[1]), F32)
    for block, side in ((near, core), (far, 1 - core)):
        for z in range(halves):
            where = columns_of(z, side, quarter)
            v = block[:, z].reshape(total, quarter).astype(F32)
            v = (v * scaling * gains[1:2, where]).astype(BF16)
            gate = gate + dot_rows(v, wg[0, :, where])
            up = up + dot_rows(v, wu[0, :, where])
    a = (gate / (1.0 + jnp.exp(-gate)) * up).astype(BF16)
    units[...] = a
    for z in range(halves):
        part = dot(a, wd[0, :, columns_of(z, 1 - core, quarter)])
        theirs[:, z] = part.astype(BF16).reshape(peers, rows, quarter)


def shards(
    tokens,
    norm_gains,
    w_kv,
    w_query,
    w_out,
    w_gate,
    w_up,
    w_down,
    kv_pages,
    page_table,
    cache_len,
    route_ids,
    route_gates,
    new_slot,
):
    req_count = lax.axis_size("req")
    rep_count = lax.axis_size("rep")
    mine, _, width = tokens.shape
    rows = 2 * mine
    total = rows * req_count
    half = width // 2
    quarter = width // rep_count
    wide = kv_pages.shape[-1]
    rep = lax.axis_index("rep")
    swap = [(p, p ^ 1) for p in range(rep_count)]
    wide_groups = [
        [r * rep_count + 2 * z + c for r in range(req_count) for z in range(rep_count // 2)]
        for c in range(2)
    ]
    peers = req_count * rep_count // 2
    split = (req_count, rep_count // 2, rows, quarter)

    def spread_req(value):
        return lax.all_to_all(value, "req", split_axis=0, concat_axis=0, tiled=True)

    def spread_wide(value):
        return lax.all_to_all(
            value,
            ("req", "rep"),
            split_axis=0,
            concat_axis=0,
            tiled=True,
            axis_index_groups=wide_groups,
        )

    def other_core(value):
        return lax.ppermute(value, "rep", swap)

    inputs = tokens.reshape(rows, width)
    ids = route_ids.transpose(0, 2, 1, 3).reshape(rows, 2, 2)
    gates = route_gates.astype(F32).transpose(0, 2, 1, 3).reshape(rows, 2, 2)
    experts_row = jnp.arange(EXPERTS, dtype=jnp.int32)
    shares = jnp.sum(jnp.where(ids[..., None] == experts_row, gates[..., None], 0.0), axis=2)

    message = call(message_kernel, shape_of((req_count, rows, half + HD)), [SM, SM, VM, VM])(
        new_slot, route_ids.transpose(1, 2, 3, 0), tokens, norm_gains
    )
    near = spread_req(message)
    length = page_table.shape[1] * kv_pages.shape[1]
    cache = call(
        page_kernel,
        pltpu.VMEM((mine, length) + kv_pages.shape[2:], BF16),
        [SM, SM, ANY],
        [pltpu.SemaphoreType.DMA((mine, length // SPAN))],
        20,
    )(page_table, cache_len, kv_pages)
    far = other_core(near)
    ordered = call(query_kernel, shape_of((req_count, rows, HD)), [VM] * 3)(near, far, w_query)
    arrived = spread_req(ordered)
    sel, own = call(own_kernel, [shape_of((rows, HD), F32), shape_of((rows, width))], [VM] * 2)(
        near, far
    )
    fresh = jnp.einsum("rd,dtc->rtc", own, w_kv, preferred_element_type=F32).astype(BF16)
    back = call(
        attention_kernel,
        shape_of((req_count, rows, HD)),
        [SM, VM, VM, VM, VM],
        [
            pltpu.VMEM((2 * wide // HD, rows, HD), F32),
            pltpu.VMEM((2 * wide // HD, rows, HD), F32),
            pltpu.VMEM((mine, length // SPAN, 4 * wide // HD, 2 * SPAN), F32),
            pltpu.VMEM((HD, wide), BF16),
        ],
        20,
    )(cache_len, sel, arrived, fresh, cache)
    returned = spread_req(back)
    answers, theirs = call(
        project_kernel, [shape_of((total, w_out.shape[1])), shape_of(split)], [VM] * 3
    )(near, returned, w_out)

    def reduce_wide(left, theirs, weight, share):
        summed = call(add_kernel, shape_of(split), [VM] * 3)(left, other_core(theirs), weight)
        got = spread_wide(summed.reshape(peers, rows, quarter))
        got = got.reshape(EXPERTS, peers // EXPERTS, rows, quarter).astype(F32)
        return jnp.sum(jnp.sum(got, axis=1) * share.T[:, :, None], axis=0)

    kept = lax.dynamic_slice_in_dim(inputs, rep * quarter, quarter, 1).astype(F32)
    hidden = kept + reduce_wide(answers, theirs, w_out, shares[:, 0])
    block = spread_wide(jnp.broadcast_to(hidden.astype(BF16)[None], (peers, rows, quarter)))
    units, theirs = call(
        expert_kernel, [shape_of((total, w_down.shape[1])), shape_of(split)], [VM] * 6
    )(
        block.reshape(split),
        other_core(block).reshape(split),
        norm_gains,
        w_gate.transpose(0, 2, 1),
        w_up.transpose(0, 2, 1),
        w_down,
    )
    feed = reduce_wide(units, theirs, w_down, shares[:, 1])
    final = lax.all_gather((hidden + feed).astype(BF16), "rep", axis=1, tiled=True)
    return final.reshape(mine, 2, width)


def solution(mesh):
    in_specs = (
        P("req", None, None),
        P(),
        P(None, None, "rep"),
        P("req", None, "rep"),
        P("req", "rep", None),
        P("req", None, "rep"),
        P("req", None, "rep"),
        P("req", "rep", None),
        P("req", None, None, "rep"),
        P("req", None),
        P("req"),
        P("req", None, None, None),
        P("req", None, None, None),
        P("req"),
    )
    out_specs = P("req", None, None)
    return jax.shard_map(shards, mesh=mesh, in_specs=in_specs, out_specs=out_specs, check_vma=False)
```

```python
import functools
import math

import jax
import jax.numpy as jnp
from jax import lax
from jax.experimental import pallas as pl
from jax.experimental.pallas import tpu as pltpu
from jax.sharding import PartitionSpec as P

HD = 128
EXPERTS = 8
SPAN = 256
EPSILON = 1e-06
MASKED = -1e30
F32 = jnp.float32
BF16 = jnp.bfloat16
VM = pl.BlockSpec(memory_space=pltpu.VMEM)
SM = pl.BlockSpec(memory_space=pltpu.SMEM)
FAR = pl.BlockSpec(memory_space=pltpu.HBM)
ROWS_BY_ROWS = (((1,), (1,)), ((), ()))


def dot(a, b):
    return jnp.dot(a, b, preferred_element_type=F32)


def dot_rows(a, b):
    return lax.dot_general(a, b, ROWS_BY_ROWS, preferred_element_type=F32)


def call(body, out, ins, scratch=(), limit=12, outs=None):
    many = isinstance(out, (list, tuple))
    return pl.pallas_call(
        body,
        out_shape=out,
        in_specs=ins,
        out_specs=outs or ([VM] * len(out) if many else VM),
        scratch_shapes=scratch,
        compiler_params=pltpu.CompilerParams(vmem_limit_bytes=limit << 20),
    )


def in_hbm(value):
    return pltpu.with_memory_space_constraint(value, pltpu.HBM)


def in_vmem(value):
    return pltpu.with_memory_space_constraint(value, pltpu.VMEM)


def shape_of(shape, dtype=BF16):
    return jax.ShapeDtypeStruct(shape, dtype)


def message_kernel(slots_far, ids_far, tokens_far, gains_far, out, slots, ids, tokens, gains, sems):
    pairs = ((slots_far, slots), (ids_far, ids), (tokens_far, tokens), (gains_far, gains))
    copies = [pltpu.make_async_copy(a, b, sems.at[i]) for i, (a, b) in enumerate(pairs)]
    for copy in copies:
        copy.start()
    for copy in copies:
        copy.wait()
    count, _, width = tokens.shape
    rows = 2 * count
    half = width // 2
    rank, core = lax.axis_index("req"), lax.axis_index("rep") % 2
    x = tokens[...].reshape(rows, width).astype(F32)
    scaling = lax.rsqrt(jnp.mean(x * x, axis=1, keepdims=True) + EPSILON)
    normed = (x * scaling * gains[0:1]).astype(BF16)
    out[0, :, :half] = jnp.where(core == 0, normed[:, :half], normed[:, half:])
    row = lax.broadcasted_iota(jnp.int32, (rows, HD), 0)
    lane = lax.broadcasted_iota(jnp.int32, (rows, HD), 1)
    notes = jnp.zeros((rows, HD), jnp.int32)
    for j in range(count):
        for s in range(2):
            here = row == 2 * j + s
            source = 2 * (rank * count + j) if s == 0 else 2 * slots[j] + 1
            notes = jnp.where(here & (lane == 0), source, notes)
            for k in range(2):
                notes = jnp.where(here & (lane == 1 + k), ids[0, s, k, j], notes)
    out[0, :, half:] = notes.astype(F32).astype(BF16)
    message = out[0]
    for r in range(1, out.shape[0]):
        out[r] = message


def order_of(near):
    peers, rows, wide = near.shape
    source = near[:, :, wide - HD :].reshape(peers * rows, HD)[:, :1]
    column = lax.broadcasted_iota(jnp.int32, (peers * rows, peers * rows), 1)
    return (source.astype(jnp.int32) == column).astype(BF16)


def query_kernel(near, far, wq, out):
    peers, rows, wide = near.shape
    half = wide - HD
    core = lax.axis_index("rep") % 2
    a = near[:, :, :half].reshape(peers * rows, half)
    b = far[:, :, :half].reshape(peers * rows, half)
    q = dot(a, wq[0, pl.ds(pl.multiple_of(core * half, half), half)])
    q = q + dot(b, wq[0, pl.ds(pl.multiple_of((1 - core) * half, half), half)])
    out[...] = dot(order_of(near), q.astype(BF16)).astype(BF16).reshape(out.shape)


def own_kernel(near, far, wkv, sel, fresh):
    peers, rows, wide = near.shape
    half = wide - HD
    rank, core = lax.axis_index("req"), lax.axis_index("rep") % 2
    source = near[rank][:, half : half + 1]
    column = lax.broadcasted_iota(jnp.int32, (rows, peers * rows), 1)
    order = (source.astype(jnp.int32) == column).astype(BF16)
    a = dot(order, near[...].reshape(peers * rows, wide))
    b = dot(order, far[:, :, :half].reshape(peers * rows, half)).astype(BF16)
    sel[...] = a[:, half:]
    a = a[:, :half].astype(BF16)
    parts = (jnp.where(core == 0, a, b), jnp.where(core == 0, b, a))
    spans = half // HD
    chunks = [part[:, c * HD : (c + 1) * HD] for part in parts for c in range(spans)]
    twice = (HD, 2 * HD)
    feature = lax.broadcasted_iota(jnp.int32, twice, 1) // 2
    doubling = (lax.broadcasted_iota(jnp.int32, twice, 0) == feature).astype(BF16)
    doubled = dot(jnp.concatenate(chunks, axis=0), doubling)
    even = lax.broadcasted_iota(jnp.int32, (rows, 2 * HD), 1) % 2 == 0
    total = jnp.zeros(fresh.shape, F32)
    for c in range(2 * spans):
        v = doubled[c * rows : (c + 1) * rows]
        v = jnp.concatenate([jnp.where(even, v, 0.0), jnp.where(even, 0.0, v)], axis=0)
        w = wkv[c * HD : (c + 1) * HD].reshape(2 * HD, fresh.shape[1])
        total = total + dot(v.astype(BF16), w)
    fresh[...] = total.astype(BF16)


def page_kernel(table_far, lens_far, pool, out, table, lens, sems, small):
    first = pltpu.make_async_copy(table_far, table, small.at[0])
    second = pltpu.make_async_copy(lens_far, lens, small.at[1])
    first.start()
    second.start()
    first.wait()
    second.wait()
    count, length = out.shape[:2]
    page = pool.shape[1]
    chunks = length // SPAN

    def each(act):
        for j in range(count):
            for c in range(chunks):
                pl.when(c * SPAN < lens[j])(functools.partial(act, j, c))

    def start(j, c):
        for p in range(SPAN // page):
            pltpu.make_async_copy(
                pool.at[table[j, c * (SPAN // page) + p]],
                out.at[j, pl.ds(c * SPAN + p * page, page)],
                sems.at[j, c],
            ).start()

    def wait(j, c):
        block = out.at[j, pl.ds(c * SPAN, SPAN)]
        pltpu.make_async_copy(block, block, sems.at[j, c]).wait()

    each(start)
    each(wait)


def attention_kernel(lens, sel, arrived, fresh, cache_far, out, cache, qs, os, sc, ef, sems):
    def copy_of(j, c):
        span = pl.ds(c * SPAN, SPAN)
        return pltpu.make_async_copy(cache_far.at[j, span], cache.at[j, span], sems.at[j, c])

    for c in range(cache.shape[1] // SPAN):
        for j in range(cache.shape[0]):

            @pl.when(c * SPAN < lens[j])
            def _(j=j, c=c):
                copy_of(j, c).start()

    peers, rows, _ = arrived.shape
    count, _, _, wide = cache.shape
    heads = wide // HD
    group = 2 * heads
    inv_scale = 1.0 / math.sqrt(HD)
    picks = sel[...]
    masks = [[picks[:, 1 + k : 2 + k] == float(e) for e in range(EXPERTS)] for k in range(2)]
    for h in range(heads):
        values = [arrived[e * heads + h].astype(F32) for e in range(EXPERTS)]
        for k in range(2):
            total = jnp.where(masks[k][0], values[0], 0.0)
            for e in range(1, EXPERTS):
                total = total + jnp.where(masks[k][e], values[e], 0.0)
            qs[k * heads + h] = total
    ef[...] = jnp.zeros_like(ef)
    ef[0 : 2 * rows] = fresh[...]
    extra = ef[...]
    big = (2 * group, wide)
    block_row = lax.broadcasted_iota(jnp.int32, big, 0) % heads
    diagonal = block_row == lax.broadcasted_iota(jnp.int32, big, 1) // HD
    scores_shape = (2 * group, 2 * SPAN)
    column = lax.broadcasted_iota(jnp.int32, scores_shape, 1)
    keys = column % 2 == 0
    e_col = lax.broadcasted_iota(jnp.int32, (2 * group, HD), 1)
    e_row = lax.broadcasted_iota(jnp.int32, (2 * group, HD), 0)
    requests = range(count)

    def block(j, c):
        return cache[j, pl.ds(c * SPAN, SPAN)].reshape(2 * SPAN, wide)

    def masked_scores(q, j, c):
        copy_of(j, c).wait()
        s = dot_rows(q, block(j, c)) * inv_scale
        return jnp.where(keys & (column < 2 * (lens[j] - c * SPAN)), s, MASKED)

    def highest(s):
        return jnp.max(s, axis=1, keepdims=True)

    def added(p):
        return jnp.sum(p, axis=1, keepdims=True)

    def onto_values(p, distance=1):
        return pltpu.roll(p, distance, 1).astype(BF16)

    chunks = [(lens[j] + SPAN - 1) // SPAN for j in requests]
    queries, extras, firsts, tops = [], [], [], []
    for j in requests:
        q = jnp.concatenate([qs[:, 2 * j, :], qs[:, 2 * j + 1, :]], axis=0)
        q = jnp.where(diagonal, jnp.concatenate([q] * heads, axis=1), 0.0).astype(BF16)
        live = (e_col == 2 * j) | ((e_col == 2 * j + 1) & (e_row >= group))
        e = jnp.where(live, dot_rows(q, extra) * inv_scale, MASKED)
        s = masked_scores(q, j, 0)
        queries.append(q)
        extras.append(e)
        firsts.append(s)
        tops.append(jnp.maximum(highest(e), highest(s)))

    for j in requests:

        def score(c, top, j=j):
            s = masked_scores(queries[j], j, c)
            sc[j, c] = s
            return jnp.maximum(top, highest(s))

        tops[j] = lax.fori_loop(1, chunks[j], score, tops[j])

    extras = [jnp.exp(extras[j] - tops[j]) for j in requests]
    firsts = [jnp.exp(firsts[j] - tops[j]) for j in requests]
    sums = [added(extras[j]) + added(firsts[j]) for j in requests]
    for j in requests:

        def weigh(c, total, j=j):
            p = jnp.exp(sc[j, c] - tops[j])
            sc[j, c] = p
            return total + added(p)

        sums[j] = lax.fori_loop(1, chunks[j], weigh, sums[j])

    inverses = [1.0 / sums[j] for j in requests]
    mixed = [
        dot(onto_values(extras[j] * inverses[j], rows), extra)
        + dot(onto_values(firsts[j] * inverses[j]), block(j, 0))
        for j in requests
    ]
    for j in requests:

        def gather(c, total, j=j):
            return total + dot(onto_values(sc[j, c] * inverses[j]), block(j, c))

        mixed[j] = lax.fori_loop(1, chunks[j], gather, mixed[j])

    for j in requests:
        kept = jnp.where(diagonal, mixed[j], 0.0)
        o = kept[:, :HD]
        for h in range(1, heads):
            o = o + kept[:, h * HD : (h + 1) * HD]
        os[:, 2 * j, :] = o[:group]
        os[:, 2 * j + 1, :] = o[group:]
    for h in range(heads):
        first, second = os[h], os[heads + h]
        for e in range(EXPERTS):
            value = jnp.where(masks[0][e], first, 0.0) + jnp.where(masks[1][e], second, 0.0)
            out[e * heads + h] = value.astype(BF16)


def columns_of(z, core, quarter):
    return pl.ds(pl.multiple_of((2 * z + core) * quarter, quarter), quarter)


def project_kernel(near, returned, wo, answers, theirs):
    peers, halves, rows, quarter = theirs.shape
    core = lax.axis_index("rep") % 2
    values = returned[...].reshape(peers * rows, returned.shape[2])
    a = lax.dot_general(
        order_of(near), values, (((0,), (0,)), ((), ())), preferred_element_type=F32
    ).astype(BF16)
    answers[...] = a
    for z in range(halves):
        part = dot(a, wo[0, :, columns_of(z, 1 - core, quarter)])
        theirs[:, z] = part.astype(BF16).reshape(peers, rows, quarter)


def part_kernel(left, weight, out):
    peers, halves, rows, quarter = out.shape
    core = lax.axis_index("rep") % 2
    a = left[...]
    for z in range(halves):
        part = dot(a, weight[0, :, columns_of(z, core, quarter)])
        out[:, z] = part.reshape(peers, rows, quarter)


def place_kernel(*refs):
    pieces, out = refs[:-1], refs[-1]
    rep = lax.axis_index("rep")
    count, _, width = out.shape
    quarter = width // len(pieces)
    for m, piece in enumerate(pieces):
        place = pl.multiple_of((rep ^ m) * quarter, quarter)
        out[:, :, pl.ds(place, quarter)] = piece[...].reshape(count, 2, quarter)


def fetch_kernel(*refs):
    count = len(refs) // 2
    sems = refs[-1]
    copies = [pltpu.make_async_copy(refs[i], refs[count + i], sems.at[i]) for i in range(count)]
    for copy in copies:
        copy.start()
    for copy in copies:
        copy.wait()


def fetch(*arrays):
    return call(
        fetch_kernel,
        [pltpu.VMEM(a.shape, a.dtype) for a in arrays],
        [FAR] * len(arrays),
        [pltpu.SemaphoreType.DMA((len(arrays),))],
    )(*[in_hbm(a) for a in arrays])


def expert_kernel(near, far, gains, wg, wu, wd_far, units, theirs, wd, sem):
    load = pltpu.make_async_copy(wd_far, wd, sem)
    load.start()
    peers, halves, rows, quarter = near.shape
    core = lax.axis_index("rep") % 2
    total = peers * rows
    squares = jnp.zeros((total, 1), F32)
    for block in (near, far):
        for z in range(halves):
            v = block[:, z].reshape(total, quarter).astype(F32)
            squares = squares + jnp.sum(v * v, axis=1, keepdims=True)
    scaling = lax.rsqrt(squares / (2 * halves * quarter) + EPSILON)
    gate = jnp.zeros((total, wg.shape[1]), F32)
    up = jnp.zeros((total, wg.shape[1]), F32)
    for block, side in ((near, core), (far, 1 - core)):
        for z in range(halves):
            where = columns_of(z, side, quarter)
            v = block[:, z].reshape(total, quarter).astype(F32)
            v = (v * scaling * gains[1:2, where]).astype(BF16)
            gate = gate + dot_rows(v, wg[0, :, where])
            up = up + dot_rows(v, wu[0, :, where])
    a = (gate / (1.0 + jnp.exp(-gate)) * up).astype(BF16)
    units[...] = a
    load.wait()
    for z in range(halves):
        part = dot(a, wd[0, :, columns_of(z, 1 - core, quarter)])
        theirs[:, z] = part.astype(BF16).reshape(peers, rows, quarter)


def shards(
    tokens,
    norm_gains,
    w_kv,
    w_query,
    w_out,
    w_gate,
    w_up,
    w_down,
    kv_pages,
    page_table,
    cache_len,
    route_ids,
    route_gates,
    new_slot,
):
    req_count = lax.axis_size("req")
    rep_count = lax.axis_size("rep")
    mine, _, width = tokens.shape
    rows = 2 * mine
    total = rows * req_count
    half = width // 2
    quarter = width // rep_count
    wide = kv_pages.shape[-1]
    rep = lax.axis_index("rep")
    swap = [(p, p ^ 1) for p in range(rep_count)]
    wide_groups = [
        [r * rep_count + 2 * z + c for r in range(req_count) for z in range(rep_count // 2)]
        for c in range(2)
    ]
    peers = req_count * rep_count // 2
    split = (req_count, rep_count // 2, rows, quarter)

    def spread_req(value):
        return lax.all_to_all(value, "req", split_axis=0, concat_axis=0, tiled=True)

    def spread_wide(value):
        return lax.all_to_all(
            value,
            ("req", "rep"),
            split_axis=0,
            concat_axis=0,
            tiled=True,
            axis_index_groups=wide_groups,
        )

    def other_core(value):
        return lax.ppermute(value, "rep", swap)

    inputs = tokens.reshape(rows, width)
    ids = route_ids.transpose(0, 2, 1, 3).reshape(rows, 2, 2)
    gates = route_gates.astype(F32).transpose(0, 2, 1, 3).reshape(rows, 2, 2)
    experts_row = jnp.arange(EXPERTS, dtype=jnp.int32)
    shares = jnp.sum(jnp.where(ids[..., None] == experts_row, gates[..., None], 0.0), axis=2)

    routes = route_ids.transpose(1, 2, 3, 0)
    message = call(
        message_kernel,
        shape_of((req_count, rows, half + HD)),
        [FAR] * 4,
        [
            pltpu.SMEM(new_slot.shape, jnp.int32),
            pltpu.SMEM(routes.shape, jnp.int32),
            pltpu.VMEM(tokens.shape, BF16),
            pltpu.VMEM(norm_gains.shape, F32),
            pltpu.SemaphoreType.DMA((4,)),
        ],
    )(in_hbm(new_slot), in_hbm(routes), in_hbm(tokens), in_hbm(norm_gains))
    near = spread_req(message)
    length = page_table.shape[1] * kv_pages.shape[1]
    cache = call(
        page_kernel,
        pltpu.HBM((mine, length) + kv_pages.shape[2:], BF16),
        [FAR] * 3,
        [
            pltpu.SMEM(page_table.shape, jnp.int32),
            pltpu.SMEM(cache_len.shape, jnp.int32),
            pltpu.SemaphoreType.DMA((mine, length // SPAN)),
            pltpu.SemaphoreType.DMA((2,)),
        ],
        outs=FAR,
    )(in_hbm(page_table), in_hbm(cache_len), in_hbm(kv_pages))
    near, cache = lax.optimization_barrier((near, cache))
    far = other_core(near)
    ordered = call(query_kernel, shape_of((req_count, rows, HD)), [VM] * 3)(near, far, w_query)
    arrived = spread_req(ordered)
    sel, fresh = call(
        own_kernel, [shape_of((rows, HD), F32), shape_of((2 * rows, wide))], [VM] * 3
    )(near, far, w_kv)
    back = call(
        attention_kernel,
        shape_of((req_count, rows, HD)),
        [SM, VM, VM, VM, FAR],
        [
            pltpu.VMEM(cache.shape, BF16),
            pltpu.VMEM((2 * wide // HD, rows, HD), F32),
            pltpu.VMEM((2 * wide // HD, rows, HD), F32),
            pltpu.VMEM((mine, length // SPAN, 4 * wide // HD, 2 * SPAN), F32),
            pltpu.VMEM((HD, wide), BF16),
            pltpu.SemaphoreType.DMA((mine, length // SPAN)),
        ],
        16,
    )(cache_len, sel, arrived, fresh, in_hbm(cache))
    returned = spread_req(back)
    answers, theirs = call(
        project_kernel, [shape_of((total, w_out.shape[1])), shape_of(split)], [VM] * 3
    )(near, returned, w_out)

    def reduce_wide(left, theirs, weight, share):
        part = call(part_kernel, shape_of(split, F32), [VM] * 2)(left, weight)
        summed = (part + other_core(theirs).astype(F32)).astype(BF16)
        got = spread_wide(summed.reshape(peers, rows, quarter))
        got = got.reshape(EXPERTS, peers // EXPERTS, rows, quarter).astype(F32)
        return jnp.sum(jnp.sum(got, axis=1) * share.T[:, :, None], axis=0)

    kept = lax.dynamic_slice_in_dim(inputs, rep * quarter, quarter, 1).astype(F32)
    hidden = kept + reduce_wide(answers, theirs, w_out, shares[:, 0])
    copies = jnp.broadcast_to(hidden.astype(BF16)[None], (peers, rows, quarter))
    copies, *weights = lax.optimization_barrier(
        (copies, w_gate.transpose(0, 2, 1), w_up.transpose(0, 2, 1))
    )
    block = spread_wide(copies)
    block, *weights = lax.optimization_barrier((block, *fetch(*weights)))
    units, theirs, down = call(
        expert_kernel,
        [
            shape_of((total, w_down.shape[1])),
            shape_of(split),
            pltpu.VMEM(w_down.shape, BF16),
        ],
        [VM] * 5 + [FAR],
        [pltpu.SemaphoreType.DMA],
    )(
        block.reshape(split),
        other_core(block).reshape(split),
        norm_gains,
        *[in_vmem(w) for w in weights],
        in_hbm(w_down),
    )
    feed = reduce_wide(units, theirs, in_vmem(down), shares[:, 1])
    piece = (hidden + feed).astype(BF16)
    pieces = [piece] + [
        lax.ppermute(piece, "rep", [(p, p ^ m) for p in range(rep_count)])
        for m in range(1, rep_count)
    ]
    return call(place_kernel, shape_of((mine, 2, width)), [VM] * rep_count)(*pieces)


def solution(mesh):
    in_specs = (
        P("req", None, None),
        P(),
        P(None, None, "rep"),
        P("req", None, "rep"),
        P("req", "rep", None),
        P("req", None, "rep"),
        P("req", None, "rep"),
        P("req", "rep", None),
        P("req", None, None, "rep"),
        P("req", None),
        P("req"),
        P("req", None, None, None),
        P("req", None, None, None),
        P("req"),
    )
    out_specs = P("req", None, None)
    return jax.shard_map(shards, mesh=mesh, in_specs=in_specs, out_specs=out_specs, check_vma=False)
```

```python
import functools
import math

import jax
import jax.numpy as jnp
from jax import lax
from jax.experimental import pallas as pl
from jax.experimental.pallas import tpu as pltpu
from jax.sharding import PartitionSpec as P

HD = 128
EXPERTS = 8
SPAN = 256
EPSILON = 1e-06
MASKED = -1e30
F32 = jnp.float32
BF16 = jnp.bfloat16
VM = pl.BlockSpec(memory_space=pltpu.VMEM)
SM = pl.BlockSpec(memory_space=pltpu.SMEM)
FAR = pl.BlockSpec(memory_space=pltpu.HBM)
ROWS_BY_ROWS = (((1,), (1,)), ((), ()))


def dot(a, b):
    return jnp.dot(a, b, preferred_element_type=F32)


def dot_rows(a, b):
    return lax.dot_general(a, b, ROWS_BY_ROWS, preferred_element_type=F32)


def call(body, out, ins, scratch=(), limit=12, outs=None):
    many = isinstance(out, (list, tuple))
    return pl.pallas_call(
        body,
        out_shape=out,
        in_specs=ins,
        out_specs=outs or ([VM] * len(out) if many else VM),
        scratch_shapes=scratch,
        compiler_params=pltpu.CompilerParams(vmem_limit_bytes=limit << 20),
    )


def in_hbm(value):
    return pltpu.with_memory_space_constraint(value, pltpu.HBM)


def in_vmem(value):
    return pltpu.with_memory_space_constraint(value, pltpu.VMEM)


def shape_of(shape, dtype=BF16):
    return jax.ShapeDtypeStruct(shape, dtype)


def message_kernel(slots_far, ids_far, tokens_far, gains_far, out, slots, ids, tokens, gains, sems):
    pairs = ((slots_far, slots), (ids_far, ids), (tokens_far, tokens), (gains_far, gains))
    copies = [pltpu.make_async_copy(a, b, sems.at[i]) for i, (a, b) in enumerate(pairs)]
    for copy in copies:
        copy.start()
    for copy in copies:
        copy.wait()
    count, _, width = tokens.shape
    rows = 2 * count
    half = width // 2
    rank, core = lax.axis_index("req"), lax.axis_index("rep") % 2
    x = tokens[...].reshape(rows, width).astype(F32)
    scaling = lax.rsqrt(jnp.mean(x * x, axis=1, keepdims=True) + EPSILON)
    normed = (x * scaling * gains[0:1]).astype(BF16)
    out[0, :, :half] = jnp.where(core == 0, normed[:, :half], normed[:, half:])
    row = lax.broadcasted_iota(jnp.int32, (rows, HD), 0)
    lane = lax.broadcasted_iota(jnp.int32, (rows, HD), 1)
    notes = jnp.zeros((rows, HD), jnp.int32)
    for j in range(count):
        for s in range(2):
            here = row == 2 * j + s
            source = 2 * (rank * count + j) if s == 0 else 2 * slots[j] + 1
            notes = jnp.where(here & (lane == 0), source, notes)
            for k in range(2):
                notes = jnp.where(here & (lane == 1 + k), ids[0, s, k, j], notes)
    out[0, :, half:] = notes.astype(F32).astype(BF16)
    message = out[0]
    for r in range(1, out.shape[0]):
        out[r] = message


def order_of(near):
    peers, rows, wide = near.shape
    source = near[:, :, wide - HD :].reshape(peers * rows, HD)[:, :1]
    column = lax.broadcasted_iota(jnp.int32, (peers * rows, peers * rows), 1)
    return (source.astype(jnp.int32) == column).astype(BF16)


def query_kernel(near, far, wq, out):
    peers, rows, wide = near.shape
    half = wide - HD
    core = lax.axis_index("rep") % 2
    a = near[:, :, :half].reshape(peers * rows, half)
    b = far[:, :, :half].reshape(peers * rows, half)
    q = dot(a, wq[0, pl.ds(pl.multiple_of(core * half, half), half)])
    q = q + dot(b, wq[0, pl.ds(pl.multiple_of((1 - core) * half, half), half)])
    out[...] = dot(order_of(near), q.astype(BF16)).astype(BF16).reshape(out.shape)


def own_kernel(near, far, wkv, sel, fresh):
    peers, rows, wide = near.shape
    half = wide - HD
    rank, core = lax.axis_index("req"), lax.axis_index("rep") % 2
    source = near[rank][:, half : half + 1]
    column = lax.broadcasted_iota(jnp.int32, (rows, peers * rows), 1)
    order = (source.astype(jnp.int32) == column).astype(BF16)
    a = dot(order, near[...].reshape(peers * rows, wide))
    b = dot(order, far[:, :, :half].reshape(peers * rows, half)).astype(BF16)
    sel[...] = a[:, half:]
    a = a[:, :half].astype(BF16)
    parts = (jnp.where(core == 0, a, b), jnp.where(core == 0, b, a))
    spans = half // HD
    chunks = [part[:, c * HD : (c + 1) * HD] for part in parts for c in range(spans)]
    twice = (HD, 2 * HD)
    feature = lax.broadcasted_iota(jnp.int32, twice, 1) // 2
    doubling = (lax.broadcasted_iota(jnp.int32, twice, 0) == feature).astype(BF16)
    doubled = dot(jnp.concatenate(chunks, axis=0), doubling)
    even = lax.broadcasted_iota(jnp.int32, (rows, 2 * HD), 1) % 2 == 0
    total = jnp.zeros(fresh.shape, F32)
    for c in range(2 * spans):
        v = doubled[c * rows : (c + 1) * rows]
        v = jnp.concatenate([jnp.where(even, v, 0.0), jnp.where(even, 0.0, v)], axis=0)
        w = wkv[c * HD : (c + 1) * HD].reshape(2 * HD, fresh.shape[1])
        total = total + dot(v.astype(BF16), w)
    fresh[...] = total.astype(BF16)


def page_kernel(table_far, lens_far, pool, out, table, lens, staged, sems, back, small):
    first = pltpu.make_async_copy(table_far, table, small.at[0])
    second = pltpu.make_async_copy(lens_far, lens, small.at[1])
    first.start()
    second.start()
    first.wait()
    second.wait()
    count, length = out.shape[:2]
    page = pool.shape[1]
    chunks = length // SPAN

    def each(act):
        for j in range(count):
            for c in range(chunks):
                pl.when(c * SPAN < lens[j])(functools.partial(act, j, c))

    def start(j, c):
        for p in range(SPAN // page):
            pltpu.make_async_copy(
                pool.at[table[j, c * (SPAN // page) + p]],
                staged.at[j, pl.ds(c * SPAN + p * page, page)],
                sems.at[j, c],
            ).start()

    def write(j, c):
        span = pl.ds(c * SPAN, SPAN)
        return pltpu.make_async_copy(staged.at[j, span], out.at[j, span], back.at[j, c])

    def forward(j, c):
        block = staged.at[j, pl.ds(c * SPAN, SPAN)]
        pltpu.make_async_copy(block, block, sems.at[j, c]).wait()
        write(j, c).start()

    def finish(j, c):
        write(j, c).wait()

    each(start)
    each(forward)
    each(finish)


def attention_kernel(lens, sel, arrived, fresh, cache_far, out, cache, qs, os, sc, ef, sems):
    def copy_of(j, c):
        span = pl.ds(c * SPAN, SPAN)
        return pltpu.make_async_copy(cache_far.at[j, span], cache.at[j, span], sems.at[j, c])

    for c in range(cache.shape[1] // SPAN):
        for j in range(cache.shape[0]):

            @pl.when(c * SPAN < lens[j])
            def _(j=j, c=c):
                copy_of(j, c).start()

    peers, rows, _ = arrived.shape
    count, _, _, wide = cache.shape
    heads = wide // HD
    group = 2 * heads
    inv_scale = 1.0 / math.sqrt(HD)
    picks = sel[...]
    masks = [[picks[:, 1 + k : 2 + k] == float(e) for e in range(EXPERTS)] for k in range(2)]
    for h in range(heads):
        values = [arrived[e * heads + h].astype(F32) for e in range(EXPERTS)]
        for k in range(2):
            total = jnp.where(masks[k][0], values[0], 0.0)
            for e in range(1, EXPERTS):
                total = total + jnp.where(masks[k][e], values[e], 0.0)
            qs[k * heads + h] = total
    ef[...] = jnp.zeros_like(ef)
    ef[0 : 2 * rows] = fresh[...]
    extra = ef[...]
    big = (2 * group, wide)
    block_row = lax.broadcasted_iota(jnp.int32, big, 0) % heads
    diagonal = block_row == lax.broadcasted_iota(jnp.int32, big, 1) // HD
    scores_shape = (2 * group, 2 * SPAN)
    column = lax.broadcasted_iota(jnp.int32, scores_shape, 1)
    keys = column % 2 == 0
    e_col = lax.broadcasted_iota(jnp.int32, (2 * group, HD), 1)
    e_row = lax.broadcasted_iota(jnp.int32, (2 * group, HD), 0)
    requests = range(count)

    def block(j, c):
        return cache[j, pl.ds(c * SPAN, SPAN)].reshape(2 * SPAN, wide)

    def masked_scores(q, j, c):
        copy_of(j, c).wait()
        s = dot_rows(q, block(j, c)) * inv_scale
        return jnp.where(keys & (column < 2 * (lens[j] - c * SPAN)), s, MASKED)

    def highest(s):
        return jnp.max(s, axis=1, keepdims=True)

    def added(p):
        return jnp.sum(p, axis=1, keepdims=True)

    def onto_values(p, distance=1):
        return pltpu.roll(p, distance, 1).astype(BF16)

    chunks = [(lens[j] + SPAN - 1) // SPAN for j in requests]
    queries, extras, firsts, tops = [], [], [], []
    for j in requests:
        q = jnp.concatenate([qs[:, 2 * j, :], qs[:, 2 * j + 1, :]], axis=0)
        q = jnp.where(diagonal, jnp.concatenate([q] * heads, axis=1), 0.0).astype(BF16)
        live = (e_col == 2 * j) | ((e_col == 2 * j + 1) & (e_row >= group))
        e = jnp.where(live, dot_rows(q, extra) * inv_scale, MASKED)
        s = masked_scores(q, j, 0)
        queries.append(q)
        extras.append(e)
        firsts.append(s)
        tops.append(jnp.maximum(highest(e), highest(s)))

    for j in requests:

        def score(c, top, j=j):
            s = masked_scores(queries[j], j, c)
            sc[j, c] = s
            return jnp.maximum(top, highest(s))

        tops[j] = lax.fori_loop(1, chunks[j], score, tops[j])

    extras = [jnp.exp(extras[j] - tops[j]) for j in requests]
    firsts = [jnp.exp(firsts[j] - tops[j]) for j in requests]
    sums = [added(extras[j]) + added(firsts[j]) for j in requests]
    for j in requests:

        def weigh(c, total, j=j):
            p = jnp.exp(sc[j, c] - tops[j])
            sc[j, c] = p
            return total + added(p)

        sums[j] = lax.fori_loop(1, chunks[j], weigh, sums[j])

    inverses = [1.0 / sums[j] for j in requests]
    mixed = [
        dot(onto_values(extras[j] * inverses[j], rows), extra)
        + dot(onto_values(firsts[j] * inverses[j]), block(j, 0))
        for j in requests
    ]
    for j in requests:

        def gather(c, total, j=j):
            return total + dot(onto_values(sc[j, c] * inverses[j]), block(j, c))

        mixed[j] = lax.fori_loop(1, chunks[j], gather, mixed[j])

    for j in requests:
        kept = jnp.where(diagonal, mixed[j], 0.0)
        o = kept[:, :HD]
        for h in range(1, heads):
            o = o + kept[:, h * HD : (h + 1) * HD]
        os[:, 2 * j, :] = o[:group]
        os[:, 2 * j + 1, :] = o[group:]
    for h in range(heads):
        first, second = os[h], os[heads + h]
        for e in range(EXPERTS):
            value = jnp.where(masks[0][e], first, 0.0) + jnp.where(masks[1][e], second, 0.0)
            out[e * heads + h] = value.astype(BF16)


def columns_of(z, core, quarter):
    return pl.ds(pl.multiple_of((2 * z + core) * quarter, quarter), quarter)


def project_kernel(near, returned, wo, answers, theirs):
    peers, halves, rows, quarter = theirs.shape
    core = lax.axis_index("rep") % 2
    values = returned[...].reshape(peers * rows, returned.shape[2])
    a = lax.dot_general(
        order_of(near), values, (((0,), (0,)), ((), ())), preferred_element_type=F32
    ).astype(BF16)
    answers[...] = a
    for z in range(halves):
        part = dot(a, wo[0, :, columns_of(z, 1 - core, quarter)])
        theirs[:, z] = part.astype(BF16).reshape(peers, rows, quarter)


def part_kernel(left, weight, out):
    peers, halves, rows, quarter = out.shape
    core = lax.axis_index("rep") % 2
    a = left[...]
    for z in range(halves):
        part = dot(a, weight[0, :, columns_of(z, core, quarter)])
        out[:, z] = part.reshape(peers, rows, quarter)


def place_kernel(*refs):
    pieces, out = refs[:-1], refs[-1]
    rep = lax.axis_index("rep")
    count, _, width = out.shape
    quarter = width // len(pieces)
    for m, piece in enumerate(pieces):
        place = pl.multiple_of((rep ^ m) * quarter, quarter)
        out[:, :, pl.ds(place, quarter)] = piece[...].reshape(count, 2, quarter)


def fetch_kernel(*refs):
    count = len(refs) // 2
    sems = refs[-1]
    copies = [pltpu.make_async_copy(refs[i], refs[count + i], sems.at[i]) for i in range(count)]
    for copy in copies:
        copy.start()
    for copy in copies:
        copy.wait()


def fetch(*arrays):
    return call(
        fetch_kernel,
        [pltpu.VMEM(a.shape, a.dtype) for a in arrays],
        [FAR] * len(arrays),
        [pltpu.SemaphoreType.DMA((len(arrays),))],
    )(*[in_hbm(a) for a in arrays])


def expert_kernel(near, far, gains, wg, wu, wd_far, units, theirs, wd, sem):
    load = pltpu.make_async_copy(wd_far, wd, sem)
    load.start()
    peers, halves, rows, quarter = near.shape
    core = lax.axis_index("rep") % 2
    total = peers * rows
    squares = jnp.zeros((total, 1), F32)
    for block in (near, far):
        for z in range(halves):
            v = block[:, z].reshape(total, quarter).astype(F32)
            squares = squares + jnp.sum(v * v, axis=1, keepdims=True)
    scaling = lax.rsqrt(squares / (2 * halves * quarter) + EPSILON)
    gate = jnp.zeros((total, wg.shape[1]), F32)
    up = jnp.zeros((total, wg.shape[1]), F32)
    for block, side in ((near, core), (far, 1 - core)):
        for z in range(halves):
            where = columns_of(z, side, quarter)
            v = block[:, z].reshape(total, quarter).astype(F32)
            v = (v * scaling * gains[1:2, where]).astype(BF16)
            gate = gate + dot_rows(v, wg[0, :, where])
            up = up + dot_rows(v, wu[0, :, where])
    a = (gate / (1.0 + jnp.exp(-gate)) * up).astype(BF16)
    units[...] = a
    load.wait()
    for z in range(halves):
        part = dot(a, wd[0, :, columns_of(z, 1 - core, quarter)])
        theirs[:, z] = part.astype(BF16).reshape(peers, rows, quarter)


def shards(
    tokens,
    norm_gains,
    w_kv,
    w_query,
    w_out,
    w_gate,
    w_up,
    w_down,
    kv_pages,
    page_table,
    cache_len,
    route_ids,
    route_gates,
    new_slot,
):
    req_count = lax.axis_size("req")
    rep_count = lax.axis_size("rep")
    mine, _, width = tokens.shape
    rows = 2 * mine
    total = rows * req_count
    half = width // 2
    quarter = width // rep_count
    wide = kv_pages.shape[-1]
    rep = lax.axis_index("rep")
    swap = [(p, p ^ 1) for p in range(rep_count)]
    wide_groups = [
        [r * rep_count + 2 * z + c for r in range(req_count) for z in range(rep_count // 2)]
        for c in range(2)
    ]
    peers = req_count * rep_count // 2
    split = (req_count, rep_count // 2, rows, quarter)

    def spread_req(value):
        return lax.all_to_all(value, "req", split_axis=0, concat_axis=0, tiled=True)

    def spread_wide(value):
        return lax.all_to_all(
            value,
            ("req", "rep"),
            split_axis=0,
            concat_axis=0,
            tiled=True,
            axis_index_groups=wide_groups,
        )

    def other_core(value):
        return lax.ppermute(value, "rep", swap)

    inputs = tokens.reshape(rows, width)
    ids = route_ids.transpose(0, 2, 1, 3).reshape(rows, 2, 2)
    gates = route_gates.astype(F32).transpose(0, 2, 1, 3).reshape(rows, 2, 2)
    experts_row = jnp.arange(EXPERTS, dtype=jnp.int32)
    shares = jnp.sum(jnp.where(ids[..., None] == experts_row, gates[..., None], 0.0), axis=2)

    routes = route_ids.transpose(1, 2, 3, 0)
    message = call(
        message_kernel,
        shape_of((req_count, rows, half + HD)),
        [FAR] * 4,
        [
            pltpu.SMEM(new_slot.shape, jnp.int32),
            pltpu.SMEM(routes.shape, jnp.int32),
            pltpu.VMEM(tokens.shape, BF16),
            pltpu.VMEM(norm_gains.shape, F32),
            pltpu.SemaphoreType.DMA((4,)),
        ],
    )(in_hbm(new_slot), in_hbm(routes), in_hbm(tokens), in_hbm(norm_gains))
    near = spread_req(message)
    length = page_table.shape[1] * kv_pages.shape[1]
    cache = call(
        page_kernel,
        pltpu.HBM((mine, length) + kv_pages.shape[2:], BF16),
        [FAR] * 3,
        [
            pltpu.SMEM(page_table.shape, jnp.int32),
            pltpu.SMEM(cache_len.shape, jnp.int32),
            pltpu.VMEM((mine, length) + kv_pages.shape[2:], BF16),
            pltpu.SemaphoreType.DMA((mine, length // SPAN)),
            pltpu.SemaphoreType.DMA((mine, length // SPAN)),
            pltpu.SemaphoreType.DMA((2,)),
        ],
        outs=FAR,
    )(in_hbm(page_table), in_hbm(cache_len), in_hbm(kv_pages))
    near, cache = lax.optimization_barrier((near, cache))
    far = other_core(near)
    ordered = call(query_kernel, shape_of((req_count, rows, HD)), [VM] * 3)(near, far, w_query)
    arrived = spread_req(ordered)
    sel, fresh = call(
        own_kernel, [shape_of((rows, HD), F32), shape_of((2 * rows, wide))], [VM] * 3
    )(near, far, w_kv)
    back = call(
        attention_kernel,
        shape_of((req_count, rows, HD)),
        [SM, VM, VM, VM, FAR],
        [
            pltpu.VMEM(cache.shape, BF16),
            pltpu.VMEM((2 * wide // HD, rows, HD), F32),
            pltpu.VMEM((2 * wide // HD, rows, HD), F32),
            pltpu.VMEM((mine, length // SPAN, 4 * wide // HD, 2 * SPAN), F32),
            pltpu.VMEM((HD, wide), BF16),
            pltpu.SemaphoreType.DMA((mine, length // SPAN)),
        ],
        16,
    )(cache_len, sel, arrived, fresh, in_hbm(cache))
    returned = spread_req(back)
    answers, theirs = call(
        project_kernel, [shape_of((total, w_out.shape[1])), shape_of(split)], [VM] * 3
    )(near, returned, w_out)

    def reduce_wide(left, theirs, weight, share):
        part = call(part_kernel, shape_of(split, F32), [VM] * 2)(left, weight)
        summed = (part + other_core(theirs).astype(F32)).astype(BF16)
        got = spread_wide(summed.reshape(peers, rows, quarter))
        got = got.reshape(EXPERTS, peers // EXPERTS, rows, quarter).astype(F32)
        return jnp.sum(jnp.sum(got, axis=1) * share.T[:, :, None], axis=0)

    kept = lax.dynamic_slice_in_dim(inputs, rep * quarter, quarter, 1).astype(F32)
    hidden = kept + reduce_wide(answers, theirs, w_out, shares[:, 0])
    copies = jnp.broadcast_to(hidden.astype(BF16)[None], (peers, rows, quarter))
    copies, *weights = lax.optimization_barrier(
        (copies, w_gate.transpose(0, 2, 1), w_up.transpose(0, 2, 1))
    )
    block = spread_wide(copies)
    block, *weights = lax.optimization_barrier((block, *fetch(*weights)))
    units, theirs, down = call(
        expert_kernel,
        [
            shape_of((total, w_down.shape[1])),
            shape_of(split),
            pltpu.VMEM(w_down.shape, BF16),
        ],
        [VM] * 5 + [FAR],
        [pltpu.SemaphoreType.DMA],
    )(
        block.reshape(split),
        other_core(block).reshape(split),
        norm_gains,
        *[in_vmem(w) for w in weights],
        in_hbm(w_down),
    )
    feed = reduce_wide(units, theirs, in_vmem(down), shares[:, 1])
    piece = (hidden + feed).astype(BF16)
    pieces = [piece] + [
        lax.ppermute(piece, "rep", [(p, p ^ m) for p in range(rep_count)])
        for m in range(1, rep_count)
    ]
    return call(place_kernel, shape_of((mine, 2, width)), [VM] * rep_count)(*pieces)


def solution(mesh):
    in_specs = (
        P("req", None, None),
        P(),
        P(None, None, "rep"),
        P("req", None, "rep"),
        P("req", "rep", None),
        P("req", None, "rep"),
        P("req", None, "rep"),
        P("req", "rep", None),
        P("req", None, None, "rep"),
        P("req", None),
        P("req"),
        P("req", None, None, None),
        P("req", None, None, None),
        P("req"),
    )
    out_specs = P("req", None, None)
    return jax.shard_map(shards, mesh=mesh, in_specs=in_specs, out_specs=out_specs, check_vma=False)
```

```python
import functools
import math

import jax
import jax.numpy as jnp
from jax import lax
from jax.experimental import pallas as pl
from jax.experimental.pallas import tpu as pltpu
from jax.sharding import PartitionSpec as P

HD = 128
EXPERTS = 8
SPAN = 256
EPSILON = 1e-06
MASKED = -1e30
F32 = jnp.float32
BF16 = jnp.bfloat16
VM = pl.BlockSpec(memory_space=pltpu.VMEM)
SM = pl.BlockSpec(memory_space=pltpu.SMEM)
FAR = pl.BlockSpec(memory_space=pltpu.HBM)
ROWS_BY_ROWS = (((1,), (1,)), ((), ()))


def dot(a, b):
    return jnp.dot(a, b, preferred_element_type=F32)


def dot_rows(a, b):
    return lax.dot_general(a, b, ROWS_BY_ROWS, preferred_element_type=F32)


def call(body, out, ins, scratch=(), limit=12, outs=None):
    many = isinstance(out, (list, tuple))
    return pl.pallas_call(
        body,
        out_shape=out,
        in_specs=ins,
        out_specs=outs or ([VM] * len(out) if many else VM),
        scratch_shapes=scratch,
        compiler_params=pltpu.CompilerParams(vmem_limit_bytes=limit << 20),
    )


def in_hbm(value):
    return pltpu.with_memory_space_constraint(value, pltpu.HBM)


def in_vmem(value):
    return pltpu.with_memory_space_constraint(value, pltpu.VMEM)


def shape_of(shape, dtype=BF16):
    return jax.ShapeDtypeStruct(shape, dtype)


def message_kernel(slots_far, ids_far, tokens_far, gains_far, out, slots, ids, tokens, gains, sems):
    pairs = ((slots_far, slots), (ids_far, ids), (tokens_far, tokens), (gains_far, gains))
    copies = [pltpu.make_async_copy(a, b, sems.at[i]) for i, (a, b) in enumerate(pairs)]
    for copy in copies:
        copy.start()
    for copy in copies:
        copy.wait()
    count, _, width = tokens.shape
    rows = 2 * count
    half = width // 2
    rank, core = lax.axis_index("req"), lax.axis_index("rep") % 2
    x = tokens[...].reshape(rows, width).astype(F32)
    scaling = lax.rsqrt(jnp.mean(x * x, axis=1, keepdims=True) + EPSILON)
    normed = (x * scaling * gains[0:1]).astype(BF16)
    out[0, :, :half] = jnp.where(core == 0, normed[:, :half], normed[:, half:])
    row = lax.broadcasted_iota(jnp.int32, (rows, HD), 0)
    lane = lax.broadcasted_iota(jnp.int32, (rows, HD), 1)
    notes = jnp.zeros((rows, HD), jnp.int32)
    for j in range(count):
        for s in range(2):
            here = row == 2 * j + s
            source = 2 * (rank * count + j) if s == 0 else 2 * slots[j] + 1
            notes = jnp.where(here & (lane == 0), source, notes)
            for k in range(2):
                notes = jnp.where(here & (lane == 1 + k), ids[0, s, k, j], notes)
    out[0, :, half:] = notes.astype(F32).astype(BF16)
    message = out[0]
    for r in range(1, out.shape[0]):
        out[r] = message


def order_of(notes):
    source = notes[:, :1]
    column = lax.broadcasted_iota(jnp.int32, (notes.shape[0], notes.shape[0]), 1)
    return (source.astype(jnp.int32) == column).astype(BF16)


def near_query_kernel(near, wq_far, wq, out, sem):
    load = pltpu.make_async_copy(wq_far, wq, sem)
    load.start()
    peers, rows, wide = near.shape
    half = wide - HD
    core = lax.axis_index("rep") % 2
    a = near[:, :, :half].reshape(peers * rows, half)
    load.wait()
    out[...] = dot(a, wq[0, pl.ds(pl.multiple_of(core * half, half), half)])


def query_kernel(near, far, wq, begun, out, notes):
    peers, rows, wide = near.shape
    half = wide - HD
    core = lax.axis_index("rep") % 2
    b = far[:, :, :half].reshape(peers * rows, half)
    q = begun[...] + dot(b, wq[0, pl.ds(pl.multiple_of((1 - core) * half, half), half)])
    marks = near[:, :, half:].reshape(peers * rows, HD)
    notes[...] = marks
    out[...] = dot(order_of(marks), q.astype(BF16)).astype(BF16).reshape(out.shape)


def own_kernel(near, far, wkv, sel, fresh):
    peers, rows, wide = near.shape
    half = wide - HD
    rank, core = lax.axis_index("req"), lax.axis_index("rep") % 2
    source = near[rank][:, half : half + 1]
    column = lax.broadcasted_iota(jnp.int32, (rows, peers * rows), 1)
    order = (source.astype(jnp.int32) == column).astype(BF16)
    a = dot(order, near[...].reshape(peers * rows, wide))
    b = dot(order, far[:, :, :half].reshape(peers * rows, half)).astype(BF16)
    sel[...] = a[:, half:]
    a = a[:, :half].astype(BF16)
    parts = (jnp.where(core == 0, a, b), jnp.where(core == 0, b, a))
    spans = half // HD
    chunks = [part[:, c * HD : (c + 1) * HD] for part in parts for c in range(spans)]
    twice = (HD, 2 * HD)
    feature = lax.broadcasted_iota(jnp.int32, twice, 1) // 2
    doubling = (lax.broadcasted_iota(jnp.int32, twice, 0) == feature).astype(BF16)
    doubled = dot(jnp.concatenate(chunks, axis=0), doubling)
    even = lax.broadcasted_iota(jnp.int32, (rows, 2 * HD), 1) % 2 == 0
    total = jnp.zeros(fresh.shape, F32)
    for c in range(2 * spans):
        v = doubled[c * rows : (c + 1) * rows]
        v = jnp.concatenate([jnp.where(even, v, 0.0), jnp.where(even, 0.0, v)], axis=0)
        w = wkv[c * HD : (c + 1) * HD].reshape(2 * HD, fresh.shape[1])
        total = total + dot(v.astype(BF16), w)
    fresh[...] = total.astype(BF16)


def page_kernel(table_far, lens_far, pool, start, out, table, lens, staged, sems, back, small):
    first = pltpu.make_async_copy(table_far, table, small.at[0])
    second = pltpu.make_async_copy(lens_far, lens, small.at[1])
    first.start()
    second.start()
    first.wait()
    second.wait()
    count = out.shape[0]
    page = pool.shape[1]
    chunks = 1 + out.shape[1] // SPAN

    def each(act):
        for j in range(count):
            for c in range(chunks):
                pl.when(c * SPAN < lens[j])(functools.partial(act, j, c))

    def block_of(j, c):
        return start.at[j] if c == 0 else staged.at[j, pl.ds((c - 1) * SPAN, SPAN)]

    def read(j, c):
        block = block_of(j, c)
        for p in range(SPAN // page):
            pltpu.make_async_copy(
                pool.at[table[j, c * (SPAN // page) + p]],
                block.at[pl.ds(p * page, page)],
                sems.at[j, c],
            ).start()

    def write(j, c):
        place = out.at[j, pl.ds((c - 1) * SPAN, SPAN)]
        return pltpu.make_async_copy(block_of(j, c), place, back.at[j, c])

    def forward(j, c):
        block = block_of(j, c)
        pltpu.make_async_copy(block, block, sems.at[j, c]).wait()
        if c:
            write(j, c).start()

    def finish(j, c):
        if c:
            write(j, c).wait()

    each(read)
    each(forward)
    each(finish)


def attention_kernel(lens, sel, arrived, fresh, start, far, out, cache, qs, os, sc, ef, sems):
    def copy_of(j, c):
        span = pl.ds((c - 1) * SPAN, SPAN)
        return pltpu.make_async_copy(far.at[j, span], cache.at[j, span], sems.at[j, c])

    count, _, _, wide = cache.shape
    for c in range(1, 1 + cache.shape[1] // SPAN):
        for j in range(count):

            @pl.when(c * SPAN < lens[j])
            def _(j=j, c=c):
                copy_of(j, c).start()

    peers, rows, _ = arrived.shape
    heads = wide // HD
    group = 2 * heads
    inv_scale = 1.0 / math.sqrt(HD)
    picks = sel[...]
    masks = [[picks[:, 1 + k : 2 + k] == float(e) for e in range(EXPERTS)] for k in range(2)]
    for h in range(heads):
        values = [arrived[e * heads + h].astype(F32) for e in range(EXPERTS)]
        for k in range(2):
            total = jnp.where(masks[k][0], values[0], 0.0)
            for e in range(1, EXPERTS):
                total = total + jnp.where(masks[k][e], values[e], 0.0)
            qs[k * heads + h] = total
    ef[...] = jnp.zeros_like(ef)
    ef[0 : 2 * rows] = fresh[...]
    extra = ef[...]
    big = (2 * group, wide)
    block_row = lax.broadcasted_iota(jnp.int32, big, 0) % heads
    diagonal = block_row == lax.broadcasted_iota(jnp.int32, big, 1) // HD
    scores_shape = (2 * group, 2 * SPAN)
    column = lax.broadcasted_iota(jnp.int32, scores_shape, 1)
    keys = column % 2 == 0
    e_col = lax.broadcasted_iota(jnp.int32, (2 * group, HD), 1)
    e_row = lax.broadcasted_iota(jnp.int32, (2 * group, HD), 0)
    requests = range(count)

    def first(j):
        return start[j].reshape(2 * SPAN, wide)

    def block(j, c):
        return cache[j, pl.ds((c - 1) * SPAN, SPAN)].reshape(2 * SPAN, wide)

    def masked_scores(q, rows_of, j, c):
        s = dot_rows(q, rows_of) * inv_scale
        return jnp.where(keys & (column < 2 * (lens[j] - c * SPAN)), s, MASKED)

    def highest(s):
        return jnp.max(s, axis=1, keepdims=True)

    def added(p):
        return jnp.sum(p, axis=1, keepdims=True)

    def onto_values(p, distance=1):
        return pltpu.roll(p, distance, 1).astype(BF16)

    chunks = [(lens[j] + SPAN - 1) // SPAN for j in requests]
    queries, extras, firsts, tops = [], [], [], []
    for j in requests:
        q = jnp.concatenate([qs[:, 2 * j, :], qs[:, 2 * j + 1, :]], axis=0)
        q = jnp.where(diagonal, jnp.concatenate([q] * heads, axis=1), 0.0).astype(BF16)
        live = (e_col == 2 * j) | ((e_col == 2 * j + 1) & (e_row >= group))
        e = jnp.where(live, dot_rows(q, extra) * inv_scale, MASKED)
        s = masked_scores(q, first(j), j, 0)
        queries.append(q)
        extras.append(e)
        firsts.append(s)
        tops.append(jnp.maximum(highest(e), highest(s)))

    for j in requests:

        def score(c, top, j=j):
            copy_of(j, c).wait()
            s = masked_scores(queries[j], block(j, c), j, c)
            sc[j, c - 1] = s
            return jnp.maximum(top, highest(s))

        tops[j] = lax.fori_loop(1, chunks[j], score, tops[j])

    extras = [jnp.exp(extras[j] - tops[j]) for j in requests]
    firsts = [jnp.exp(firsts[j] - tops[j]) for j in requests]
    sums = [added(extras[j]) + added(firsts[j]) for j in requests]
    mixed = [
        dot(onto_values(extras[j], rows), extra) + dot(onto_values(firsts[j]), first(j))
        for j in requests
    ]
    for j in requests:

        def gather(c, state, j=j):
            p = jnp.exp(sc[j, c - 1] - tops[j])
            return state[0] + added(p), state[1] + dot(onto_values(p), block(j, c))

        sums[j], mixed[j] = lax.fori_loop(1, chunks[j], gather, (sums[j], mixed[j]))

    for j in requests:
        kept = jnp.where(diagonal, mixed[j], 0.0)
        o = kept[:, :HD]
        for h in range(1, heads):
            o = o + kept[:, h * HD : (h + 1) * HD]
        o = o / sums[j]
        os[:, 2 * j, :] = o[:group]
        os[:, 2 * j + 1, :] = o[group:]
    for h in range(heads):
        one, two = os[h], os[heads + h]
        for e in range(EXPERTS):
            value = jnp.where(masks[0][e], one, 0.0) + jnp.where(masks[1][e], two, 0.0)
            out[e * heads + h] = value.astype(BF16)


def columns_of(z, core, quarter):
    return pl.ds(pl.multiple_of((2 * z + core) * quarter, quarter), quarter)


def project_kernel(notes, returned, wo, answers, theirs):
    peers, halves, rows, quarter = theirs.shape
    core = lax.axis_index("rep") % 2
    values = returned[...].reshape(peers * rows, returned.shape[2])
    a = lax.dot_general(
        order_of(notes[...]), values, (((0,), (0,)), ((), ())), preferred_element_type=F32
    ).astype(BF16)
    answers[...] = a
    for z in range(halves):
        part = dot(a, wo[0, :, columns_of(z, 1 - core, quarter)])
        theirs[:, z] = part.astype(BF16).reshape(peers, rows, quarter)


def part_kernel(left, weight, out):
    peers, halves, rows, quarter = out.shape
    core = lax.axis_index("rep") % 2
    a = left[...]
    for z in range(halves):
        part = dot(a, weight[0, :, columns_of(z, core, quarter)])
        out[:, z] = part.reshape(peers, rows, quarter)


def place_kernel(*refs):
    pieces, out = refs[:-1], refs[-1]
    rep = lax.axis_index("rep")
    count, _, width = out.shape
    quarter = width // len(pieces)
    for m, piece in enumerate(pieces):
        place = pl.multiple_of((rep ^ m) * quarter, quarter)
        out[:, :, pl.ds(place, quarter)] = piece[...].reshape(count, 2, quarter)


def raw_products(block, side, gains, wg, wu):
    peers, halves, rows, quarter = block.shape
    total = peers * rows
    squares = jnp.zeros((total, 1), F32)
    gate = jnp.zeros((total, wg.shape[1]), F32)
    up = jnp.zeros((total, wg.shape[1]), F32)
    for z in range(halves):
        where = columns_of(z, side, quarter)
        v = block[:, z].reshape(total, quarter).astype(F32)
        squares = squares + jnp.sum(v * v, axis=1, keepdims=True)
        v = (v * gains[1:2, where]).astype(BF16)
        gate = gate + dot_rows(v, wg[0, :, where])
        up = up + dot_rows(v, wu[0, :, where])
    return squares, gate, up


def near_kernel(near, gains, wg_far, wu_far, wd_far, wg, wu, wd, squares, gate, up, sems):
    pairs = ((wg_far, wg), (wu_far, wu), (wd_far, wd))
    copies = [pltpu.make_async_copy(a, b, sems.at[i]) for i, (a, b) in enumerate(pairs)]
    for copy in copies:
        copy.start()
    core = lax.axis_index("rep") % 2
    copies[0].wait()
    copies[1].wait()
    a, b, c = raw_products(near, core, gains, wg, wu)
    squares[...] = jnp.broadcast_to(a, squares.shape)
    gate[...] = b
    up[...] = c
    copies[2].wait()


def expert_kernel(far, gains, wg, wu, wd, near_squares, near_gate, near_up, units, theirs):
    peers, halves, rows, quarter = far.shape
    core = lax.axis_index("rep") % 2
    squares, gate, up = raw_products(far, 1 - core, gains, wg, wu)
    squares = squares + near_squares[:, :1]
    scaling = lax.rsqrt(squares / (2 * halves * quarter) + EPSILON)
    gate = (gate + near_gate[...]) * scaling
    up = (up + near_up[...]) * scaling
    a = (gate / (1.0 + jnp.exp(-gate)) * up).astype(BF16)
    units[...] = a
    for z in range(halves):
        part = dot(a, wd[0, :, columns_of(z, 1 - core, quarter)])
        theirs[:, z] = part.astype(BF16).reshape(peers, rows, quarter)


def shards(
    tokens,
    norm_gains,
    w_kv,
    w_query,
    w_out,
    w_gate,
    w_up,
    w_down,
    kv_pages,
    page_table,
    cache_len,
    route_ids,
    route_gates,
    new_slot,
):
    req_count = lax.axis_size("req")
    rep_count = lax.axis_size("rep")
    mine, _, width = tokens.shape
    rows = 2 * mine
    total = rows * req_count
    half = width // 2
    quarter = width // rep_count
    wide = kv_pages.shape[-1]
    rep = lax.axis_index("rep")
    swap = [(p, p ^ 1) for p in range(rep_count)]
    wide_groups = [
        [r * rep_count + 2 * z + c for r in range(req_count) for z in range(rep_count // 2)]
        for c in range(2)
    ]
    peers = req_count * rep_count // 2
    split = (req_count, rep_count // 2, rows, quarter)

    def spread_req(value):
        return lax.all_to_all(value, "req", split_axis=0, concat_axis=0, tiled=True)

    def spread_wide(value):
        return lax.all_to_all(
            value,
            ("req", "rep"),
            split_axis=0,
            concat_axis=0,
            tiled=True,
            axis_index_groups=wide_groups,
        )

    def other_core(value):
        return lax.ppermute(value, "rep", swap)

    inputs = tokens.reshape(rows, width)
    ids = route_ids.transpose(0, 2, 1, 3).reshape(rows, 2, 2)
    gates = route_gates.astype(F32).transpose(0, 2, 1, 3).reshape(rows, 2, 2)
    experts_row = jnp.arange(EXPERTS, dtype=jnp.int32)
    shares = jnp.sum(jnp.where(ids[..., None] == experts_row, gates[..., None], 0.0), axis=2)
    shares = shares.transpose(1, 2, 0)[..., None]
    shares = [shares[0], shares[1]]
    kept = lax.dynamic_slice_in_dim(inputs, rep * quarter, quarter, 1).astype(F32)

    routes = route_ids.transpose(1, 2, 3, 0)
    message = call(
        message_kernel,
        shape_of((req_count, rows, half + HD)),
        [FAR] * 4,
        [
            pltpu.SMEM(new_slot.shape, jnp.int32),
            pltpu.SMEM(routes.shape, jnp.int32),
            pltpu.VMEM(tokens.shape, BF16),
            pltpu.VMEM(norm_gains.shape, F32),
            pltpu.SemaphoreType.DMA((4,)),
        ],
    )(in_hbm(new_slot), in_hbm(routes), in_hbm(tokens), in_hbm(norm_gains))
    near = spread_req(message)
    length = page_table.shape[1] * kv_pages.shape[1]
    tail = (mine, length - SPAN) + kv_pages.shape[2:]
    start, cache = call(
        page_kernel,
        [pltpu.VMEM((mine, SPAN) + kv_pages.shape[2:], BF16), pltpu.HBM(tail, BF16)],
        [FAR] * 3,
        [
            pltpu.SMEM(page_table.shape, jnp.int32),
            pltpu.SMEM(cache_len.shape, jnp.int32),
            pltpu.VMEM(tail, BF16),
            pltpu.SemaphoreType.DMA((mine, length // SPAN)),
            pltpu.SemaphoreType.DMA((mine, length // SPAN)),
            pltpu.SemaphoreType.DMA((2,)),
        ],
        outs=[VM, FAR],
    )(in_hbm(page_table), in_hbm(cache_len), in_hbm(kv_pages))
    near, start, cache, shares, kept = lax.optimization_barrier(
        (near, start, cache, shares, kept)
    )
    far = other_core(near)
    wq, begun = call(
        near_query_kernel,
        [pltpu.VMEM(w_query.shape, BF16), shape_of((total, HD), F32)],
        [VM, FAR],
        [pltpu.SemaphoreType.DMA],
    )(near, in_hbm(w_query))
    ordered, notes = call(
        query_kernel, [shape_of((req_count, rows, HD)), shape_of((total, HD))], [VM] * 4
    )(near, far, in_vmem(wq), begun)
    arrived = spread_req(ordered)
    sel, fresh = call(
        own_kernel, [shape_of((rows, HD), F32), shape_of((2 * rows, wide))], [VM] * 3
    )(near, far, w_kv)
    back = call(
        attention_kernel,
        shape_of((req_count, rows, HD)),
        [SM, VM, VM, VM, VM, FAR],
        [
            pltpu.VMEM(cache.shape, BF16),
            pltpu.VMEM((2 * wide // HD, rows, HD), F32),
            pltpu.VMEM((2 * wide // HD, rows, HD), F32),
            pltpu.VMEM((mine, length // SPAN - 1, 4 * wide // HD, 2 * SPAN), F32),
            pltpu.VMEM((HD, wide), BF16),
            pltpu.SemaphoreType.DMA((mine, length // SPAN)),
        ],
        16,
    )(cache_len, sel, arrived, fresh, in_vmem(start), in_hbm(cache))
    returned = spread_req(back)
    answers, theirs = call(
        project_kernel, [shape_of((total, w_out.shape[1])), shape_of(split)], [VM] * 3
    )(notes, returned, w_out)

    def reduce_wide(left, theirs, weight, share):
        part = call(part_kernel, shape_of(split, F32), [VM] * 2)(left, weight)
        summed = (part + other_core(theirs).astype(F32)).astype(BF16)
        got = spread_wide(summed.reshape(peers, rows, quarter))
        got = got.reshape(EXPERTS, peers // EXPERTS, rows, quarter).astype(F32)
        return jnp.sum(jnp.sum(got, axis=1) * share, axis=0)

    hidden = kept + reduce_wide(answers, theirs, w_out, shares[0])
    copies = jnp.broadcast_to(hidden.astype(BF16)[None], (peers, rows, quarter))
    block = spread_wide(copies)
    far = other_core(block).reshape(split)
    block, *weights = lax.optimization_barrier(
        (block, w_gate.transpose(0, 2, 1), w_up.transpose(0, 2, 1), w_down)
    )
    units_dev = w_down.shape[1]
    wg, wu, wd, squares, gate, up = call(
        near_kernel,
        [pltpu.VMEM(w.shape, BF16) for w in weights]
        + [shape_of((total, HD), F32)]
        + [shape_of((total, units_dev), F32)] * 2,
        [VM, VM, FAR, FAR, FAR],
        [pltpu.SemaphoreType.DMA((3,))],
    )(block.reshape(split), norm_gains, *[in_hbm(w) for w in weights])
    units, theirs = call(
        expert_kernel, [shape_of((total, units_dev)), shape_of(split)], [VM] * 8
    )(far, norm_gains, in_vmem(wg), in_vmem(wu), in_vmem(wd), squares, gate, up)
    feed = reduce_wide(units, theirs, in_vmem(wd), shares[1])
    piece = (hidden + feed).astype(BF16)
    pieces = [piece] + [
        lax.ppermute(piece, "rep", [(p, p ^ m) for p in range(rep_count)])
        for m in range(1, rep_count)
    ]
    return call(place_kernel, shape_of((mine, 2, width)), [VM] * rep_count)(*pieces)


def solution(mesh):
    in_specs = (
        P("req", None, None),
        P(),
        P(None, None, "rep"),
        P("req", None, "rep"),
        P("req", "rep", None),
        P("req", None, "rep"),
        P("req", None, "rep"),
        P("req", "rep", None),
        P("req", None, None, "rep"),
        P("req", None),
        P("req"),
        P("req", None, None, None),
        P("req", None, None, None),
        P("req"),
    )
    out_specs = P("req", None, None)
    return jax.shard_map(shards, mesh=mesh, in_specs=in_specs, out_specs=out_specs, check_vma=False)
```

```python
import functools
import math

import jax
import jax.numpy as jnp
from jax import lax
from jax.experimental import pallas as pl
from jax.experimental.pallas import tpu as pltpu
from jax.sharding import PartitionSpec as P

HD = 128
EXPERTS = 8
SPAN = 256
EPSILON = 1e-06
MASKED = -1e30
F32 = jnp.float32
BF16 = jnp.bfloat16
VM = pl.BlockSpec(memory_space=pltpu.VMEM)
SM = pl.BlockSpec(memory_space=pltpu.SMEM)
FAR = pl.BlockSpec(memory_space=pltpu.HBM)
ROWS_BY_ROWS = (((1,), (1,)), ((), ()))


def dot(a, b):
    return jnp.dot(a, b, preferred_element_type=F32)


def dot_rows(a, b):
    return lax.dot_general(a, b, ROWS_BY_ROWS, preferred_element_type=F32)


def call(body, out, ins, scratch=(), limit=12, outs=None):
    many = isinstance(out, (list, tuple))
    return pl.pallas_call(
        body,
        out_shape=out,
        in_specs=ins,
        out_specs=outs or ([VM] * len(out) if many else VM),
        scratch_shapes=scratch,
        compiler_params=pltpu.CompilerParams(vmem_limit_bytes=limit << 20),
    )


def in_hbm(value):
    return pltpu.with_memory_space_constraint(value, pltpu.HBM)


def in_vmem(value):
    return pltpu.with_memory_space_constraint(value, pltpu.VMEM)


def shape_of(shape, dtype=BF16):
    return jax.ShapeDtypeStruct(shape, dtype)


def message_kernel(slots_far, ids_far, tokens_far, gains_far, out, slots, ids, tokens, gains, sems):
    pairs = ((slots_far, slots), (ids_far, ids), (tokens_far, tokens), (gains_far, gains))
    copies = [pltpu.make_async_copy(a, b, sems.at[i]) for i, (a, b) in enumerate(pairs)]
    for copy in copies:
        copy.start()
    for copy in copies:
        copy.wait()
    count, _, width = tokens.shape
    rows = 2 * count
    half = width // 2
    rank, core = lax.axis_index("req"), lax.axis_index("rep") % 2
    x = tokens[...].reshape(rows, width).astype(F32)
    scaling = lax.rsqrt(jnp.mean(x * x, axis=1, keepdims=True) + EPSILON)
    normed = (x * scaling * gains[0:1]).astype(BF16)
    out[0, :, :half] = jnp.where(core == 0, normed[:, :half], normed[:, half:])
    row = lax.broadcasted_iota(jnp.int32, (rows, HD), 0)
    lane = lax.broadcasted_iota(jnp.int32, (rows, HD), 1)
    notes = jnp.zeros((rows, HD), jnp.int32)
    for j in range(count):
        for s in range(2):
            here = row == 2 * j + s
            source = 2 * (rank * count + j) if s == 0 else 2 * slots[j] + 1
            notes = jnp.where(here & (lane == 0), source, notes)
            for k in range(2):
                notes = jnp.where(here & (lane == 1 + k), ids[0, s, k, j], notes)
    out[0, :, half:] = notes.astype(F32).astype(BF16)
    message = out[0]
    for r in range(1, out.shape[0]):
        out[r] = message


def order_of(notes):
    source = notes[:, :1]
    column = lax.broadcasted_iota(jnp.int32, (notes.shape[0], notes.shape[0]), 1)
    return (source.astype(jnp.int32) == column).astype(BF16)


def near_query_kernel(near, wq_far, wq, out, sem):
    load = pltpu.make_async_copy(wq_far, wq, sem)
    load.start()
    peers, rows, wide = near.shape
    half = wide - HD
    core = lax.axis_index("rep") % 2
    a = near[:, :, :half].reshape(peers * rows, half)
    load.wait()
    out[...] = dot(a, wq[0, pl.ds(pl.multiple_of(core * half, half), half)])


def query_kernel(near, far, wq, begun, out, notes):
    peers, rows, wide = near.shape
    half = wide - HD
    core = lax.axis_index("rep") % 2
    b = far[:, :, :half].reshape(peers * rows, half)
    q = begun[...] + dot(b, wq[0, pl.ds(pl.multiple_of((1 - core) * half, half), half)])
    marks = near[:, :, half:].reshape(peers * rows, HD)
    notes[...] = marks
    out[...] = dot(order_of(marks), q.astype(BF16)).astype(BF16).reshape(out.shape)


def own_kernel(near, far, wkv, sel, fresh):
    peers, rows, wide = near.shape
    half = wide - HD
    rank, core = lax.axis_index("req"), lax.axis_index("rep") % 2
    source = near[rank][:, half : half + 1]
    column = lax.broadcasted_iota(jnp.int32, (rows, peers * rows), 1)
    order = (source.astype(jnp.int32) == column).astype(BF16)
    a = dot(order, near[...].reshape(peers * rows, wide))
    b = dot(order, far[:, :, :half].reshape(peers * rows, half)).astype(BF16)
    sel[...] = a[:, half:]
    a = a[:, :half].astype(BF16)
    parts = (jnp.where(core == 0, a, b), jnp.where(core == 0, b, a))
    spans = half // HD
    chunks = [part[:, c * HD : (c + 1) * HD] for part in parts for c in range(spans)]
    twice = (HD, 2 * HD)
    feature = lax.broadcasted_iota(jnp.int32, twice, 1) // 2
    doubling = (lax.broadcasted_iota(jnp.int32, twice, 0) == feature).astype(BF16)
    doubled = dot(jnp.concatenate(chunks, axis=0), doubling)
    even = lax.broadcasted_iota(jnp.int32, (rows, 2 * HD), 1) % 2 == 0
    total = jnp.zeros(fresh.shape, F32)
    for c in range(2 * spans):
        v = doubled[c * rows : (c + 1) * rows]
        v = jnp.concatenate([jnp.where(even, v, 0.0), jnp.where(even, 0.0, v)], axis=0)
        w = wkv[c * HD : (c + 1) * HD].reshape(2 * HD, fresh.shape[1])
        total = total + dot(v.astype(BF16), w)
    fresh[...] = total.astype(BF16)


def page_kernel(table_far, lens_far, pool, start, out, table, lens, staged, sems, back, small):
    first = pltpu.make_async_copy(table_far, table, small.at[0])
    second = pltpu.make_async_copy(lens_far, lens, small.at[1])
    first.start()
    second.start()
    first.wait()
    second.wait()
    count = out.shape[0]
    page = pool.shape[1]
    chunks = 1 + out.shape[1] // SPAN

    def each(act):
        for c in range(chunks):
            for j in range(count):
                if c < 2:
                    act(j, c)
                else:
                    pl.when(lens[j] > 2 * SPAN)(functools.partial(act, j, c))

    def block_of(j, c):
        return start.at[j] if c == 0 else staged.at[j, pl.ds((c - 1) * SPAN, SPAN)]

    def read(j, c):
        block = block_of(j, c)
        for p in range(SPAN // page):
            pltpu.make_async_copy(
                pool.at[table[j, c * (SPAN // page) + p]],
                block.at[pl.ds(p * page, page)],
                sems.at[j, c],
            ).start()

    def write(j, c):
        place = out.at[j, pl.ds((c - 1) * SPAN, SPAN)]
        return pltpu.make_async_copy(block_of(j, c), place, back.at[j, c])

    def forward(j, c):
        block = block_of(j, c)
        pltpu.make_async_copy(block, block, sems.at[j, c]).wait()
        if c:
            write(j, c).start()

    def finish(j, c):
        if c:
            write(j, c).wait()

    each(read)
    each(forward)
    each(finish)


def pages_call(table, lens, pool):
    mine, pages = table.shape
    length = pages * pool.shape[1]
    tail = (mine, length - SPAN) + pool.shape[2:]
    return call(
        page_kernel,
        [pltpu.VMEM((mine, SPAN) + pool.shape[2:], BF16), pltpu.HBM(tail, BF16)],
        [FAR] * 3,
        [
            pltpu.SMEM(table.shape, jnp.int32),
            pltpu.SMEM(lens.shape, jnp.int32),
            pltpu.VMEM(tail, BF16),
            pltpu.SemaphoreType.DMA((mine, length // SPAN)),
            pltpu.SemaphoreType.DMA((mine, length // SPAN)),
            pltpu.SemaphoreType.DMA((2,)),
        ],
        outs=[VM, FAR],
    )(in_hbm(table), in_hbm(lens), in_hbm(pool))


def attention_kernel(lens, sel, arrived, fresh, start, far, out, cache, qs, os, sc, ef, sems):
    count, tail, _, wide = cache.shape
    requests = range(count)
    spans = (pl.ds(0, SPAN), pl.ds(SPAN, tail - SPAN))

    def copy_of(j, part):
        span = spans[part]
        return pltpu.make_async_copy(far.at[j, span], cache.at[j, span], sems.at[j, part])

    for j in requests:
        copy_of(j, 0).start()
    for j in requests:

        @pl.when(lens[j] > 2 * SPAN)
        def _(j=j):
            copy_of(j, 1).start()

    peers, rows, _ = arrived.shape
    heads = wide // HD
    group = 2 * heads
    inv_scale = 1.0 / math.sqrt(HD)
    picks = sel[...]
    masks = [[picks[:, 1 + k : 2 + k] == float(e) for e in range(EXPERTS)] for k in range(2)]
    for h in range(heads):
        values = [arrived[e * heads + h].astype(F32) for e in range(EXPERTS)]
        for k in range(2):
            total = jnp.where(masks[k][0], values[0], 0.0)
            for e in range(1, EXPERTS):
                total = total + jnp.where(masks[k][e], values[e], 0.0)
            qs[k * heads + h] = total
    ef[...] = jnp.zeros_like(ef)
    ef[0 : 2 * rows] = fresh[...]
    extra = ef[...]
    big = (2 * group, wide)
    block_row = lax.broadcasted_iota(jnp.int32, big, 0) % heads
    diagonal = block_row == lax.broadcasted_iota(jnp.int32, big, 1) // HD
    e_col = lax.broadcasted_iota(jnp.int32, (2 * group, HD), 1)
    e_row = lax.broadcasted_iota(jnp.int32, (2 * group, HD), 0)

    def rows_of(j, part):
        if part == 0:
            return start[j].reshape(2 * SPAN, wide)
        if part == 1:
            return cache[j, :SPAN].reshape(2 * SPAN, wide)
        return cache[j, SPAN:].reshape(2 * (tail - SPAN), wide)

    def masked_scores(q, j, part):
        s = dot_rows(q, rows_of(j, part)) * inv_scale
        column = lax.broadcasted_iota(jnp.int32, s.shape, 1)
        return jnp.where(
            (column % 2 == 0) & (column < 2 * (lens[j] - part * SPAN)), s, MASKED
        )

    def highest(s):
        return jnp.max(s, axis=1, keepdims=True)

    def added(p):
        return jnp.sum(p, axis=1, keepdims=True)

    def onto_values(p, distance=1):
        return pltpu.roll(p, distance, 1).astype(BF16)

    longer = [jnp.where(lens[j] > 2 * SPAN, 1, 0) for j in requests]
    queries, extras, firsts, seconds, tops = [], [], [], [], []
    for j in requests:
        q = jnp.concatenate([qs[:, 2 * j, :], qs[:, 2 * j + 1, :]], axis=0)
        q = jnp.where(diagonal, jnp.concatenate([q] * heads, axis=1), 0.0).astype(BF16)
        live = (e_col == 2 * j) | ((e_col == 2 * j + 1) & (e_row >= group))
        queries.append(q)
        extras.append(jnp.where(live, dot_rows(q, extra) * inv_scale, MASKED))
        firsts.append(masked_scores(q, j, 0))
    for j in requests:
        copy_of(j, 0).wait()
    for j in requests:
        seconds.append(masked_scores(queries[j], j, 1))
        top = jnp.maximum(highest(extras[j]), highest(firsts[j]))
        tops.append(jnp.maximum(top, highest(seconds[j])))

    for j in requests:

        def score(_, top, j=j):
            copy_of(j, 1).wait()
            s = masked_scores(queries[j], j, 2)
            sc[j] = s
            return jnp.maximum(top, highest(s))

        tops[j] = lax.fori_loop(0, longer[j], score, tops[j])

    extras = [jnp.exp(extras[j] - tops[j]) for j in requests]
    firsts = [jnp.exp(firsts[j] - tops[j]) for j in requests]
    seconds = [jnp.exp(seconds[j] - tops[j]) for j in requests]
    sums = [added(extras[j]) + added(firsts[j]) + added(seconds[j]) for j in requests]
    mixed = [
        dot(onto_values(extras[j], rows), extra)
        + dot(onto_values(firsts[j]), rows_of(j, 0))
        + dot(onto_values(seconds[j]), rows_of(j, 1))
        for j in requests
    ]
    for j in requests:

        def gather(_, state, j=j):
            p = jnp.exp(sc[j] - tops[j])
            return state[0] + added(p), state[1] + dot(onto_values(p), rows_of(j, 2))

        sums[j], mixed[j] = lax.fori_loop(0, longer[j], gather, (sums[j], mixed[j]))

    for j in requests:
        kept = jnp.where(diagonal, mixed[j], 0.0)
        o = kept[:, :HD]
        for h in range(1, heads):
            o = o + kept[:, h * HD : (h + 1) * HD]
        o = o / sums[j]
        os[:, 2 * j, :] = o[:group]
        os[:, 2 * j + 1, :] = o[group:]
    for h in range(heads):
        one, two = os[h], os[heads + h]
        for e in range(EXPERTS):
            value = jnp.where(masks[0][e], one, 0.0) + jnp.where(masks[1][e], two, 0.0)
            out[e * heads + h] = value.astype(BF16)


def attention_call(lens, sel, arrived, fresh, start, cache):
    rows, wide = arrived.shape[1], cache.shape[-1]
    mine, tail = cache.shape[:2]
    pairs = 2 * wide // HD
    return call(
        attention_kernel,
        shape_of(arrived.shape),
        [SM, VM, VM, VM, VM, FAR],
        [
            pltpu.VMEM(cache.shape, BF16),
            pltpu.VMEM((pairs, rows, HD), F32),
            pltpu.VMEM((pairs, rows, HD), F32),
            pltpu.VMEM((mine, 2 * pairs, 2 * (tail - SPAN)), F32),
            pltpu.VMEM((HD, wide), BF16),
            pltpu.SemaphoreType.DMA((mine, 2)),
        ],
        16,
    )(lens, sel, arrived, fresh, in_vmem(start), in_hbm(cache))


def columns_of(z, core, quarter):
    return pl.ds(pl.multiple_of((2 * z + core) * quarter, quarter), quarter)


def project_kernel(notes, returned, wo, answers, theirs):
    peers, halves, rows, quarter = theirs.shape
    core = lax.axis_index("rep") % 2
    values = returned[...].reshape(peers * rows, returned.shape[2])
    a = lax.dot_general(
        order_of(notes[...]), values, (((0,), (0,)), ((), ())), preferred_element_type=F32
    ).astype(BF16)
    answers[...] = a
    for z in range(halves):
        part = dot(a, wo[0, :, columns_of(z, 1 - core, quarter)])
        theirs[:, z] = part.astype(BF16).reshape(peers, rows, quarter)


def part_kernel(left, weight, out):
    peers, halves, rows, quarter = out.shape
    core = lax.axis_index("rep") % 2
    a = left[...]
    for z in range(halves):
        part = dot(a, weight[0, :, columns_of(z, core, quarter)])
        out[:, z] = part.reshape(peers, rows, quarter)


def place_kernel(*refs):
    pieces, out = refs[:-1], refs[-1]
    rep = lax.axis_index("rep")
    count, _, width = out.shape
    quarter = width // len(pieces)
    for m, piece in enumerate(pieces):
        place = pl.multiple_of((rep ^ m) * quarter, quarter)
        out[:, :, pl.ds(place, quarter)] = piece[...].reshape(count, 2, quarter)


def raw_products(block, side, gains, wg, wu):
    peers, halves, rows, quarter = block.shape
    total = peers * rows
    squares = jnp.zeros((total, 1), F32)
    gate = jnp.zeros((total, wg.shape[1]), F32)
    up = jnp.zeros((total, wg.shape[1]), F32)
    for z in range(halves):
        where = columns_of(z, side, quarter)
        v = block[:, z].reshape(total, quarter).astype(F32)
        squares = squares + jnp.sum(v * v, axis=1, keepdims=True)
        v = (v * gains[1:2, where]).astype(BF16)
        gate = gate + dot_rows(v, wg[0, :, where])
        up = up + dot_rows(v, wu[0, :, where])
    return squares, gate, up


def near_kernel(near, gains, wg, wu, squares, gate, up):
    core = lax.axis_index("rep") % 2
    a, b, c = raw_products(near, core, gains, wg, wu)
    squares[...] = jnp.broadcast_to(a, squares.shape)
    gate[...] = b
    up[...] = c


def expert_kernel(far, gains, wg, wu, wd, near_squares, near_gate, near_up, units, theirs):
    peers, halves, rows, quarter = far.shape
    core = lax.axis_index("rep") % 2
    squares, gate, up = raw_products(far, 1 - core, gains, wg, wu)
    squares = squares + near_squares[:, :1]
    scaling = lax.rsqrt(squares / (2 * halves * quarter) + EPSILON)
    gate = (gate + near_gate[...]) * scaling
    up = (up + near_up[...]) * scaling
    a = (gate / (1.0 + jnp.exp(-gate)) * up).astype(BF16)
    units[...] = a
    for z in range(halves):
        part = dot(a, wd[0, :, columns_of(z, 1 - core, quarter)])
        theirs[:, z] = part.astype(BF16).reshape(peers, rows, quarter)


def shards(
    tokens,
    norm_gains,
    w_kv,
    w_query,
    w_out,
    w_gate,
    w_up,
    w_down,
    kv_pages,
    page_table,
    cache_len,
    route_ids,
    route_gates,
    new_slot,
):
    req_count = lax.axis_size("req")
    rep_count = lax.axis_size("rep")
    mine, _, width = tokens.shape
    rows = 2 * mine
    total = rows * req_count
    half = width // 2
    quarter = width // rep_count
    wide = kv_pages.shape[-1]
    rep = lax.axis_index("rep")
    swap = [(p, p ^ 1) for p in range(rep_count)]
    wide_groups = [
        [r * rep_count + 2 * z + c for r in range(req_count) for z in range(rep_count // 2)]
        for c in range(2)
    ]
    peers = req_count * rep_count // 2
    split = (req_count, rep_count // 2, rows, quarter)

    def spread_req(value):
        return lax.all_to_all(value, "req", split_axis=0, concat_axis=0, tiled=True)

    def spread_wide(value):
        return lax.all_to_all(
            value,
            ("req", "rep"),
            split_axis=0,
            concat_axis=0,
            tiled=True,
            axis_index_groups=wide_groups,
        )

    def other_core(value):
        return lax.ppermute(value, "rep", swap)

    inputs = tokens.reshape(rows, width)
    ids = route_ids.transpose(0, 2, 1, 3).reshape(rows, 2, 2)
    gates = route_gates.astype(F32).transpose(0, 2, 1, 3).reshape(rows, 2, 2)
    experts_row = jnp.arange(EXPERTS, dtype=jnp.int32)
    shares = jnp.sum(jnp.where(ids[..., None] == experts_row, gates[..., None], 0.0), axis=2)
    shares = shares.transpose(1, 2, 0)[..., None]
    shares = [shares[0], shares[1]]
    kept = lax.dynamic_slice_in_dim(inputs, rep * quarter, quarter, 1).astype(F32)

    routes = route_ids.transpose(1, 2, 3, 0)
    message = call(
        message_kernel,
        shape_of((req_count, rows, half + HD)),
        [FAR] * 4,
        [
            pltpu.SMEM(new_slot.shape, jnp.int32),
            pltpu.SMEM(routes.shape, jnp.int32),
            pltpu.VMEM(tokens.shape, BF16),
            pltpu.VMEM(norm_gains.shape, F32),
            pltpu.SemaphoreType.DMA((4,)),
        ],
    )(in_hbm(new_slot), in_hbm(routes), in_hbm(tokens), in_hbm(norm_gains))
    near = spread_req(message)
    start, cache = pages_call(page_table, cache_len, kv_pages)
    near, start, cache, shares, kept = lax.optimization_barrier(
        (near, start, cache, shares, kept)
    )
    far = other_core(near)
    wq, begun = call(
        near_query_kernel,
        [pltpu.VMEM(w_query.shape, BF16), shape_of((total, HD), F32)],
        [VM, FAR],
        [pltpu.SemaphoreType.DMA],
    )(near, in_hbm(w_query))
    ordered, notes = call(
        query_kernel, [shape_of((req_count, rows, HD)), shape_of((total, HD))], [VM] * 4
    )(near, far, in_vmem(wq), begun)
    arrived = spread_req(ordered)
    sel, fresh = call(
        own_kernel, [shape_of((rows, HD), F32), shape_of((2 * rows, wide))], [VM] * 3
    )(near, far, w_kv)
    back = attention_call(cache_len, sel, arrived, fresh, start, cache)
    returned = spread_req(back)
    answers, theirs = call(
        project_kernel, [shape_of((total, w_out.shape[1])), shape_of(split)], [VM] * 3
    )(notes, returned, w_out)

    def reduce_wide(left, theirs, weight, share):
        part = call(part_kernel, shape_of(split, F32), [VM] * 2)(left, weight)
        summed = (part + other_core(theirs).astype(F32)).astype(BF16)
        got = spread_wide(summed.reshape(peers, rows, quarter))
        got = got.reshape(EXPERTS, peers // EXPERTS, rows, quarter).astype(F32)
        return jnp.sum(jnp.sum(got, axis=1) * share, axis=0)

    hidden = kept + reduce_wide(answers, theirs, w_out, shares[0])
    copies = jnp.broadcast_to(hidden.astype(BF16)[None], (peers, rows, quarter))
    block = spread_wide(copies)
    far = other_core(block).reshape(split)
    wg, wu = w_gate.transpose(0, 2, 1), w_up.transpose(0, 2, 1)
    units_dev = w_down.shape[1]
    squares, gate, up = call(
        near_kernel,
        [shape_of((total, HD), F32)] + [shape_of((total, units_dev), F32)] * 2,
        [VM] * 4,
    )(block.reshape(split), norm_gains, wg, wu)
    units, theirs = call(
        expert_kernel, [shape_of((total, units_dev)), shape_of(split)], [VM] * 8
    )(far, norm_gains, wg, wu, w_down, squares, gate, up)
    feed = reduce_wide(units, theirs, w_down, shares[1])
    piece = (hidden + feed).astype(BF16)
    pieces = [piece] + [
        lax.ppermute(piece, "rep", [(p, p ^ m) for p in range(rep_count)])
        for m in range(1, rep_count)
    ]
    return call(place_kernel, shape_of((mine, 2, width)), [VM] * rep_count)(*pieces)


def solution(mesh):
    in_specs = (
        P("req", None, None),
        P(),
        P(None, None, "rep"),
        P("req", None, "rep"),
        P("req", "rep", None),
        P("req", None, "rep"),
        P("req", None, "rep"),
        P("req", "rep", None),
        P("req", None, None, "rep"),
        P("req", None),
        P("req"),
        P("req", None, None, None),
        P("req", None, None, None),
        P("req"),
    )
    out_specs = P("req", None, None)
    return jax.shard_map(shards, mesh=mesh, in_specs=in_specs, out_specs=out_specs, check_vma=False)
```

```python
import functools
import math

import jax
import jax.numpy as jnp
from jax import lax
from jax.experimental import pallas as pl
from jax.experimental.pallas import tpu as pltpu
from jax.sharding import PartitionSpec as P

HD = 128
EXPERTS = 8
SPAN = 256
EPSILON = 1e-06
MASKED = -1e30
F32 = jnp.float32
BF16 = jnp.bfloat16
VM = pl.BlockSpec(memory_space=pltpu.VMEM)
SM = pl.BlockSpec(memory_space=pltpu.SMEM)
FAR = pl.BlockSpec(memory_space=pltpu.HBM)
ROWS_BY_ROWS = (((1,), (1,)), ((), ()))


def dot(a, b):
    return jnp.dot(a, b, preferred_element_type=F32)


def dot_rows(a, b):
    return lax.dot_general(a, b, ROWS_BY_ROWS, preferred_element_type=F32)


def call(body, out, ins, scratch=(), limit=12, outs=None):
    many = isinstance(out, (list, tuple))
    return pl.pallas_call(
        body,
        out_shape=out,
        in_specs=ins,
        out_specs=outs or ([VM] * len(out) if many else VM),
        scratch_shapes=scratch,
        compiler_params=pltpu.CompilerParams(vmem_limit_bytes=limit << 20),
    )


def in_hbm(value):
    return pltpu.with_memory_space_constraint(value, pltpu.HBM)


def in_vmem(value):
    return pltpu.with_memory_space_constraint(value, pltpu.VMEM)


def shape_of(shape, dtype=BF16):
    return jax.ShapeDtypeStruct(shape, dtype)


def message_kernel(slots_far, ids_far, tokens_far, gains_far, out, slots, ids, tokens, gains, sems):
    pairs = ((slots_far, slots), (ids_far, ids), (tokens_far, tokens), (gains_far, gains))
    copies = [pltpu.make_async_copy(a, b, sems.at[i]) for i, (a, b) in enumerate(pairs)]
    for copy in copies:
        copy.start()
    for copy in copies:
        copy.wait()
    count, _, width = tokens.shape
    rows = 2 * count
    half = width // 2
    rank, core = lax.axis_index("req"), lax.axis_index("rep") % 2
    x = tokens[...].reshape(rows, width).astype(F32)
    scaling = lax.rsqrt(jnp.mean(x * x, axis=1, keepdims=True) + EPSILON)
    normed = (x * scaling * gains[0:1]).astype(BF16)
    out[0, :, :half] = jnp.where(core == 0, normed[:, :half], normed[:, half:])
    row = lax.broadcasted_iota(jnp.int32, (rows, HD), 0)
    lane = lax.broadcasted_iota(jnp.int32, (rows, HD), 1)
    notes = jnp.zeros((rows, HD), jnp.int32)
    for j in range(count):
        for s in range(2):
            here = row == 2 * j + s
            source = 2 * (rank * count + j) if s == 0 else 2 * slots[j] + 1
            notes = jnp.where(here & (lane == 0), source, notes)
            for k in range(2):
                notes = jnp.where(here & (lane == 1 + k), ids[0, s, k, j], notes)
    out[0, :, half:] = notes.astype(F32).astype(BF16)
    message = out[0]
    for r in range(1, out.shape[0]):
        out[r] = message


def order_of(notes):
    source = notes[:, :1]
    column = lax.broadcasted_iota(jnp.int32, (notes.shape[0], notes.shape[0]), 1)
    return (source.astype(jnp.int32) == column).astype(BF16)


def near_query_kernel(near, wq_far, wq, out, sem):
    load = pltpu.make_async_copy(wq_far, wq, sem)
    load.start()
    peers, rows, wide = near.shape
    half = wide - HD
    core = lax.axis_index("rep") % 2
    a = near[:, :, :half].reshape(peers * rows, half)
    load.wait()
    out[...] = dot(a, wq[0, pl.ds(pl.multiple_of(core * half, half), half)])


def query_kernel(near, far, wq, begun, out, notes):
    peers, rows, wide = near.shape
    half = wide - HD
    core = lax.axis_index("rep") % 2
    b = far[:, :, :half].reshape(peers * rows, half)
    q = begun[...] + dot(b, wq[0, pl.ds(pl.multiple_of((1 - core) * half, half), half)])
    marks = near[:, :, half:].reshape(peers * rows, HD)
    notes[...] = marks
    out[...] = dot(order_of(marks), q.astype(BF16)).astype(BF16).reshape(out.shape)


def own_kernel(near, far, wkv, weight, sel, fresh, picked, sems):
    halves, _, quarter = picked.shape
    side = 1 - lax.axis_index("rep") % 2
    copies = [
        pltpu.make_async_copy(weight.at[0, :, columns_of(z, side, quarter)], picked.at[z], sems.at[z])
        for z in range(halves)
    ]
    for copy in copies:
        copy.start()
    peers, rows, wide = near.shape
    half = wide - HD
    rank, core = lax.axis_index("req"), lax.axis_index("rep") % 2
    source = near[rank][:, half : half + 1]
    column = lax.broadcasted_iota(jnp.int32, (rows, peers * rows), 1)
    order = (source.astype(jnp.int32) == column).astype(BF16)
    a = dot(order, near[...].reshape(peers * rows, wide))
    b = dot(order, far[:, :, :half].reshape(peers * rows, half)).astype(BF16)
    sel[...] = a[:, half:]
    a = a[:, :half].astype(BF16)
    parts = (jnp.where(core == 0, a, b), jnp.where(core == 0, b, a))
    spans = half // HD
    chunks = [part[:, c * HD : (c + 1) * HD] for part in parts for c in range(spans)]
    twice = (HD, 2 * HD)
    feature = lax.broadcasted_iota(jnp.int32, twice, 1) // 2
    doubling = (lax.broadcasted_iota(jnp.int32, twice, 0) == feature).astype(BF16)
    doubled = dot(jnp.concatenate(chunks, axis=0), doubling)
    even = lax.broadcasted_iota(jnp.int32, (rows, 2 * HD), 1) % 2 == 0
    total = jnp.zeros(fresh.shape, F32)
    for c in range(2 * spans):
        v = doubled[c * rows : (c + 1) * rows]
        v = jnp.concatenate([jnp.where(even, v, 0.0), jnp.where(even, 0.0, v)], axis=0)
        w = wkv[c * HD : (c + 1) * HD].reshape(2 * HD, fresh.shape[1])
        total = total + dot(v.astype(BF16), w)
    fresh[...] = total.astype(BF16)
    for copy in copies:
        copy.wait()


def page_kernel(table_far, lens_far, pool, start, out, table, lens, staged, sems, back, small):
    first = pltpu.make_async_copy(table_far, table, small.at[0])
    second = pltpu.make_async_copy(lens_far, lens, small.at[1])
    first.start()
    second.start()
    first.wait()
    second.wait()
    count = out.shape[0]
    page = pool.shape[1]
    chunks = 1 + out.shape[1] // SPAN

    def each(act):
        for c in range(chunks):
            for j in range(count):
                if c < 2:
                    act(j, c)
                else:
                    pl.when(lens[j] > 2 * SPAN)(functools.partial(act, j, c))

    def block_of(j, c):
        return start.at[j] if c == 0 else staged.at[j, pl.ds((c - 1) * SPAN, SPAN)]

    def read(j, c):
        block = block_of(j, c)
        for p in range(SPAN // page):
            pltpu.make_async_copy(
                pool.at[table[j, c * (SPAN // page) + p]],
                block.at[pl.ds(p * page, page)],
                sems.at[j, c],
            ).start()

    def write(j, c):
        place = out.at[j, pl.ds((c - 1) * SPAN, SPAN)]
        return pltpu.make_async_copy(block_of(j, c), place, back.at[j, c])

    def forward(j, c):
        block = block_of(j, c)
        pltpu.make_async_copy(block, block, sems.at[j, c]).wait()
        if c:
            write(j, c).start()

    def finish(j, c):
        if c:
            write(j, c).wait()

    each(read)
    each(forward)
    each(finish)


def pages_call(table, lens, pool):
    mine, pages = table.shape
    length = pages * pool.shape[1]
    tail = (mine, length - SPAN) + pool.shape[2:]
    return call(
        page_kernel,
        [pltpu.VMEM((mine, SPAN) + pool.shape[2:], BF16), pltpu.HBM(tail, BF16)],
        [FAR] * 3,
        [
            pltpu.SMEM(table.shape, jnp.int32),
            pltpu.SMEM(lens.shape, jnp.int32),
            pltpu.VMEM(tail, BF16),
            pltpu.SemaphoreType.DMA((mine, length // SPAN)),
            pltpu.SemaphoreType.DMA((mine, length // SPAN)),
            pltpu.SemaphoreType.DMA((2,)),
        ],
        outs=[VM, FAR],
    )(in_hbm(table), in_hbm(lens), in_hbm(pool))


def attention_kernel(lens, sel, arrived, fresh, start, far, out, cache, qs, os, sc, ef, sems):
    count, tail, _, wide = cache.shape
    requests = range(count)
    spans = (pl.ds(0, SPAN), pl.ds(SPAN, tail - SPAN))

    def copy_of(j, part):
        span = spans[part]
        return pltpu.make_async_copy(far.at[j, span], cache.at[j, span], sems.at[j, part])

    for j in requests:
        copy_of(j, 0).start()
    for j in requests:

        @pl.when(lens[j] > 2 * SPAN)
        def _(j=j):
            copy_of(j, 1).start()

    peers, rows, _ = arrived.shape
    heads = wide // HD
    group = 2 * heads
    inv_scale = 1.0 / math.sqrt(HD)
    picks = sel[...]
    masks = [[picks[:, 1 + k : 2 + k] == float(e) for e in range(EXPERTS)] for k in range(2)]
    for h in range(heads):
        values = [arrived[e * heads + h].astype(F32) for e in range(EXPERTS)]
        for k in range(2):
            total = jnp.where(masks[k][0], values[0], 0.0)
            for e in range(1, EXPERTS):
                total = total + jnp.where(masks[k][e], values[e], 0.0)
            qs[k * heads + h] = total
    ef[...] = jnp.zeros_like(ef)
    ef[0 : 2 * rows] = fresh[...]
    extra = ef[...]
    big = (2 * group, wide)
    block_row = lax.broadcasted_iota(jnp.int32, big, 0) % heads
    diagonal = block_row == lax.broadcasted_iota(jnp.int32, big, 1) // HD
    e_col = lax.broadcasted_iota(jnp.int32, (2 * group, HD), 1)
    e_row = lax.broadcasted_iota(jnp.int32, (2 * group, HD), 0)

    def rows_of(j, part):
        if part == 0:
            return start[j].reshape(2 * SPAN, wide)
        if part == 1:
            return cache[j, :SPAN].reshape(2 * SPAN, wide)
        return cache[j, SPAN:].reshape(2 * (tail - SPAN), wide)

    def masked_scores(q, j, part):
        s = dot_rows(q, rows_of(j, part)) * inv_scale
        column = lax.broadcasted_iota(jnp.int32, s.shape, 1)
        return jnp.where(
            (column % 2 == 0) & (column < 2 * (lens[j] - part * SPAN)), s, MASKED
        )

    def highest(s):
        return jnp.max(s, axis=1, keepdims=True)

    def added(p):
        return jnp.sum(p, axis=1, keepdims=True)

    def onto_values(p, distance=1):
        return pltpu.roll(p, distance, 1).astype(BF16)

    longer = [jnp.where(lens[j] > 2 * SPAN, 1, 0) for j in requests]
    queries, extras, firsts, seconds, tops = [], [], [], [], []
    for j in requests:
        q = jnp.concatenate([qs[:, 2 * j, :], qs[:, 2 * j + 1, :]], axis=0)
        q = jnp.where(diagonal, jnp.concatenate([q] * heads, axis=1), 0.0).astype(BF16)
        live = (e_col == 2 * j) | ((e_col == 2 * j + 1) & (e_row >= group))
        queries.append(q)
        extras.append(jnp.where(live, dot_rows(q, extra) * inv_scale, MASKED))
        firsts.append(masked_scores(q, j, 0))
    for j in requests:
        copy_of(j, 0).wait()
    for j in requests:
        seconds.append(masked_scores(queries[j], j, 1))
        top = jnp.maximum(highest(extras[j]), highest(firsts[j]))
        tops.append(jnp.maximum(top, highest(seconds[j])))

    for j in requests:

        def score(_, top, j=j):
            copy_of(j, 1).wait()
            s = masked_scores(queries[j], j, 2)
            sc[j] = s
            return jnp.maximum(top, highest(s))

        tops[j] = lax.fori_loop(0, longer[j], score, tops[j])

    extras = [jnp.exp(extras[j] - tops[j]) for j in requests]
    firsts = [jnp.exp(firsts[j] - tops[j]) for j in requests]
    seconds = [jnp.exp(seconds[j] - tops[j]) for j in requests]
    sums = [added(extras[j]) + added(firsts[j]) + added(seconds[j]) for j in requests]
    mixed = [
        dot(onto_values(extras[j], rows), extra)
        + dot(onto_values(firsts[j]), rows_of(j, 0))
        + dot(onto_values(seconds[j]), rows_of(j, 1))
        for j in requests
    ]
    for j in requests:

        def gather(_, state, j=j):
            p = jnp.exp(sc[j] - tops[j])
            return state[0] + added(p), state[1] + dot(onto_values(p), rows_of(j, 2))

        sums[j], mixed[j] = lax.fori_loop(0, longer[j], gather, (sums[j], mixed[j]))

    for j in requests:
        kept = jnp.where(diagonal, mixed[j], 0.0)
        o = kept[:, :HD]
        for h in range(1, heads):
            o = o + kept[:, h * HD : (h + 1) * HD]
        o = o / sums[j]
        os[:, 2 * j, :] = o[:group]
        os[:, 2 * j + 1, :] = o[group:]
    for h in range(heads):
        one, two = os[h], os[heads + h]
        for e in range(EXPERTS):
            value = jnp.where(masks[0][e], one, 0.0) + jnp.where(masks[1][e], two, 0.0)
            out[e * heads + h] = value.astype(BF16)


def attention_call(lens, sel, arrived, fresh, start, cache):
    rows, wide = arrived.shape[1], cache.shape[-1]
    mine, tail = cache.shape[:2]
    pairs = 2 * wide // HD
    return call(
        attention_kernel,
        shape_of(arrived.shape),
        [SM, VM, VM, VM, VM, FAR],
        [
            pltpu.VMEM(cache.shape, BF16),
            pltpu.VMEM((pairs, rows, HD), F32),
            pltpu.VMEM((pairs, rows, HD), F32),
            pltpu.VMEM((mine, 2 * pairs, 2 * (tail - SPAN)), F32),
            pltpu.VMEM((HD, wide), BF16),
            pltpu.SemaphoreType.DMA((mine, 2)),
        ],
        16,
    )(lens, sel, arrived, fresh, in_vmem(start), in_hbm(cache))


def columns_of(z, core, quarter):
    return pl.ds(pl.multiple_of((2 * z + core) * quarter, quarter), quarter)


def answers_of(notes, returned):
    peers, rows, wide = returned.shape
    values = returned[...].reshape(peers * rows, wide)
    return lax.dot_general(
        order_of(notes[...]), values, (((0,), (0,)), ((), ())), preferred_element_type=F32
    ).astype(BF16)


def own_part(a, weight, out):
    peers, halves, rows, quarter = out.shape
    core = lax.axis_index("rep") % 2
    for z in range(halves):
        part = dot(a, weight[0, :, columns_of(z, core, quarter)])
        out[:, z] = part.reshape(peers, rows, quarter)


def other_part(a, weight, part, out):
    peers, halves, rows, quarter = out.shape
    for z in range(halves):
        more = dot(a, weight[z]).reshape(peers, rows, quarter)
        out[:, z] = (part[:, z] + more).astype(BF16)


def project_kernel(notes, returned, weight, out):
    own_part(answers_of(notes, returned), weight, out)


def finish_project_kernel(notes, returned, weight, part, out):
    other_part(answers_of(notes, returned), weight, part, out)


def part_kernel(units, weight, out):
    own_part(units[...], weight, out)


def place_kernel(*refs):
    pieces, out = refs[:-1], refs[-1]
    rep = lax.axis_index("rep")
    count, _, width = out.shape
    quarter = width // len(pieces)
    for m, piece in enumerate(pieces):
        place = pl.multiple_of((rep ^ m) * quarter, quarter)
        out[:, :, pl.ds(place, quarter)] = piece[...].reshape(count, 2, quarter)


def raw_products(block, side, gains, wg, wu):
    peers, halves, rows, quarter = block.shape
    total = peers * rows
    squares = jnp.zeros((total, 1), F32)
    gate = jnp.zeros((total, wg.shape[1]), F32)
    up = jnp.zeros((total, wg.shape[1]), F32)
    for z in range(halves):
        where = columns_of(z, side, quarter)
        v = block[:, z].reshape(total, quarter).astype(F32)
        squares = squares + jnp.sum(v * v, axis=1, keepdims=True)
        v = (v * gains[1:2, where]).astype(BF16)
        gate = gate + dot_rows(v, wg[0, :, where])
        up = up + dot_rows(v, wu[0, :, where])
    return squares, gate, up


def near_kernel(near, gains, wg, wu, squares, gate, up):
    core = lax.axis_index("rep") % 2
    a, b, c = raw_products(near, core, gains, wg, wu)
    squares[...] = jnp.broadcast_to(a, squares.shape)
    gate[...] = b
    up[...] = c


def expert_kernel(far, gains, wg, wu, wd, near_squares, near_gate, near_up, units, theirs):
    peers, halves, rows, quarter = far.shape
    core = lax.axis_index("rep") % 2
    squares, gate, up = raw_products(far, 1 - core, gains, wg, wu)
    squares = squares + near_squares[:, :1]
    scaling = lax.rsqrt(squares / (2 * halves * quarter) + EPSILON)
    gate = (gate + near_gate[...]) * scaling
    up = (up + near_up[...]) * scaling
    a = (gate / (1.0 + jnp.exp(-gate)) * up).astype(BF16)
    units[...] = a
    for z in range(halves):
        part = dot(a, wd[0, :, columns_of(z, 1 - core, quarter)])
        theirs[:, z] = part.astype(BF16).reshape(peers, rows, quarter)


def shards(
    tokens,
    norm_gains,
    w_kv,
    w_query,
    w_out,
    w_gate,
    w_up,
    w_down,
    kv_pages,
    page_table,
    cache_len,
    route_ids,
    route_gates,
    new_slot,
):
    req_count = lax.axis_size("req")
    rep_count = lax.axis_size("rep")
    mine, _, width = tokens.shape
    rows = 2 * mine
    total = rows * req_count
    half = width // 2
    quarter = width // rep_count
    wide = kv_pages.shape[-1]
    rep = lax.axis_index("rep")
    swap = [(p, p ^ 1) for p in range(rep_count)]
    wide_groups = [
        [r * rep_count + 2 * z + c for r in range(req_count) for z in range(rep_count // 2)]
        for c in range(2)
    ]
    peers = req_count * rep_count // 2
    split = (req_count, rep_count // 2, rows, quarter)

    def spread_req(value):
        return lax.all_to_all(value, "req", split_axis=0, concat_axis=0, tiled=True)

    def spread_wide(value):
        return lax.all_to_all(
            value,
            ("req", "rep"),
            split_axis=0,
            concat_axis=0,
            tiled=True,
            axis_index_groups=wide_groups,
        )

    def other_core(value):
        return lax.ppermute(value, "rep", swap)

    inputs = tokens.reshape(rows, width)
    ids = route_ids.transpose(0, 2, 1, 3).reshape(rows, 2, 2)
    gates = route_gates.astype(F32).transpose(0, 2, 1, 3).reshape(rows, 2, 2)
    experts_row = jnp.arange(EXPERTS, dtype=jnp.int32)
    shares = jnp.sum(jnp.where(ids[..., None] == experts_row, gates[..., None], 0.0), axis=2)
    shares = shares.transpose(1, 2, 0)[..., None]
    shares = [shares[0], shares[1]]
    kept = lax.dynamic_slice_in_dim(inputs, rep * quarter, quarter, 1).astype(F32)

    routes = route_ids.transpose(1, 2, 3, 0)
    message = call(
        message_kernel,
        shape_of((req_count, rows, half + HD)),
        [FAR] * 4,
        [
            pltpu.SMEM(new_slot.shape, jnp.int32),
            pltpu.SMEM(routes.shape, jnp.int32),
            pltpu.VMEM(tokens.shape, BF16),
            pltpu.VMEM(norm_gains.shape, F32),
            pltpu.SemaphoreType.DMA((4,)),
        ],
    )(in_hbm(new_slot), in_hbm(routes), in_hbm(tokens), in_hbm(norm_gains))
    near = spread_req(message)
    start, cache = pages_call(page_table, cache_len, kv_pages)
    near, start, cache, shares, kept = lax.optimization_barrier(
        (near, start, cache, shares, kept)
    )
    far = other_core(near)
    wq, begun = call(
        near_query_kernel,
        [pltpu.VMEM(w_query.shape, BF16), shape_of((total, HD), F32)],
        [VM, FAR],
        [pltpu.SemaphoreType.DMA],
    )(near, in_hbm(w_query))
    ordered, notes = call(
        query_kernel, [shape_of((req_count, rows, HD)), shape_of((total, HD))], [VM] * 4
    )(near, far, in_vmem(wq), begun)
    arrived = spread_req(ordered)
    sel, fresh, picked = call(
        own_kernel,
        [
            shape_of((rows, HD), F32),
            shape_of((2 * rows, wide)),
            shape_of((rep_count // 2, w_out.shape[1], quarter)),
        ],
        [VM, VM, VM, FAR],
        [pltpu.SemaphoreType.DMA((rep_count // 2,))],
    )(near, far, w_kv, in_hbm(w_out))
    arrived, picked = lax.optimization_barrier((arrived, picked))
    out_x = other_core(picked)
    back = attention_call(cache_len, sel, arrived, fresh, start, cache)
    returned = spread_req(back)
    returned_x = other_core(returned)
    part = call(project_kernel, shape_of(split, F32), [VM] * 3)(notes, returned, w_out)
    summed = call(finish_project_kernel, shape_of(split), [VM] * 4)(
        notes, returned_x, out_x, part
    )

    def reduce_wide(summed, share):
        got = spread_wide(summed.reshape(peers, rows, quarter))
        got = got.reshape(EXPERTS, peers // EXPERTS, rows, quarter).astype(F32)
        return jnp.sum(jnp.sum(got, axis=1) * share, axis=0)

    hidden = kept + reduce_wide(summed, shares[0])
    copies = jnp.broadcast_to(hidden.astype(BF16)[None], (peers, rows, quarter))
    block = spread_wide(copies)
    far = other_core(block).reshape(split)
    wg, wu = w_gate.transpose(0, 2, 1), w_up.transpose(0, 2, 1)
    units_dev = w_down.shape[1]
    squares, gate, up = call(
        near_kernel,
        [shape_of((total, HD), F32)] + [shape_of((total, units_dev), F32)] * 2,
        [VM] * 4,
    )(block.reshape(split), norm_gains, wg, wu)
    units, theirs = call(
        expert_kernel, [shape_of((total, units_dev)), shape_of(split)], [VM] * 8
    )(far, norm_gains, wg, wu, w_down, squares, gate, up)
    theirs = other_core(theirs)
    part = call(part_kernel, shape_of(split, F32), [VM] * 2)(units, w_down)
    feed = reduce_wide((part + theirs.astype(F32)).astype(BF16), shares[1])
    piece = (hidden + feed).astype(BF16)
    pieces = [piece] + [
        lax.ppermute(piece, "rep", [(p, p ^ m) for p in range(rep_count)])
        for m in range(1, rep_count)
    ]
    return call(place_kernel, shape_of((mine, 2, width)), [VM] * rep_count)(*pieces)


def solution(mesh):
    in_specs = (
        P("req", None, None),
        P(),
        P(None, None, "rep"),
        P("req", None, "rep"),
        P("req", "rep", None),
        P("req", None, "rep"),
        P("req", None, "rep"),
        P("req", "rep", None),
        P("req", None, None, "rep"),
        P("req", None),
        P("req"),
        P("req", None, None, None),
        P("req", None, None, None),
        P("req"),
    )
    out_specs = P("req", None, None)
    return jax.shard_map(shards, mesh=mesh, in_specs=in_specs, out_specs=out_specs, check_vma=False)
```

```python
import functools
import math

import jax
import jax.numpy as jnp
from jax import lax
from jax.experimental import pallas as pl
from jax.experimental.pallas import tpu as pltpu
from jax.sharding import PartitionSpec as P

HD = 128
EXPERTS = 8
SPAN = 256
EPSILON = 1e-06
MASKED = -1e30
F32 = jnp.float32
BF16 = jnp.bfloat16
VM = pl.BlockSpec(memory_space=pltpu.VMEM)
SM = pl.BlockSpec(memory_space=pltpu.SMEM)
FAR = pl.BlockSpec(memory_space=pltpu.HBM)
ROWS_BY_ROWS = (((1,), (1,)), ((), ()))


def dot(a, b):
    return jnp.dot(a, b, preferred_element_type=F32)


def dot_rows(a, b):
    return lax.dot_general(a, b, ROWS_BY_ROWS, preferred_element_type=F32)


def call(body, out, ins, scratch=(), limit=12, outs=None):
    many = isinstance(out, (list, tuple))
    return pl.pallas_call(
        body,
        out_shape=out,
        in_specs=ins,
        out_specs=outs or ([VM] * len(out) if many else VM),
        scratch_shapes=scratch,
        compiler_params=pltpu.CompilerParams(vmem_limit_bytes=limit << 20),
    )


def in_hbm(value):
    return pltpu.with_memory_space_constraint(value, pltpu.HBM)


def in_vmem(value):
    return pltpu.with_memory_space_constraint(value, pltpu.VMEM)


def shape_of(shape, dtype=BF16):
    return jax.ShapeDtypeStruct(shape, dtype)


def message_kernel(slots_far, ids_far, tokens_far, gains_far, out, slots, ids, tokens, gains, sems):
    pairs = ((slots_far, slots), (ids_far, ids), (tokens_far, tokens), (gains_far, gains))
    copies = [pltpu.make_async_copy(a, b, sems.at[i]) for i, (a, b) in enumerate(pairs)]
    for copy in copies:
        copy.start()
    for copy in copies:
        copy.wait()
    count, _, width = tokens.shape
    rows = 2 * count
    half = width // 2
    rank, core = lax.axis_index("req"), lax.axis_index("rep") % 2
    x = tokens[...].reshape(rows, width).astype(F32)
    scaling = lax.rsqrt(jnp.mean(x * x, axis=1, keepdims=True) + EPSILON)
    normed = (x * scaling * gains[0:1]).astype(BF16)
    out[0, :, :half] = jnp.where(core == 0, normed[:, :half], normed[:, half:])
    row = lax.broadcasted_iota(jnp.int32, (rows, HD), 0)
    lane = lax.broadcasted_iota(jnp.int32, (rows, HD), 1)
    notes = jnp.zeros((rows, HD), jnp.int32)
    for j in range(count):
        for s in range(2):
            here = row == 2 * j + s
            source = 2 * (rank * count + j) if s == 0 else 2 * slots[j] + 1
            notes = jnp.where(here & (lane == 0), source, notes)
            for k in range(2):
                notes = jnp.where(here & (lane == 1 + k), ids[0, s, k, j], notes)
    out[0, :, half:] = notes.astype(F32).astype(BF16)
    message = out[0]
    for r in range(1, out.shape[0]):
        out[r] = message


def order_of(notes):
    source = notes[:, :1]
    column = lax.broadcasted_iota(jnp.int32, (notes.shape[0], notes.shape[0]), 1)
    return (source.astype(jnp.int32) == column).astype(BF16)


def near_query_kernel(near, wq_far, wq, out, sem):
    load = pltpu.make_async_copy(wq_far, wq, sem)
    load.start()
    peers, rows, wide = near.shape
    half = wide - HD
    core = lax.axis_index("rep") % 2
    a = near[:, :, :half].reshape(peers * rows, half)
    load.wait()
    out[...] = dot(a, wq[0, pl.ds(pl.multiple_of(core * half, half), half)])


def query_kernel(near, far, wq, begun, out, notes):
    peers, rows, wide = near.shape
    half = wide - HD
    core = lax.axis_index("rep") % 2
    b = far[:, :, :half].reshape(peers * rows, half)
    q = begun[...] + dot(b, wq[0, pl.ds(pl.multiple_of((1 - core) * half, half), half)])
    marks = near[:, :, half:].reshape(peers * rows, HD)
    notes[...] = marks
    out[...] = dot(order_of(marks), q.astype(BF16)).astype(BF16).reshape(out.shape)


def own_kernel(near, far, wkv, weight, sel, fresh, picked, sems):
    halves, _, quarter = picked.shape
    side = 1 - lax.axis_index("rep") % 2
    copies = [
        pltpu.make_async_copy(weight.at[0, :, columns_of(z, side, quarter)], picked.at[z], sems.at[z])
        for z in range(halves)
    ]
    for copy in copies:
        copy.start()
    peers, rows, wide = near.shape
    half = wide - HD
    rank, core = lax.axis_index("req"), lax.axis_index("rep") % 2
    source = near[rank][:, half : half + 1]
    column = lax.broadcasted_iota(jnp.int32, (rows, peers * rows), 1)
    order = (source.astype(jnp.int32) == column).astype(BF16)
    a = dot(order, near[...].reshape(peers * rows, wide))
    b = dot(order, far[:, :, :half].reshape(peers * rows, half)).astype(BF16)
    sel[...] = a[:, half:]
    a = a[:, :half].astype(BF16)
    parts = (jnp.where(core == 0, a, b), jnp.where(core == 0, b, a))
    spans = half // HD
    chunks = [part[:, c * HD : (c + 1) * HD] for part in parts for c in range(spans)]
    twice = (HD, 2 * HD)
    feature = lax.broadcasted_iota(jnp.int32, twice, 1) // 2
    doubling = (lax.broadcasted_iota(jnp.int32, twice, 0) == feature).astype(BF16)
    doubled = dot(jnp.concatenate(chunks, axis=0), doubling)
    even = lax.broadcasted_iota(jnp.int32, (rows, 2 * HD), 1) % 2 == 0
    total = jnp.zeros(fresh.shape, F32)
    for c in range(2 * spans):
        v = doubled[c * rows : (c + 1) * rows]
        v = jnp.concatenate([jnp.where(even, v, 0.0), jnp.where(even, 0.0, v)], axis=0)
        w = wkv[c * HD : (c + 1) * HD].reshape(2 * HD, fresh.shape[1])
        total = total + dot(v.astype(BF16), w)
    fresh[...] = total.astype(BF16)
    for copy in copies:
        copy.wait()


def page_kernel(table_far, lens_far, pool, start, out, table, lens, staged, sems, back, small):
    first = pltpu.make_async_copy(table_far, table, small.at[0])
    second = pltpu.make_async_copy(lens_far, lens, small.at[1])
    first.start()
    second.start()
    first.wait()
    second.wait()
    count = out.shape[0]
    page = pool.shape[1]
    chunks = 1 + out.shape[1] // SPAN

    def each(act):
        for c in range(chunks):
            for j in range(count):
                if c < 2:
                    act(j, c)
                else:
                    pl.when(lens[j] > 2 * SPAN)(functools.partial(act, j, c))

    def block_of(j, c):
        return start.at[j] if c == 0 else staged.at[j, pl.ds((c - 1) * SPAN, SPAN)]

    def read(j, c):
        block = block_of(j, c)
        for p in range(SPAN // page):
            pltpu.make_async_copy(
                pool.at[table[j, c * (SPAN // page) + p]],
                block.at[pl.ds(p * page, page)],
                sems.at[j, c],
            ).start()

    def write(j, c):
        place = out.at[j, pl.ds((c - 1) * SPAN, SPAN)]
        return pltpu.make_async_copy(block_of(j, c), place, back.at[j, c])

    def forward(j, c):
        block = block_of(j, c)
        pltpu.make_async_copy(block, block, sems.at[j, c]).wait()
        if c:
            write(j, c).start()

    def finish(j, c):
        if c:
            write(j, c).wait()

    each(read)
    each(forward)
    each(finish)


def pages_call(table, lens, pool):
    mine, pages = table.shape
    length = pages * pool.shape[1]
    tail = (mine, length - SPAN) + pool.shape[2:]
    return call(
        page_kernel,
        [pltpu.VMEM((mine, SPAN) + pool.shape[2:], BF16), pltpu.HBM(tail, BF16)],
        [FAR] * 3,
        [
            pltpu.SMEM(table.shape, jnp.int32),
            pltpu.SMEM(lens.shape, jnp.int32),
            pltpu.VMEM(tail, BF16),
            pltpu.SemaphoreType.DMA((mine, length // SPAN)),
            pltpu.SemaphoreType.DMA((mine, length // SPAN)),
            pltpu.SemaphoreType.DMA((2,)),
        ],
        outs=[VM, FAR],
    )(in_hbm(table), in_hbm(lens), in_hbm(pool))


def attention_kernel(lens, sel, arrived, fresh, start, far, out, cache, qs, os, sc, ef, sems):
    count, tail, _, wide = cache.shape
    requests = range(count)
    spans = (pl.ds(0, SPAN), pl.ds(SPAN, tail - SPAN))

    def copy_of(j, part):
        span = spans[part]
        return pltpu.make_async_copy(far.at[j, span], cache.at[j, span], sems.at[j, part])

    for j in requests:
        copy_of(j, 0).start()
    for j in requests:

        @pl.when(lens[j] > 2 * SPAN)
        def _(j=j):
            copy_of(j, 1).start()

    peers, rows, _ = arrived.shape
    heads = wide // HD
    group = 2 * heads
    inv_scale = 1.0 / math.sqrt(HD)
    picks = sel[...]
    masks = [[picks[:, 1 + k : 2 + k] == float(e) for e in range(EXPERTS)] for k in range(2)]
    for h in range(heads):
        values = [arrived[e * heads + h].astype(F32) for e in range(EXPERTS)]
        for k in range(2):
            total = jnp.where(masks[k][0], values[0], 0.0)
            for e in range(1, EXPERTS):
                total = total + jnp.where(masks[k][e], values[e], 0.0)
            qs[k * heads + h] = total
    ef[...] = jnp.zeros_like(ef)
    ef[0 : 2 * rows] = fresh[...]
    extra = ef[...]
    big = (2 * group, wide)
    block_row = lax.broadcasted_iota(jnp.int32, big, 0) % heads
    diagonal = block_row == lax.broadcasted_iota(jnp.int32, big, 1) // HD
    e_col = lax.broadcasted_iota(jnp.int32, (2 * group, HD), 1)
    e_row = lax.broadcasted_iota(jnp.int32, (2 * group, HD), 0)

    def rows_of(j, part):
        if part == 0:
            return start[j].reshape(2 * SPAN, wide)
        if part == 1:
            return cache[j, :SPAN].reshape(2 * SPAN, wide)
        return cache[j, SPAN:].reshape(2 * (tail - SPAN), wide)

    def masked_scores(q, j, part):
        s = dot_rows(q, rows_of(j, part)) * inv_scale
        column = lax.broadcasted_iota(jnp.int32, s.shape, 1)
        return jnp.where(
            (column % 2 == 0) & (column < 2 * (lens[j] - part * SPAN)), s, MASKED
        )

    def highest(s):
        return jnp.max(s, axis=1, keepdims=True)

    def added(p):
        return jnp.sum(p, axis=1, keepdims=True)

    def onto_values(p, distance=1):
        return pltpu.roll(p, distance, 1).astype(BF16)

    longer = [jnp.where(lens[j] > 2 * SPAN, 1, 0) for j in requests]
    queries, extras, firsts, seconds, tops = [], [], [], [], []
    for j in requests:
        q = jnp.concatenate([qs[:, 2 * j, :], qs[:, 2 * j + 1, :]], axis=0)
        q = jnp.where(diagonal, jnp.concatenate([q] * heads, axis=1), 0.0).astype(BF16)
        live = (e_col == 2 * j) | ((e_col == 2 * j + 1) & (e_row >= group))
        queries.append(q)
        extras.append(jnp.where(live, dot_rows(q, extra) * inv_scale, MASKED))
        firsts.append(masked_scores(q, j, 0))
    for j in requests:
        copy_of(j, 0).wait()
    for j in requests:
        seconds.append(masked_scores(queries[j], j, 1))
        top = jnp.maximum(highest(extras[j]), highest(firsts[j]))
        tops.append(jnp.maximum(top, highest(seconds[j])))

    for j in requests:

        def score(_, top, j=j):
            copy_of(j, 1).wait()
            s = masked_scores(queries[j], j, 2)
            sc[j] = s
            return jnp.maximum(top, highest(s))

        tops[j] = lax.fori_loop(0, longer[j], score, tops[j])

    extras = [jnp.exp(extras[j] - tops[j]) for j in requests]
    firsts = [jnp.exp(firsts[j] - tops[j]) for j in requests]
    seconds = [jnp.exp(seconds[j] - tops[j]) for j in requests]
    sums = [added(extras[j]) + added(firsts[j]) + added(seconds[j]) for j in requests]
    mixed = [
        dot(onto_values(extras[j], rows), extra)
        + dot(onto_values(firsts[j]), rows_of(j, 0))
        + dot(onto_values(seconds[j]), rows_of(j, 1))
        for j in requests
    ]
    for j in requests:

        def gather(_, state, j=j):
            p = jnp.exp(sc[j] - tops[j])
            return state[0] + added(p), state[1] + dot(onto_values(p), rows_of(j, 2))

        sums[j], mixed[j] = lax.fori_loop(0, longer[j], gather, (sums[j], mixed[j]))

    for j in requests:
        kept = jnp.where(diagonal, mixed[j], 0.0)
        o = kept[:, :HD]
        for h in range(1, heads):
            o = o + kept[:, h * HD : (h + 1) * HD]
        o = o / sums[j]
        os[:, 2 * j, :] = o[:group]
        os[:, 2 * j + 1, :] = o[group:]
    for h in range(heads):
        one, two = os[h], os[heads + h]
        for e in range(EXPERTS):
            value = jnp.where(masks[0][e], one, 0.0) + jnp.where(masks[1][e], two, 0.0)
            out[e * heads + h] = value.astype(BF16)


def attention_call(lens, sel, arrived, fresh, start, cache):
    rows, wide = arrived.shape[1], cache.shape[-1]
    mine, tail = cache.shape[:2]
    pairs = 2 * wide // HD
    return call(
        attention_kernel,
        shape_of(arrived.shape),
        [SM, VM, VM, VM, VM, FAR],
        [
            pltpu.VMEM(cache.shape, BF16),
            pltpu.VMEM((pairs, rows, HD), F32),
            pltpu.VMEM((pairs, rows, HD), F32),
            pltpu.VMEM((mine, 2 * pairs, 2 * (tail - SPAN)), F32),
            pltpu.VMEM((HD, wide), BF16),
            pltpu.SemaphoreType.DMA((mine, 2)),
        ],
        16,
    )(lens, sel, arrived, fresh, in_vmem(start), in_hbm(cache))


def columns_of(z, core, quarter):
    return pl.ds(pl.multiple_of((2 * z + core) * quarter, quarter), quarter)


def answers_of(notes, returned):
    peers, rows, wide = returned.shape
    values = returned[...].reshape(peers * rows, wide)
    return lax.dot_general(
        order_of(notes[...]), values, (((0,), (0,)), ((), ())), preferred_element_type=F32
    ).astype(BF16)


def own_part(a, weight, out):
    peers, halves, rows, quarter = out.shape
    core = lax.axis_index("rep") % 2
    for z in range(halves):
        part = dot(a, weight[0, :, columns_of(z, core, quarter)])
        out[:, z] = part.reshape(peers, rows, quarter)


def other_part(a, weight, part, out):
    peers, halves, rows, quarter = out.shape
    for z in range(halves):
        more = dot(a, weight[z]).reshape(peers, rows, quarter)
        out[:, z] = (part[:, z] + more).astype(BF16)


def project_kernel(notes, returned, weight, out):
    own_part(answers_of(notes, returned), weight, out)


def finish_project_kernel(notes, returned, weight, part, out):
    other_part(answers_of(notes, returned), weight, part, out)


def part_kernel(units, weight, out):
    own_part(units[...], weight, out)


def place_kernel(*refs):
    pieces, out = refs[:-1], refs[-1]
    rep = lax.axis_index("rep")
    count, _, width = out.shape
    quarter = width // len(pieces)
    for m, piece in enumerate(pieces):
        place = pl.multiple_of((rep ^ m) * quarter, quarter)
        out[:, :, pl.ds(place, quarter)] = piece[...].reshape(count, 2, quarter)


def raw_products(block, side, gains, wg, wu):
    peers, halves, rows, quarter = block.shape
    total = peers * rows
    squares = jnp.zeros((total, 1), F32)
    gate = jnp.zeros((total, wg.shape[1]), F32)
    up = jnp.zeros((total, wg.shape[1]), F32)
    for z in range(halves):
        where = columns_of(z, side, quarter)
        v = block[:, z].reshape(total, quarter).astype(F32)
        squares = squares + jnp.sum(v * v, axis=1, keepdims=True)
        v = (v * gains[1:2, where]).astype(BF16)
        gate = gate + dot_rows(v, wg[0, :, where])
        up = up + dot_rows(v, wu[0, :, where])
    return squares, gate, up


def near_kernel(near, gains, wg, wu, squares, gate, up):
    core = lax.axis_index("rep") % 2
    a, b, c = raw_products(near, core, gains, wg, wu)
    squares[...] = jnp.broadcast_to(a, squares.shape)
    gate[...] = b
    up[...] = c


def expert_kernel(far, gains, wg, wu, wd, near_squares, near_gate, near_up, units, theirs):
    peers, halves, rows, quarter = far.shape
    core = lax.axis_index("rep") % 2
    squares, gate, up = raw_products(far, 1 - core, gains, wg, wu)
    squares = squares + near_squares[:, :1]
    scaling = lax.rsqrt(squares / (2 * halves * quarter) + EPSILON)
    gate = (gate + near_gate[...]) * scaling
    up = (up + near_up[...]) * scaling
    a = (gate / (1.0 + jnp.exp(-gate)) * up).astype(BF16)
    units[...] = a
    for z in range(halves):
        part = dot(a, wd[0, :, columns_of(z, 1 - core, quarter)])
        theirs[:, z] = part.astype(BF16).reshape(peers, rows, quarter)


def shards(
    tokens,
    norm_gains,
    w_kv,
    w_query,
    w_out,
    w_gate,
    w_up,
    w_down,
    kv_pages,
    page_table,
    cache_len,
    route_ids,
    route_gates,
    new_slot,
):
    req_count = lax.axis_size("req")
    rep_count = lax.axis_size("rep")
    mine, _, width = tokens.shape
    rows = 2 * mine
    total = rows * req_count
    half = width // 2
    quarter = width // rep_count
    wide = kv_pages.shape[-1]
    rep = lax.axis_index("rep")
    swap = [(p, p ^ 1) for p in range(rep_count)]
    wide_groups = [
        [r * rep_count + 2 * z + c for r in range(req_count) for z in range(rep_count // 2)]
        for c in range(2)
    ]
    peers = req_count * rep_count // 2
    split = (req_count, rep_count // 2, rows, quarter)

    def spread_req(value):
        return lax.all_to_all(value, "req", split_axis=0, concat_axis=0, tiled=True)

    def spread_wide(value):
        return lax.all_to_all(
            value,
            ("req", "rep"),
            split_axis=0,
            concat_axis=0,
            tiled=True,
            axis_index_groups=wide_groups,
        )

    def other_core(value):
        return lax.ppermute(value, "rep", swap)

    inputs = tokens.reshape(rows, width)
    ids = route_ids.transpose(0, 2, 1, 3).reshape(rows, 2, 2)
    gates = route_gates.astype(F32).transpose(0, 2, 1, 3).reshape(rows, 2, 2)
    experts_row = jnp.arange(EXPERTS, dtype=jnp.int32)
    shares = jnp.sum(jnp.where(ids[..., None] == experts_row, gates[..., None], 0.0), axis=2)
    shares = shares.transpose(1, 2, 0)[..., None]
    shares = [shares[0], shares[1]]
    kept = lax.dynamic_slice_in_dim(inputs, rep * quarter, quarter, 1).astype(F32)

    routes = route_ids.transpose(1, 2, 3, 0)
    message = call(
        message_kernel,
        shape_of((req_count, rows, half + HD)),
        [FAR] * 4,
        [
            pltpu.SMEM(new_slot.shape, jnp.int32),
            pltpu.SMEM(routes.shape, jnp.int32),
            pltpu.VMEM(tokens.shape, BF16),
            pltpu.VMEM(norm_gains.shape, F32),
            pltpu.SemaphoreType.DMA((4,)),
        ],
    )(in_hbm(new_slot), in_hbm(routes), in_hbm(tokens), in_hbm(norm_gains))
    near = spread_req(message)
    start, cache = pages_call(page_table, cache_len, kv_pages)
    near, start, cache, shares, kept = lax.optimization_barrier(
        (near, start, cache, shares, kept)
    )
    far = other_core(near)
    wq, begun = call(
        near_query_kernel,
        [pltpu.VMEM(w_query.shape, BF16), shape_of((total, HD), F32)],
        [VM, FAR],
        [pltpu.SemaphoreType.DMA],
    )(near, in_hbm(w_query))
    ordered, notes = call(
        query_kernel, [shape_of((req_count, rows, HD)), shape_of((total, HD))], [VM] * 4
    )(near, far, in_vmem(wq), begun)
    arrived = spread_req(ordered)
    sel, fresh, picked = call(
        own_kernel,
        [
            shape_of((rows, HD), F32),
            shape_of((2 * rows, wide)),
            shape_of((rep_count // 2, w_out.shape[1], quarter)),
        ],
        [VM, VM, VM, FAR],
        [pltpu.SemaphoreType.DMA((rep_count // 2,))],
    )(near, far, w_kv, in_hbm(w_out))
    back = attention_call(cache_len, sel, arrived, fresh, start, cache)
    returned = spread_req(back)
    returned, picked = lax.optimization_barrier((returned, picked))
    returned_x, out_x = other_core(returned), other_core(picked)
    part = call(project_kernel, shape_of(split, F32), [VM] * 3)(notes, returned, w_out)
    summed = call(finish_project_kernel, shape_of(split), [VM] * 4)(
        notes, returned_x, out_x, part
    )

    def reduce_wide(summed, share):
        got = spread_wide(summed.reshape(peers, rows, quarter))
        got = got.reshape(EXPERTS, peers // EXPERTS, rows, quarter).astype(F32)
        return jnp.sum(jnp.sum(got, axis=1) * share, axis=0)

    hidden = kept + reduce_wide(summed, shares[0])
    copies = jnp.broadcast_to(hidden.astype(BF16)[None], (peers, rows, quarter))
    block = spread_wide(copies)
    far = other_core(block).reshape(split)
    wg, wu = w_gate.transpose(0, 2, 1), w_up.transpose(0, 2, 1)
    units_dev = w_down.shape[1]
    squares, gate, up = call(
        near_kernel,
        [shape_of((total, HD), F32)] + [shape_of((total, units_dev), F32)] * 2,
        [VM] * 4,
    )(block.reshape(split), norm_gains, wg, wu)
    units, theirs = call(
        expert_kernel, [shape_of((total, units_dev)), shape_of(split)], [VM] * 8
    )(far, norm_gains, wg, wu, w_down, squares, gate, up)
    theirs = other_core(theirs)
    part = call(part_kernel, shape_of(split, F32), [VM] * 2)(units, w_down)
    feed = reduce_wide((part + theirs.astype(F32)).astype(BF16), shares[1])
    piece = (hidden + feed).astype(BF16)
    pieces = [piece] + [
        lax.ppermute(piece, "rep", [(p, p ^ m) for p in range(rep_count)])
        for m in range(1, rep_count)
    ]
    return call(place_kernel, shape_of((mine, 2, width)), [VM] * rep_count)(*pieces)


def solution(mesh):
    in_specs = (
        P("req", None, None),
        P(),
        P(None, None, "rep"),
        P("req", None, "rep"),
        P("req", "rep", None),
        P("req", None, "rep"),
        P("req", None, "rep"),
        P("req", "rep", None),
        P("req", None, None, "rep"),
        P("req", None),
        P("req"),
        P("req", None, None, None),
        P("req", None, None, None),
        P("req"),
    )
    out_specs = P("req", None, None)
    return jax.shard_map(shards, mesh=mesh, in_specs=in_specs, out_specs=out_specs, check_vma=False)
```

```python
import functools
import math

import jax
import jax.numpy as jnp
from jax import lax
from jax.experimental import pallas as pl
from jax.experimental.pallas import tpu as pltpu
from jax.sharding import PartitionSpec as P

HD = 128
EXPERTS = 8
HEAD = 192
MIDDLE = 192
EPSILON = 1e-06
MASKED = -1e30
F32 = jnp.float32
BF16 = jnp.bfloat16
VM = pl.BlockSpec(memory_space=pltpu.VMEM)
SM = pl.BlockSpec(memory_space=pltpu.SMEM)
FAR = pl.BlockSpec(memory_space=pltpu.HBM)
ROWS_BY_ROWS = (((1,), (1,)), ((), ()))


def dot(a, b):
    return jnp.dot(a, b, preferred_element_type=F32)


def dot_rows(a, b):
    return lax.dot_general(a, b, ROWS_BY_ROWS, preferred_element_type=F32)


def call(body, out, ins, scratch=(), limit=12, outs=None):
    many = isinstance(out, (list, tuple))
    return pl.pallas_call(
        body,
        out_shape=out,
        in_specs=ins,
        out_specs=outs or ([VM] * len(out) if many else VM),
        scratch_shapes=scratch,
        compiler_params=pltpu.CompilerParams(vmem_limit_bytes=limit << 20),
    )


def in_hbm(value):
    return pltpu.with_memory_space_constraint(value, pltpu.HBM)


def in_vmem(value):
    return pltpu.with_memory_space_constraint(value, pltpu.VMEM)


def shape_of(shape, dtype=BF16):
    return jax.ShapeDtypeStruct(shape, dtype)


def message_kernel(slots_far, ids_far, tokens_far, gains_far, out, slots, ids, tokens, gains, sems):
    pairs = ((slots_far, slots), (ids_far, ids), (tokens_far, tokens), (gains_far, gains))
    copies = [pltpu.make_async_copy(a, b, sems.at[i]) for i, (a, b) in enumerate(pairs)]
    for copy in copies:
        copy.start()
    for copy in copies:
        copy.wait()
    count, _, width = tokens.shape
    rows = 2 * count
    half = width // 2
    rank, core = lax.axis_index("req"), lax.axis_index("rep") % 2
    x = tokens[...].reshape(rows, width).astype(F32)
    scaling = lax.rsqrt(jnp.mean(x * x, axis=1, keepdims=True) + EPSILON)
    normed = (x * scaling * gains[0:1]).astype(BF16)
    out[0, :, :half] = jnp.where(core == 0, normed[:, :half], normed[:, half:])
    row = lax.broadcasted_iota(jnp.int32, (rows, HD), 0)
    lane = lax.broadcasted_iota(jnp.int32, (rows, HD), 1)
    notes = jnp.zeros((rows, HD), jnp.int32)
    for j in range(count):
        for s in range(2):
            here = row == 2 * j + s
            source = 2 * (rank * count + j) if s == 0 else 2 * slots[j] + 1
            notes = jnp.where(here & (lane == 0), source, notes)
            for k in range(2):
                notes = jnp.where(here & (lane == 1 + k), ids[0, s, k, j], notes)
    out[0, :, half:] = notes.astype(F32).astype(BF16)
    message = out[0]
    for r in range(1, out.shape[0]):
        out[r] = message


def order_of(notes):
    source = notes[:, :1]
    column = lax.broadcasted_iota(jnp.int32, (notes.shape[0], notes.shape[0]), 1)
    return (source.astype(jnp.int32) == column).astype(BF16)


def near_query_kernel(near, wq_far, wq, out, sem):
    load = pltpu.make_async_copy(wq_far, wq, sem)
    load.start()
    peers, rows, wide = near.shape
    half = wide - HD
    core = lax.axis_index("rep") % 2
    a = near[:, :, :half].reshape(peers * rows, half)
    load.wait()
    out[...] = dot(a, wq[0, pl.ds(pl.multiple_of(core * half, half), half)])


def query_kernel(near, far, wq, begun, out, notes):
    peers, rows, wide = near.shape
    half = wide - HD
    core = lax.axis_index("rep") % 2
    b = far[:, :, :half].reshape(peers * rows, half)
    q = begun[...] + dot(b, wq[0, pl.ds(pl.multiple_of((1 - core) * half, half), half)])
    marks = near[:, :, half:].reshape(peers * rows, HD)
    notes[...] = marks
    out[...] = dot(order_of(marks), q.astype(BF16)).astype(BF16).reshape(out.shape)


def middle_kernel(cache, out, sem):
    fetch = pltpu.make_async_copy(cache.at[:, pl.ds(0, MIDDLE)], out, sem)
    fetch.start()
    fetch.wait()


def own_kernel(near, far, wkv, weight, sel, fresh, picked_far, picked, sems, one):
    halves, _, quarter = picked.shape
    side = 1 - lax.axis_index("rep") % 2
    copies = [
        pltpu.make_async_copy(weight.at[0, :, columns_of(z, side, quarter)], picked.at[z], sems.at[z])
        for z in range(halves)
    ]
    for copy in copies:
        copy.start()
    peers, rows, wide = near.shape
    half = wide - HD
    rank, core = lax.axis_index("req"), lax.axis_index("rep") % 2
    source = near[rank][:, half : half + 1]
    column = lax.broadcasted_iota(jnp.int32, (rows, peers * rows), 1)
    order = (source.astype(jnp.int32) == column).astype(BF16)
    a = dot(order, near[...].reshape(peers * rows, wide))
    b = dot(order, far[:, :, :half].reshape(peers * rows, half)).astype(BF16)
    sel[...] = a[:, half:]
    a = a[:, :half].astype(BF16)
    parts = (jnp.where(core == 0, a, b), jnp.where(core == 0, b, a))
    spans = half // HD
    chunks = [part[:, c * HD : (c + 1) * HD] for part in parts for c in range(spans)]
    twice = (HD, 2 * HD)
    feature = lax.broadcasted_iota(jnp.int32, twice, 1) // 2
    doubling = (lax.broadcasted_iota(jnp.int32, twice, 0) == feature).astype(BF16)
    doubled = dot(jnp.concatenate(chunks, axis=0), doubling)
    even = lax.broadcasted_iota(jnp.int32, (rows, 2 * HD), 1) % 2 == 0
    total = jnp.zeros(fresh.shape, F32)
    for c in range(2 * spans):
        v = doubled[c * rows : (c + 1) * rows]
        v = jnp.concatenate([jnp.where(even, v, 0.0), jnp.where(even, 0.0, v)], axis=0)
        w = wkv[c * HD : (c + 1) * HD].reshape(2 * HD, fresh.shape[1])
        total = total + dot(v.astype(BF16), w)
    for copy in copies:
        copy.wait()
    send = pltpu.make_async_copy(picked, picked_far, one)
    send.start()
    fresh[...] = total.astype(BF16)
    send.wait()


def page_kernel(table_far, lens_far, pool, start, out, table, lens, staged, sems, back, small):
    first = pltpu.make_async_copy(table_far, table, small.at[0])
    second = pltpu.make_async_copy(lens_far, lens, small.at[1])
    first.start()
    second.start()
    first.wait()
    second.wait()
    count = out.shape[0]
    page = pool.shape[1]
    tail = out.shape[1]
    sizes = (HEAD, MIDDLE, tail - MIDDLE)
    starts = (0, HEAD, HEAD + MIDDLE)
    places = (None, pl.ds(0, MIDDLE), pl.ds(MIDDLE, tail - MIDDLE))

    def each(act):
        for part in range(3):
            for j in range(count):
                if part < 2:
                    act(j, part)
                else:
                    pl.when(lens[j] > starts[2])(functools.partial(act, j, part))

    def block_of(j, part):
        return start.at[j] if part == 0 else staged.at[j, places[part]]

    def read(j, part):
        block = block_of(j, part)
        for p in range(sizes[part] // page):
            pltpu.make_async_copy(
                pool.at[table[j, starts[part] // page + p]],
                block.at[pl.ds(p * page, page)],
                sems.at[j, part],
            ).start()

    def write(j, part):
        return pltpu.make_async_copy(block_of(j, part), out.at[j, places[part]], back.at[j, part])

    def forward(j, part):
        block = block_of(j, part)
        pltpu.make_async_copy(block, block, sems.at[j, part]).wait()
        if part:
            write(j, part).start()

    def finish(j, part):
        if part:
            write(j, part).wait()

    each(read)
    each(forward)
    each(finish)


def pages_call(table, lens, pool):
    mine, pages = table.shape
    length = pages * pool.shape[1]
    tail = (mine, length - HEAD) + pool.shape[2:]
    return call(
        page_kernel,
        [pltpu.VMEM((mine, HEAD) + pool.shape[2:], BF16), pltpu.HBM(tail, BF16)],
        [FAR] * 3,
        [
            pltpu.SMEM(table.shape, jnp.int32),
            pltpu.SMEM(lens.shape, jnp.int32),
            pltpu.VMEM(tail, BF16),
            pltpu.SemaphoreType.DMA((mine, 3)),
            pltpu.SemaphoreType.DMA((mine, 3)),
            pltpu.SemaphoreType.DMA((2,)),
        ],
        outs=[VM, FAR],
    )(in_hbm(table), in_hbm(lens), in_hbm(pool))


def attention_kernel(
    lens, sel, arrived, fresh, start, middle, far, out, cache, qs, os, sc, ef, sems
):
    count, rest, _, wide = cache.shape
    requests = range(count)

    def copy_of(j):
        return pltpu.make_async_copy(far.at[j, pl.ds(MIDDLE, rest)], cache.at[j], sems.at[j])

    for j in requests:

        @pl.when(lens[j] > HEAD + MIDDLE)
        def _(j=j):
            copy_of(j).start()

    peers, rows, _ = arrived.shape
    heads = wide // HD
    group = 2 * heads
    inv_scale = 1.0 / math.sqrt(HD)
    picks = sel[...]
    masks = [[picks[:, 1 + k : 2 + k] == float(e) for e in range(EXPERTS)] for k in range(2)]
    for h in range(heads):
        values = [arrived[e * heads + h].astype(F32) for e in range(EXPERTS)]
        for k in range(2):
            total = jnp.where(masks[k][0], values[0], 0.0)
            for e in range(1, EXPERTS):
                total = total + jnp.where(masks[k][e], values[e], 0.0)
            qs[k * heads + h] = total
    ef[...] = jnp.zeros_like(ef)
    ef[0 : 2 * rows] = fresh[...]
    extra = ef[...]
    big = (2 * group, wide)
    block_row = lax.broadcasted_iota(jnp.int32, big, 0) % heads
    diagonal = block_row == lax.broadcasted_iota(jnp.int32, big, 1) // HD
    e_col = lax.broadcasted_iota(jnp.int32, (2 * group, HD), 1)
    e_row = lax.broadcasted_iota(jnp.int32, (2 * group, HD), 0)

    starts = (0, HEAD, HEAD + MIDDLE)

    def rows_of(j, part):
        if part == 0:
            return start[j].reshape(2 * HEAD, wide)
        if part == 1:
            return middle[j].reshape(2 * MIDDLE, wide)
        return cache[j].reshape(2 * rest, wide)

    def masked_scores(q, j, part):
        s = dot_rows(q, rows_of(j, part)) * inv_scale
        column = lax.broadcasted_iota(jnp.int32, s.shape, 1)
        return jnp.where(
            (column % 2 == 0) & (column < 2 * (lens[j] - starts[part])), s, MASKED
        )

    def highest(s):
        return jnp.max(s, axis=1, keepdims=True)

    def added(p):
        return jnp.sum(p, axis=1, keepdims=True)

    def onto_values(p, distance=1):
        return pltpu.roll(p, distance, 1).astype(BF16)

    longer = [jnp.where(lens[j] > starts[2], 1, 0) for j in requests]
    queries, extras, firsts, seconds, tops = [], [], [], [], []
    for j in requests:
        q = jnp.concatenate([qs[:, 2 * j, :], qs[:, 2 * j + 1, :]], axis=0)
        q = jnp.where(diagonal, jnp.concatenate([q] * heads, axis=1), 0.0).astype(BF16)
        live = (e_col == 2 * j) | ((e_col == 2 * j + 1) & (e_row >= group))
        queries.append(q)
        extras.append(jnp.where(live, dot_rows(q, extra) * inv_scale, MASKED))
        firsts.append(masked_scores(q, j, 0))
        seconds.append(masked_scores(queries[j], j, 1))
        top = jnp.maximum(highest(extras[j]), highest(firsts[j]))
        tops.append(jnp.maximum(top, highest(seconds[j])))

    for j in requests:

        def score(_, top, j=j):
            copy_of(j).wait()
            s = masked_scores(queries[j], j, 2)
            sc[j] = s
            return jnp.maximum(top, highest(s))

        tops[j] = lax.fori_loop(0, longer[j], score, tops[j])

    extras = [jnp.exp(extras[j] - tops[j]) for j in requests]
    firsts = [jnp.exp(firsts[j] - tops[j]) for j in requests]
    seconds = [jnp.exp(seconds[j] - tops[j]) for j in requests]
    sums = [added(extras[j]) + added(firsts[j]) + added(seconds[j]) for j in requests]
    mixed = [
        dot(onto_values(extras[j], rows), extra)
        + dot(onto_values(firsts[j]), rows_of(j, 0))
        + dot(onto_values(seconds[j]), rows_of(j, 1))
        for j in requests
    ]
    for j in requests:

        def gather(_, state, j=j):
            p = jnp.exp(sc[j] - tops[j])
            return state[0] + added(p), state[1] + dot(onto_values(p), rows_of(j, 2))

        sums[j], mixed[j] = lax.fori_loop(0, longer[j], gather, (sums[j], mixed[j]))

    for j in requests:
        kept = jnp.where(diagonal, mixed[j], 0.0)
        o = kept[:, :HD]
        for h in range(1, heads):
            o = o + kept[:, h * HD : (h + 1) * HD]
        o = o / sums[j]
        os[:, 2 * j, :] = o[:group]
        os[:, 2 * j + 1, :] = o[group:]
    for h in range(heads):
        one, two = os[h], os[heads + h]
        for e in range(EXPERTS):
            value = jnp.where(masks[0][e], one, 0.0) + jnp.where(masks[1][e], two, 0.0)
            out[e * heads + h] = value.astype(BF16)


def attention_call(lens, sel, arrived, fresh, start, middle, cache):
    rows, wide = arrived.shape[1], cache.shape[-1]
    mine = cache.shape[0]
    rest = cache.shape[1] - MIDDLE
    pairs = 2 * wide // HD
    return call(
        attention_kernel,
        shape_of(arrived.shape),
        [SM, VM, VM, VM, VM, VM, FAR],
        [
            pltpu.VMEM((mine, rest) + cache.shape[2:], BF16),
            pltpu.VMEM((pairs, rows, HD), F32),
            pltpu.VMEM((pairs, rows, HD), F32),
            pltpu.VMEM((mine, 2 * pairs, 2 * rest), F32),
            pltpu.VMEM((HD, wide), BF16),
            pltpu.SemaphoreType.DMA((mine,)),
        ],
        16,
    )(lens, sel, arrived, fresh, in_vmem(start), in_vmem(middle), in_hbm(cache))


def columns_of(z, core, quarter):
    return pl.ds(pl.multiple_of((2 * z + core) * quarter, quarter), quarter)


def answers_of(notes, returned):
    peers, rows, wide = returned.shape
    values = returned[...].reshape(peers * rows, wide)
    return lax.dot_general(
        order_of(notes[...]), values, (((0,), (0,)), ((), ())), preferred_element_type=F32
    ).astype(BF16)


def own_part(a, weight, out):
    peers, halves, rows, quarter = out.shape
    core = lax.axis_index("rep") % 2
    for z in range(halves):
        part = dot(a, weight[0, :, columns_of(z, core, quarter)])
        out[:, z] = part.reshape(peers, rows, quarter)


def other_part(a, weight, part, out):
    peers, halves, rows, quarter = out.shape
    for z in range(halves):
        more = dot(a, weight[z]).reshape(peers, rows, quarter)
        out[:, z] = (part[:, z] + more).astype(BF16)


def project_kernel(notes, returned, weight, out):
    own_part(answers_of(notes, returned), weight, out)


def finish_project_kernel(notes, returned, weight, part, out):
    other_part(answers_of(notes, returned), weight, part, out)


def part_kernel(units, weight, out):
    own_part(units[...], weight, out)


def place_kernel(*refs):
    pieces, out = refs[:-1], refs[-1]
    rep = lax.axis_index("rep")
    count, _, width = out.shape
    quarter = width // len(pieces)
    for m, piece in enumerate(pieces):
        place = pl.multiple_of((rep ^ m) * quarter, quarter)
        out[:, :, pl.ds(place, quarter)] = piece[...].reshape(count, 2, quarter)


def raw_products(block, side, gains, wg, wu):
    peers, halves, rows, quarter = block.shape
    total = peers * rows
    squares = jnp.zeros((total, 1), F32)
    gate = jnp.zeros((total, wg.shape[1]), F32)
    up = jnp.zeros((total, wg.shape[1]), F32)
    for z in range(halves):
        where = columns_of(z, side, quarter)
        v = block[:, z].reshape(total, quarter).astype(F32)
        squares = squares + jnp.sum(v * v, axis=1, keepdims=True)
        v = (v * gains[1:2, where]).astype(BF16)
        gate = gate + dot_rows(v, wg[0, :, where])
        up = up + dot_rows(v, wu[0, :, where])
    return squares, gate, up


def near_kernel(near, gains, wg, wu, squares, gate, up):
    core = lax.axis_index("rep") % 2
    a, b, c = raw_products(near, core, gains, wg, wu)
    squares[...] = jnp.broadcast_to(a, squares.shape)
    gate[...] = b
    up[...] = c


def expert_kernel(far, gains, wg, wu, wd, near_squares, near_gate, near_up, units, theirs):
    peers, halves, rows, quarter = far.shape
    core = lax.axis_index("rep") % 2
    squares, gate, up = raw_products(far, 1 - core, gains, wg, wu)
    squares = squares + near_squares[:, :1]
    scaling = lax.rsqrt(squares / (2 * halves * quarter) + EPSILON)
    gate = (gate + near_gate[...]) * scaling
    up = (up + near_up[...]) * scaling
    a = (gate / (1.0 + jnp.exp(-gate)) * up).astype(BF16)
    units[...] = a
    for z in range(halves):
        part = dot(a, wd[0, :, columns_of(z, 1 - core, quarter)])
        theirs[:, z] = part.astype(BF16).reshape(peers, rows, quarter)


def shards(
    tokens,
    norm_gains,
    w_kv,
    w_query,
    w_out,
    w_gate,
    w_up,
    w_down,
    kv_pages,
    page_table,
    cache_len,
    route_ids,
    route_gates,
    new_slot,
):
    req_count = lax.axis_size("req")
    rep_count = lax.axis_size("rep")
    mine, _, width = tokens.shape
    rows = 2 * mine
    total = rows * req_count
    half = width // 2
    quarter = width // rep_count
    wide = kv_pages.shape[-1]
    rep = lax.axis_index("rep")
    swap = [(p, p ^ 1) for p in range(rep_count)]
    wide_groups = [
        [r * rep_count + 2 * z + c for r in range(req_count) for z in range(rep_count // 2)]
        for c in range(2)
    ]
    peers = req_count * rep_count // 2
    split = (req_count, rep_count // 2, rows, quarter)

    def spread_req(value):
        return lax.all_to_all(value, "req", split_axis=0, concat_axis=0, tiled=True)

    def spread_wide(value):
        return lax.all_to_all(
            value,
            ("req", "rep"),
            split_axis=0,
            concat_axis=0,
            tiled=True,
            axis_index_groups=wide_groups,
        )

    def other_core(value):
        return lax.ppermute(value, "rep", swap)

    inputs = tokens.reshape(rows, width)
    ids = route_ids.transpose(0, 2, 1, 3).reshape(rows, 2, 2)
    gates = route_gates.astype(F32).transpose(0, 2, 1, 3).reshape(rows, 2, 2)
    experts_row = jnp.arange(EXPERTS, dtype=jnp.int32)
    shares = jnp.sum(jnp.where(ids[..., None] == experts_row, gates[..., None], 0.0), axis=2)
    shares = shares.transpose(1, 2, 0)[..., None]
    shares = [shares[0], shares[1]]
    kept = lax.dynamic_slice_in_dim(inputs, rep * quarter, quarter, 1).astype(F32)

    routes = route_ids.transpose(1, 2, 3, 0)
    message = call(
        message_kernel,
        shape_of((req_count, rows, half + HD)),
        [FAR] * 4,
        [
            pltpu.SMEM(new_slot.shape, jnp.int32),
            pltpu.SMEM(routes.shape, jnp.int32),
            pltpu.VMEM(tokens.shape, BF16),
            pltpu.VMEM(norm_gains.shape, F32),
            pltpu.SemaphoreType.DMA((4,)),
        ],
    )(in_hbm(new_slot), in_hbm(routes), in_hbm(tokens), in_hbm(norm_gains))
    near = spread_req(message)
    start, cache = pages_call(page_table, cache_len, kv_pages)
    near, start, cache, shares, kept = lax.optimization_barrier(
        (near, start, cache, shares, kept)
    )
    far = other_core(near)
    wq, begun = call(
        near_query_kernel,
        [pltpu.VMEM(w_query.shape, BF16), shape_of((total, HD), F32)],
        [VM, FAR],
        [pltpu.SemaphoreType.DMA],
    )(near, in_hbm(w_query))
    ordered, notes = call(
        query_kernel, [shape_of((req_count, rows, HD)), shape_of((total, HD))], [VM] * 4
    )(near, far, in_vmem(wq), begun)
    arrived = spread_req(ordered)
    rows_shape = (rep_count // 2, w_out.shape[1], quarter)
    sel, fresh, picked = call(
        own_kernel,
        [
            shape_of((rows, HD), F32),
            shape_of((2 * rows, wide)),
            pltpu.HBM(rows_shape, BF16),
        ],
        [VM, VM, VM, FAR],
        [
            pltpu.VMEM(rows_shape, BF16),
            pltpu.SemaphoreType.DMA((rep_count // 2,)),
            pltpu.SemaphoreType.DMA,
        ],
        outs=[VM, VM, FAR],
    )(near, far, w_kv, in_hbm(w_out))
    sel, cache = lax.optimization_barrier((sel, cache))
    middle = call(
        middle_kernel,
        pltpu.VMEM((mine, MIDDLE) + cache.shape[2:], BF16),
        [FAR],
        [pltpu.SemaphoreType.DMA],
    )(in_hbm(cache))
    back = attention_call(cache_len, sel, arrived, fresh, start, middle, cache)
    returned = spread_req(back)
    returned, picked = lax.optimization_barrier((returned, picked))
    returned_x, out_x = other_core(returned), other_core(picked)
    part = call(project_kernel, shape_of(split, F32), [VM] * 3)(notes, returned, w_out)
    summed = call(finish_project_kernel, shape_of(split), [VM] * 4)(
        notes, returned_x, out_x, part
    )

    def reduce_wide(summed, share):
        got = spread_wide(summed.reshape(peers, rows, quarter))
        got = got.reshape(EXPERTS, peers // EXPERTS, rows, quarter).astype(F32)
        return jnp.sum(jnp.sum(got, axis=1) * share, axis=0)

    hidden = kept + reduce_wide(summed, shares[0])
    copies = jnp.broadcast_to(hidden.astype(BF16)[None], (peers, rows, quarter))
    block = spread_wide(copies)
    far = other_core(block).reshape(split)
    wg, wu = w_gate.transpose(0, 2, 1), w_up.transpose(0, 2, 1)
    units_dev = w_down.shape[1]
    squares, gate, up = call(
        near_kernel,
        [shape_of((total, HD), F32)] + [shape_of((total, units_dev), F32)] * 2,
        [VM] * 4,
    )(block.reshape(split), norm_gains, wg, wu)
    units, theirs = call(
        expert_kernel, [shape_of((total, units_dev)), shape_of(split)], [VM] * 8
    )(far, norm_gains, wg, wu, w_down, squares, gate, up)
    theirs = other_core(theirs)
    part = call(part_kernel, shape_of(split, F32), [VM] * 2)(units, w_down)
    feed = reduce_wide((part + theirs.astype(F32)).astype(BF16), shares[1])
    piece = (hidden + feed).astype(BF16)
    pieces = [piece] + [
        lax.ppermute(piece, "rep", [(p, p ^ m) for p in range(rep_count)])
        for m in range(1, rep_count)
    ]
    return call(place_kernel, shape_of((mine, 2, width)), [VM] * rep_count)(*pieces)


def solution(mesh):
    in_specs = (
        P("req", None, None),
        P(),
        P(None, None, "rep"),
        P("req", None, "rep"),
        P("req", "rep", None),
        P("req", None, "rep"),
        P("req", None, "rep"),
        P("req", "rep", None),
        P("req", None, None, "rep"),
        P("req", None),
        P("req"),
        P("req", None, None, None),
        P("req", None, None, None),
        P("req"),
    )
    out_specs = P("req", None, None)
    return jax.shard_map(shards, mesh=mesh, in_specs=in_specs, out_specs=out_specs, check_vma=False)
```

```python
import functools
import math

import jax
import jax.numpy as jnp
from jax import lax
from jax.experimental import pallas as pl
from jax.experimental.pallas import tpu as pltpu
from jax.sharding import PartitionSpec as P

HD = 128
EXPERTS = 8
HEAD = 256
MIDDLE = 128
EPSILON = 1e-06
MASKED = -1e30
F32 = jnp.float32
BF16 = jnp.bfloat16
VM = pl.BlockSpec(memory_space=pltpu.VMEM)
SM = pl.BlockSpec(memory_space=pltpu.SMEM)
FAR = pl.BlockSpec(memory_space=pltpu.HBM)
ROWS_BY_ROWS = (((1,), (1,)), ((), ()))


def dot(a, b):
    return jnp.dot(a, b, preferred_element_type=F32)


def dot_rows(a, b):
    return lax.dot_general(a, b, ROWS_BY_ROWS, preferred_element_type=F32)


def call(body, out, ins, scratch=(), limit=12, outs=None):
    many = isinstance(out, (list, tuple))
    return pl.pallas_call(
        body,
        out_shape=out,
        in_specs=ins,
        out_specs=outs or ([VM] * len(out) if many else VM),
        scratch_shapes=scratch,
        compiler_params=pltpu.CompilerParams(vmem_limit_bytes=limit << 20),
    )


def in_hbm(value):
    return pltpu.with_memory_space_constraint(value, pltpu.HBM)


def in_vmem(value):
    return pltpu.with_memory_space_constraint(value, pltpu.VMEM)


def shape_of(shape, dtype=BF16):
    return jax.ShapeDtypeStruct(shape, dtype)


def message_kernel(slots_far, ids_far, tokens_far, gains_far, out, slots, ids, tokens, gains, sems):
    pairs = ((slots_far, slots), (ids_far, ids), (tokens_far, tokens), (gains_far, gains))
    copies = [pltpu.make_async_copy(a, b, sems.at[i]) for i, (a, b) in enumerate(pairs)]
    for copy in copies:
        copy.start()
    for copy in copies:
        copy.wait()
    count, _, width = tokens.shape
    rows = 2 * count
    half = width // 2
    rank, core = lax.axis_index("req"), lax.axis_index("rep") % 2
    x = tokens[...].reshape(rows, width).astype(F32)
    scaling = lax.rsqrt(jnp.mean(x * x, axis=1, keepdims=True) + EPSILON)
    normed = (x * scaling * gains[0:1]).astype(BF16)
    out[0, :, :half] = jnp.where(core == 0, normed[:, :half], normed[:, half:])
    row = lax.broadcasted_iota(jnp.int32, (rows, HD), 0)
    lane = lax.broadcasted_iota(jnp.int32, (rows, HD), 1)
    notes = jnp.zeros((rows, HD), jnp.int32)
    for j in range(count):
        for s in range(2):
            here = row == 2 * j + s
            source = 2 * (rank * count + j) if s == 0 else 2 * slots[j] + 1
            notes = jnp.where(here & (lane == 0), source, notes)
            for k in range(2):
                notes = jnp.where(here & (lane == 1 + k), ids[0, s, k, j], notes)
    out[0, :, half:] = notes.astype(F32).astype(BF16)
    message = out[0]
    for r in range(1, out.shape[0]):
        out[r] = message


def order_of(notes):
    source = notes[:, :1]
    column = lax.broadcasted_iota(jnp.int32, (notes.shape[0], notes.shape[0]), 1)
    return (source.astype(jnp.int32) == column).astype(BF16)


def near_query_kernel(near, wq_far, wq, out, sem):
    load = pltpu.make_async_copy(wq_far, wq, sem)
    load.start()
    peers, rows, wide = near.shape
    half = wide - HD
    core = lax.axis_index("rep") % 2
    a = near[:, :, :half].reshape(peers * rows, half)
    load.wait()
    out[...] = dot(a, wq[0, pl.ds(pl.multiple_of(core * half, half), half)])


def query_kernel(near, far, wq, begun, out, notes):
    peers, rows, wide = near.shape
    half = wide - HD
    core = lax.axis_index("rep") % 2
    b = far[:, :, :half].reshape(peers * rows, half)
    q = begun[...] + dot(b, wq[0, pl.ds(pl.multiple_of((1 - core) * half, half), half)])
    marks = near[:, :, half:].reshape(peers * rows, HD)
    notes[...] = marks
    out[...] = dot(order_of(marks), q.astype(BF16)).astype(BF16).reshape(out.shape)


def own_kernel(near, far, wkv_far, sel, fresh, wkv, sems):
    pieces = sems.shape[0]
    size = wkv.shape[0] // pieces
    copies = [
        pltpu.make_async_copy(wkv_far.at[pl.ds(i * size, size)], wkv.at[pl.ds(i * size, size)], sems.at[i])
        for i in range(pieces)
    ]
    for copy in copies:
        copy.start()
    peers, rows, wide = near.shape
    half = wide - HD
    rank, core = lax.axis_index("req"), lax.axis_index("rep") % 2
    source = near[rank][:, half : half + 1]
    column = lax.broadcasted_iota(jnp.int32, (rows, peers * rows), 1)
    order = (source.astype(jnp.int32) == column).astype(BF16)
    a = dot(order, near[...].reshape(peers * rows, wide))
    b = dot(order, far[:, :, :half].reshape(peers * rows, half)).astype(BF16)
    sel[...] = a[:, half:]
    a = a[:, :half].astype(BF16)
    parts = (jnp.where(core == 0, a, b), jnp.where(core == 0, b, a))
    spans = half // HD
    chunks = [part[:, c * HD : (c + 1) * HD] for part in parts for c in range(spans)]
    twice = (HD, 2 * HD)
    feature = lax.broadcasted_iota(jnp.int32, twice, 1) // 2
    doubling = (lax.broadcasted_iota(jnp.int32, twice, 0) == feature).astype(BF16)
    doubled = dot(jnp.concatenate(chunks, axis=0), doubling)
    even = lax.broadcasted_iota(jnp.int32, (rows, 2 * HD), 1) % 2 == 0
    total = jnp.zeros(fresh.shape, F32)
    for c in range(2 * spans):
        if c * HD % size == 0:
            copies[c * HD // size].wait()
        v = doubled[c * rows : (c + 1) * rows]
        v = jnp.concatenate([jnp.where(even, v, 0.0), jnp.where(even, 0.0, v)], axis=0)
        w = wkv[c * HD : (c + 1) * HD].reshape(2 * HD, fresh.shape[1])
        total = total + dot(v.astype(BF16), w)
    fresh[...] = total.astype(BF16)


def page_kernel(
    table_far, lens_far, pool, weight, start, out, picked_far, table, lens, staged, picked, sems, back, small, pick
):
    halves, _, quarter = picked.shape
    side = 1 - lax.axis_index("rep") % 2
    picks = [
        pltpu.make_async_copy(weight.at[0, :, columns_of(z, side, quarter)], picked.at[z], pick.at[z])
        for z in range(halves)
    ]
    for copy in picks:
        copy.start()
    first = pltpu.make_async_copy(table_far, table, small.at[0])
    second = pltpu.make_async_copy(lens_far, lens, small.at[1])
    first.start()
    second.start()
    first.wait()
    second.wait()
    count = out.shape[0]
    page = pool.shape[1]
    tail = out.shape[1]
    sizes = (HEAD, MIDDLE, tail - MIDDLE)
    starts = (0, HEAD, HEAD + MIDDLE)
    places = (None, pl.ds(0, MIDDLE), pl.ds(MIDDLE, tail - MIDDLE))

    def each(act):
        for part in range(3):
            for j in range(count):
                if part < 2:
                    act(j, part)
                else:
                    pl.when(lens[j] > starts[2])(functools.partial(act, j, part))

    def block_of(j, part):
        return start.at[j] if part == 0 else staged.at[j, places[part]]

    def read(j, part):
        block = block_of(j, part)
        for p in range(sizes[part] // page):
            pltpu.make_async_copy(
                pool.at[table[j, starts[part] // page + p]],
                block.at[pl.ds(p * page, page)],
                sems.at[j, part],
            ).start()

    def write(j, part):
        return pltpu.make_async_copy(block_of(j, part), out.at[j, places[part]], back.at[j, part])

    def forward(j, part):
        block = block_of(j, part)
        pltpu.make_async_copy(block, block, sems.at[j, part]).wait()
        if part:
            write(j, part).start()

    def finish(j, part):
        if part:
            write(j, part).wait()

    each(read)
    for copy in picks:
        copy.wait()
    send = pltpu.make_async_copy(picked, picked_far, pick.at[halves])
    send.start()
    each(forward)
    each(finish)
    send.wait()


def pages_call(table, lens, pool, weight, quarter):
    mine, pages = table.shape
    length = pages * pool.shape[1]
    tail = (mine, length - HEAD) + pool.shape[2:]
    rows_shape = (weight.shape[2] // (2 * quarter), weight.shape[1], quarter)
    return call(
        page_kernel,
        [
            pltpu.VMEM((mine, HEAD) + pool.shape[2:], BF16),
            pltpu.HBM(tail, BF16),
            pltpu.HBM(rows_shape, BF16),
        ],
        [FAR] * 4,
        [
            pltpu.SMEM(table.shape, jnp.int32),
            pltpu.SMEM(lens.shape, jnp.int32),
            pltpu.VMEM(tail, BF16),
            pltpu.VMEM(rows_shape, BF16),
            pltpu.SemaphoreType.DMA((mine, 3)),
            pltpu.SemaphoreType.DMA((mine, 3)),
            pltpu.SemaphoreType.DMA((2,)),
            pltpu.SemaphoreType.DMA((rows_shape[0] + 1,)),
        ],
        outs=[VM, FAR, FAR],
    )(in_hbm(table), in_hbm(lens), in_hbm(pool), in_hbm(weight))


def attention_kernel(
    lens, sel, arrived, fresh, start, far, out, middle, cache, qs, os, sc, ef, sems, one
):
    fetch = pltpu.make_async_copy(far.at[:, pl.ds(0, MIDDLE)], middle, one)
    fetch.start()
    count, rest, _, wide = cache.shape
    requests = range(count)

    def copy_of(j):
        return pltpu.make_async_copy(far.at[j, pl.ds(MIDDLE, rest)], cache.at[j], sems.at[j])

    for j in requests:

        @pl.when(lens[j] > HEAD + MIDDLE)
        def _(j=j):
            copy_of(j).start()

    peers, rows, _ = arrived.shape
    heads = wide // HD
    group = 2 * heads
    inv_scale = 1.0 / math.sqrt(HD)
    picks = sel[...]
    masks = [[picks[:, 1 + k : 2 + k] == float(e) for e in range(EXPERTS)] for k in range(2)]
    for h in range(heads):
        values = [arrived[e * heads + h].astype(F32) for e in range(EXPERTS)]
        for k in range(2):
            total = jnp.where(masks[k][0], values[0], 0.0)
            for e in range(1, EXPERTS):
                total = total + jnp.where(masks[k][e], values[e], 0.0)
            qs[k * heads + h] = total
    ef[...] = jnp.zeros_like(ef)
    ef[0 : 2 * rows] = fresh[...]
    extra = ef[...]
    big = (2 * group, wide)
    block_row = lax.broadcasted_iota(jnp.int32, big, 0) % heads
    diagonal = block_row == lax.broadcasted_iota(jnp.int32, big, 1) // HD
    e_col = lax.broadcasted_iota(jnp.int32, (2 * group, HD), 1)
    e_row = lax.broadcasted_iota(jnp.int32, (2 * group, HD), 0)

    starts = (0, HEAD, HEAD + MIDDLE)

    def rows_of(j, part):
        if part == 0:
            return start[j].reshape(2 * HEAD, wide)
        if part == 1:
            return middle[j].reshape(2 * MIDDLE, wide)
        return cache[j].reshape(2 * rest, wide)

    def masked_scores(q, j, part):
        s = dot_rows(q, rows_of(j, part)) * inv_scale
        column = lax.broadcasted_iota(jnp.int32, s.shape, 1)
        return jnp.where(
            (column % 2 == 0) & (column < 2 * (lens[j] - starts[part])), s, MASKED
        )

    def highest(s):
        return jnp.max(s, axis=1, keepdims=True)

    def added(p):
        return jnp.sum(p, axis=1, keepdims=True)

    def onto_values(p, distance=1):
        return pltpu.roll(p, distance, 1).astype(BF16)

    longer = [jnp.where(lens[j] > starts[2], 1, 0) for j in requests]
    queries, extras, firsts, seconds, tops = [], [], [], [], []
    for j in requests:
        q = jnp.concatenate([qs[:, 2 * j, :], qs[:, 2 * j + 1, :]], axis=0)
        q = jnp.where(diagonal, jnp.concatenate([q] * heads, axis=1), 0.0).astype(BF16)
        live = (e_col == 2 * j) | ((e_col == 2 * j + 1) & (e_row >= group))
        queries.append(q)
        extras.append(jnp.where(live, dot_rows(q, extra) * inv_scale, MASKED))
        firsts.append(masked_scores(q, j, 0))
    fetch.wait()
    for j in requests:
        seconds.append(masked_scores(queries[j], j, 1))
        top = jnp.maximum(highest(extras[j]), highest(firsts[j]))
        tops.append(jnp.maximum(top, highest(seconds[j])))

    for j in requests:

        def score(_, top, j=j):
            copy_of(j).wait()
            s = masked_scores(queries[j], j, 2)
            sc[j] = s
            return jnp.maximum(top, highest(s))

        tops[j] = lax.fori_loop(0, longer[j], score, tops[j])

    extras = [jnp.exp(extras[j] - tops[j]) for j in requests]
    firsts = [jnp.exp(firsts[j] - tops[j]) for j in requests]
    seconds = [jnp.exp(seconds[j] - tops[j]) for j in requests]
    sums = [added(extras[j]) + added(firsts[j]) + added(seconds[j]) for j in requests]
    mixed = [
        dot(onto_values(extras[j], rows), extra)
        + dot(onto_values(firsts[j]), rows_of(j, 0))
        + dot(onto_values(seconds[j]), rows_of(j, 1))
        for j in requests
    ]
    for j in requests:

        def gather(_, state, j=j):
            p = jnp.exp(sc[j] - tops[j])
            return state[0] + added(p), state[1] + dot(onto_values(p), rows_of(j, 2))

        sums[j], mixed[j] = lax.fori_loop(0, longer[j], gather, (sums[j], mixed[j]))

    for j in requests:
        kept = jnp.where(diagonal, mixed[j], 0.0)
        o = kept[:, :HD]
        for h in range(1, heads):
            o = o + kept[:, h * HD : (h + 1) * HD]
        o = o / sums[j]
        os[:, 2 * j, :] = o[:group]
        os[:, 2 * j + 1, :] = o[group:]
    for h in range(heads):
        one, two = os[h], os[heads + h]
        for e in range(EXPERTS):
            value = jnp.where(masks[0][e], one, 0.0) + jnp.where(masks[1][e], two, 0.0)
            out[e * heads + h] = value.astype(BF16)


def attention_call(lens, sel, arrived, fresh, start, cache):
    rows, wide = arrived.shape[1], cache.shape[-1]
    mine = cache.shape[0]
    rest = cache.shape[1] - MIDDLE
    pairs = 2 * wide // HD
    return call(
        attention_kernel,
        shape_of(arrived.shape),
        [SM, VM, VM, VM, VM, FAR],
        [
            pltpu.VMEM((mine, MIDDLE) + cache.shape[2:], BF16),
            pltpu.VMEM((mine, rest) + cache.shape[2:], BF16),
            pltpu.VMEM((pairs, rows, HD), F32),
            pltpu.VMEM((pairs, rows, HD), F32),
            pltpu.VMEM((mine, 2 * pairs, 2 * rest), F32),
            pltpu.VMEM((HD, wide), BF16),
            pltpu.SemaphoreType.DMA((mine,)),
            pltpu.SemaphoreType.DMA,
        ],
        16,
    )(lens, sel, arrived, fresh, in_vmem(start), in_hbm(cache))


def columns_of(z, core, quarter):
    return pl.ds(pl.multiple_of((2 * z + core) * quarter, quarter), quarter)


def answers_of(notes, returned):
    peers, rows, wide = returned.shape
    values = returned[...].reshape(peers * rows, wide)
    return lax.dot_general(
        order_of(notes[...]), values, (((0,), (0,)), ((), ())), preferred_element_type=F32
    ).astype(BF16)


def own_part(a, weight, out):
    peers, halves, rows, quarter = out.shape
    core = lax.axis_index("rep") % 2
    for z in range(halves):
        part = dot(a, weight[0, :, columns_of(z, core, quarter)])
        out[:, z] = part.reshape(peers, rows, quarter)


def other_part(a, weight, part, out):
    peers, halves, rows, quarter = out.shape
    for z in range(halves):
        more = dot(a, weight[z]).reshape(peers, rows, quarter)
        out[:, z] = (part[:, z] + more).astype(BF16)


def project_kernel(notes, returned, weight, out):
    own_part(answers_of(notes, returned), weight, out)


def finish_project_kernel(notes, returned, weight, part, out):
    other_part(answers_of(notes, returned), weight, part, out)


def part_kernel(units, weight, out):
    own_part(units[...], weight, out)


def place_kernel(*refs):
    pieces, out = refs[:-1], refs[-1]
    rep = lax.axis_index("rep")
    count, _, width = out.shape
    quarter = width // len(pieces)
    for m, piece in enumerate(pieces):
        place = pl.multiple_of((rep ^ m) * quarter, quarter)
        out[:, :, pl.ds(place, quarter)] = piece[...].reshape(count, 2, quarter)


def raw_products(block, side, gains, wg, wu):
    peers, halves, rows, quarter = block.shape
    total = peers * rows
    squares = jnp.zeros((total, 1), F32)
    gate = jnp.zeros((total, wg.shape[1]), F32)
    up = jnp.zeros((total, wg.shape[1]), F32)
    for z in range(halves):
        where = columns_of(z, side, quarter)
        v = block[:, z].reshape(total, quarter).astype(F32)
        squares = squares + jnp.sum(v * v, axis=1, keepdims=True)
        v = (v * gains[1:2, where]).astype(BF16)
        gate = gate + dot_rows(v, wg[0, :, where])
        up = up + dot_rows(v, wu[0, :, where])
    return squares, gate, up


def near_kernel(near, gains, wg, wu, squares, gate, up):
    core = lax.axis_index("rep") % 2
    a, b, c = raw_products(near, core, gains, wg, wu)
    squares[...] = jnp.broadcast_to(a, squares.shape)
    gate[...] = b
    up[...] = c


def expert_kernel(far, gains, wg, wu, wd, near_squares, near_gate, near_up, units, theirs):
    peers, halves, rows, quarter = far.shape
    core = lax.axis_index("rep") % 2
    squares, gate, up = raw_products(far, 1 - core, gains, wg, wu)
    squares = squares + near_squares[:, :1]
    scaling = lax.rsqrt(squares / (2 * halves * quarter) + EPSILON)
    gate = (gate + near_gate[...]) * scaling
    up = (up + near_up[...]) * scaling
    a = (gate / (1.0 + jnp.exp(-gate)) * up).astype(BF16)
    units[...] = a
    for z in range(halves):
        part = dot(a, wd[0, :, columns_of(z, 1 - core, quarter)])
        theirs[:, z] = part.astype(BF16).reshape(peers, rows, quarter)


def shards(
    tokens,
    norm_gains,
    w_kv,
    w_query,
    w_out,
    w_gate,
    w_up,
    w_down,
    kv_pages,
    page_table,
    cache_len,
    route_ids,
    route_gates,
    new_slot,
):
    req_count = lax.axis_size("req")
    rep_count = lax.axis_size("rep")
    mine, _, width = tokens.shape
    rows = 2 * mine
    total = rows * req_count
    half = width // 2
    quarter = width // rep_count
    wide = kv_pages.shape[-1]
    rep = lax.axis_index("rep")
    swap = [(p, p ^ 1) for p in range(rep_count)]
    wide_groups = [
        [r * rep_count + 2 * z + c for r in range(req_count) for z in range(rep_count // 2)]
        for c in range(2)
    ]
    peers = req_count * rep_count // 2
    split = (req_count, rep_count // 2, rows, quarter)

    def spread_req(value):
        return lax.all_to_all(value, "req", split_axis=0, concat_axis=0, tiled=True)

    def spread_wide(value):
        return lax.all_to_all(
            value,
            ("req", "rep"),
            split_axis=0,
            concat_axis=0,
            tiled=True,
            axis_index_groups=wide_groups,
        )

    def other_core(value):
        return lax.ppermute(value, "rep", swap)

    inputs = tokens.reshape(rows, width)
    ids = route_ids.transpose(0, 2, 1, 3).reshape(rows, 2, 2)
    gates = route_gates.astype(F32).transpose(0, 2, 1, 3).reshape(rows, 2, 2)
    experts_row = jnp.arange(EXPERTS, dtype=jnp.int32)
    shares = jnp.sum(jnp.where(ids[..., None] == experts_row, gates[..., None], 0.0), axis=2)
    shares = shares.transpose(1, 2, 0)[..., None]
    shares = [shares[0], shares[1]]
    kept = lax.dynamic_slice_in_dim(inputs, rep * quarter, quarter, 1).astype(F32)

    routes = route_ids.transpose(1, 2, 3, 0)
    message = call(
        message_kernel,
        shape_of((req_count, rows, half + HD)),
        [FAR] * 4,
        [
            pltpu.SMEM(new_slot.shape, jnp.int32),
            pltpu.SMEM(routes.shape, jnp.int32),
            pltpu.VMEM(tokens.shape, BF16),
            pltpu.VMEM(norm_gains.shape, F32),
            pltpu.SemaphoreType.DMA((4,)),
        ],
    )(in_hbm(new_slot), in_hbm(routes), in_hbm(tokens), in_hbm(norm_gains))
    near = spread_req(message)
    start, cache, picked = pages_call(page_table, cache_len, kv_pages, w_out, quarter)
    near, start, cache, picked, shares, kept = lax.optimization_barrier(
        (near, start, cache, picked, shares, kept)
    )
    far = other_core(near)
    wq, begun = call(
        near_query_kernel,
        [pltpu.VMEM(w_query.shape, BF16), shape_of((total, HD), F32)],
        [VM, FAR],
        [pltpu.SemaphoreType.DMA],
    )(near, in_hbm(w_query))
    ordered, notes = call(
        query_kernel, [shape_of((req_count, rows, HD)), shape_of((total, HD))], [VM] * 4
    )(near, far, in_vmem(wq), begun)
    arrived = spread_req(ordered)
    sel, fresh = call(
        own_kernel,
        [shape_of((rows, HD), F32), shape_of((2 * rows, wide))],
        [VM, VM, FAR],
        [pltpu.VMEM(w_kv.shape, BF16), pltpu.SemaphoreType.DMA((8,))],
    )(near, far, in_hbm(w_kv))
    back = attention_call(cache_len, sel, arrived, fresh, start, cache)
    returned = spread_req(back)
    returned, picked = lax.optimization_barrier((returned, picked))
    returned_x, out_x = other_core(returned), other_core(picked)
    part = call(project_kernel, shape_of(split, F32), [VM] * 3)(notes, returned, w_out)
    summed = call(finish_project_kernel, shape_of(split), [VM] * 4)(
        notes, returned_x, out_x, part
    )

    def reduce_wide(summed, share):
        got = spread_wide(summed.reshape(peers, rows, quarter))
        got = got.reshape(EXPERTS, peers // EXPERTS, rows, quarter).astype(F32)
        return jnp.sum(jnp.sum(got, axis=1) * share, axis=0)

    hidden = kept + reduce_wide(summed, shares[0])
    copies = jnp.broadcast_to(hidden.astype(BF16)[None], (peers, rows, quarter))
    block = spread_wide(copies)
    far = other_core(block).reshape(split)
    wg, wu = w_gate.transpose(0, 2, 1), w_up.transpose(0, 2, 1)
    units_dev = w_down.shape[1]
    squares, gate, up = call(
        near_kernel,
        [shape_of((total, HD), F32)] + [shape_of((total, units_dev), F32)] * 2,
        [VM] * 4,
    )(block.reshape(split), norm_gains, wg, wu)
    units, theirs = call(
        expert_kernel, [shape_of((total, units_dev)), shape_of(split)], [VM] * 8
    )(far, norm_gains, wg, wu, w_down, squares, gate, up)
    theirs = other_core(theirs)
    part = call(part_kernel, shape_of(split, F32), [VM] * 2)(units, w_down)
    feed = reduce_wide((part + theirs.astype(F32)).astype(BF16), shares[1])
    piece = (hidden + feed).astype(BF16)
    pieces = [piece] + [
        lax.ppermute(piece, "rep", [(p, p ^ m) for p in range(rep_count)])
        for m in range(1, rep_count)
    ]
    return call(place_kernel, shape_of((mine, 2, width)), [VM] * rep_count)(*pieces)


def solution(mesh):
    in_specs = (
        P("req", None, None),
        P(),
        P(None, None, "rep"),
        P("req", None, "rep"),
        P("req", "rep", None),
        P("req", None, "rep"),
        P("req", None, "rep"),
        P("req", "rep", None),
        P("req", None, None, "rep"),
        P("req", None),
        P("req"),
        P("req", None, None, None),
        P("req", None, None, None),
        P("req"),
    )
    out_specs = P("req", None, None)
    return jax.shard_map(shards, mesh=mesh, in_specs=in_specs, out_specs=out_specs, check_vma=False)
```

```python
import functools
import math

import jax
import jax.numpy as jnp
from jax import lax
from jax.experimental import pallas as pl
from jax.experimental.pallas import tpu as pltpu
from jax.sharding import PartitionSpec as P

HD = 128
EXPERTS = 8
HEAD = 256
MIDDLE = 256
EPSILON = 1e-06
MASKED = -1e30
F32 = jnp.float32
BF16 = jnp.bfloat16
VM = pl.BlockSpec(memory_space=pltpu.VMEM)
SM = pl.BlockSpec(memory_space=pltpu.SMEM)
FAR = pl.BlockSpec(memory_space=pltpu.HBM)
ROWS_BY_ROWS = (((1,), (1,)), ((), ()))


def dot(a, b):
    return jnp.dot(a, b, preferred_element_type=F32)


def dot_rows(a, b):
    return lax.dot_general(a, b, ROWS_BY_ROWS, preferred_element_type=F32)


def call(body, out, ins, scratch=(), limit=12, outs=None):
    many = isinstance(out, (list, tuple))
    return pl.pallas_call(
        body,
        out_shape=out,
        in_specs=ins,
        out_specs=outs or ([VM] * len(out) if many else VM),
        scratch_shapes=scratch,
        compiler_params=pltpu.CompilerParams(vmem_limit_bytes=limit << 20),
    )


def in_hbm(value):
    return pltpu.with_memory_space_constraint(value, pltpu.HBM)


def in_vmem(value):
    return pltpu.with_memory_space_constraint(value, pltpu.VMEM)


def shape_of(shape, dtype=BF16):
    return jax.ShapeDtypeStruct(shape, dtype)


def message_kernel(slots_far, ids_far, tokens_far, gains_far, out, slots, ids, tokens, gains, sems):
    pairs = ((slots_far, slots), (ids_far, ids), (tokens_far, tokens), (gains_far, gains))
    copies = [pltpu.make_async_copy(a, b, sems.at[i]) for i, (a, b) in enumerate(pairs)]
    for copy in copies:
        copy.start()
    for copy in copies:
        copy.wait()
    count, _, width = tokens.shape
    rows = 2 * count
    half = width // 2
    rank, core = lax.axis_index("req"), lax.axis_index("rep") % 2
    x = tokens[...].reshape(rows, width).astype(F32)
    scaling = lax.rsqrt(jnp.mean(x * x, axis=1, keepdims=True) + EPSILON)
    normed = (x * scaling * gains[0:1]).astype(BF16)
    out[0, :, :half] = jnp.where(core == 0, normed[:, :half], normed[:, half:])
    row = lax.broadcasted_iota(jnp.int32, (rows, HD), 0)
    lane = lax.broadcasted_iota(jnp.int32, (rows, HD), 1)
    notes = jnp.zeros((rows, HD), jnp.int32)
    for j in range(count):
        for s in range(2):
            here = row == 2 * j + s
            source = 2 * (rank * count + j) if s == 0 else 2 * slots[j] + 1
            notes = jnp.where(here & (lane == 0), source, notes)
            for k in range(2):
                notes = jnp.where(here & (lane == 1 + k), ids[0, s, k, j], notes)
    out[0, :, half:] = notes.astype(F32).astype(BF16)
    message = out[0]
    for r in range(1, out.shape[0]):
        out[r] = message


def order_of(notes):
    source = notes[:, :1]
    column = lax.broadcasted_iota(jnp.int32, (notes.shape[0], notes.shape[0]), 1)
    return (source.astype(jnp.int32) == column).astype(BF16)


def near_query_kernel(near, wq_far, wq, out, sem):
    load = pltpu.make_async_copy(wq_far, wq, sem)
    load.start()
    peers, rows, wide = near.shape
    half = wide - HD
    core = lax.axis_index("rep") % 2
    a = near[:, :, :half].reshape(peers * rows, half)
    load.wait()
    out[...] = dot(a, wq[0, pl.ds(pl.multiple_of(core * half, half), half)])


def query_kernel(near, far, wq, begun, out, notes):
    peers, rows, wide = near.shape
    half = wide - HD
    core = lax.axis_index("rep") % 2
    b = far[:, :, :half].reshape(peers * rows, half)
    q = begun[...] + dot(b, wq[0, pl.ds(pl.multiple_of((1 - core) * half, half), half)])
    marks = near[:, :, half:].reshape(peers * rows, HD)
    notes[...] = marks
    out[...] = dot(order_of(marks), q.astype(BF16)).astype(BF16).reshape(out.shape)


def own_kernel(near, far, wkv_far, sel, fresh, wkv, sems):
    pieces = sems.shape[0]
    size = wkv.shape[0] // pieces
    copies = [
        pltpu.make_async_copy(wkv_far.at[pl.ds(i * size, size)], wkv.at[pl.ds(i * size, size)], sems.at[i])
        for i in range(pieces)
    ]
    for copy in copies:
        copy.start()
    peers, rows, wide = near.shape
    half = wide - HD
    rank, core = lax.axis_index("req"), lax.axis_index("rep") % 2
    source = near[rank][:, half : half + 1]
    column = lax.broadcasted_iota(jnp.int32, (rows, peers * rows), 1)
    order = (source.astype(jnp.int32) == column).astype(BF16)
    a = dot(order, near[...].reshape(peers * rows, wide))
    b = dot(order, far[:, :, :half].reshape(peers * rows, half)).astype(BF16)
    sel[...] = a[:, half:]
    a = a[:, :half].astype(BF16)
    parts = (jnp.where(core == 0, a, b), jnp.where(core == 0, b, a))
    spans = half // HD
    chunks = [part[:, c * HD : (c + 1) * HD] for part in parts for c in range(spans)]
    twice = (HD, 2 * HD)
    feature = lax.broadcasted_iota(jnp.int32, twice, 1) // 2
    doubling = (lax.broadcasted_iota(jnp.int32, twice, 0) == feature).astype(BF16)
    doubled = dot(jnp.concatenate(chunks, axis=0), doubling)
    even = lax.broadcasted_iota(jnp.int32, (rows, 2 * HD), 1) % 2 == 0
    total = jnp.zeros(fresh.shape, F32)
    for c in range(2 * spans):
        if c * HD % size == 0:
            copies[c * HD // size].wait()
        v = doubled[c * rows : (c + 1) * rows]
        v = jnp.concatenate([jnp.where(even, v, 0.0), jnp.where(even, 0.0, v)], axis=0)
        w = wkv[c * HD : (c + 1) * HD].reshape(2 * HD, fresh.shape[1])
        total = total + dot(v.astype(BF16), w)
    fresh[...] = total.astype(BF16)


def page_kernel(
    table_far, lens_far, pool, weight, start, out, picked_far, table, lens, staged, picked, sems, back, small, pick
):
    halves, _, quarter = picked.shape
    side = 1 - lax.axis_index("rep") % 2
    picks = [
        pltpu.make_async_copy(weight.at[0, :, columns_of(z, side, quarter)], picked.at[z], pick.at[z])
        for z in range(halves)
    ]
    for copy in picks:
        copy.start()
    first = pltpu.make_async_copy(table_far, table, small.at[0])
    second = pltpu.make_async_copy(lens_far, lens, small.at[1])
    first.start()
    second.start()
    first.wait()
    second.wait()
    count = out.shape[0]
    page = pool.shape[1]
    tail = out.shape[1]
    sizes = (HEAD, MIDDLE, tail - MIDDLE)
    starts = (0, HEAD, HEAD + MIDDLE)
    places = (None, pl.ds(0, MIDDLE), pl.ds(MIDDLE, tail - MIDDLE))

    def each(act):
        for part in range(3):
            for j in range(count):
                if part < 2:
                    act(j, part)
                else:
                    pl.when(lens[j] > starts[2])(functools.partial(act, j, part))

    def block_of(j, part):
        return start.at[j] if part == 0 else staged.at[j, places[part]]

    def read(j, part):
        block = block_of(j, part)
        for p in range(sizes[part] // page):
            pltpu.make_async_copy(
                pool.at[table[j, starts[part] // page + p]],
                block.at[pl.ds(p * page, page)],
                sems.at[j, part],
            ).start()

    def write(j, part):
        return pltpu.make_async_copy(block_of(j, part), out.at[j, places[part]], back.at[j, part])

    def forward(j, part):
        block = block_of(j, part)
        pltpu.make_async_copy(block, block, sems.at[j, part]).wait()
        if part:
            write(j, part).start()

    def finish(j, part):
        if part:
            write(j, part).wait()

    each(read)
    for copy in picks:
        copy.wait()
    send = pltpu.make_async_copy(picked, picked_far, pick.at[halves])
    send.start()
    each(forward)
    each(finish)
    send.wait()


def pages_call(table, lens, pool, weight, quarter):
    mine, pages = table.shape
    length = pages * pool.shape[1]
    tail = (mine, length - HEAD) + pool.shape[2:]
    rows_shape = (weight.shape[2] // (2 * quarter), weight.shape[1], quarter)
    return call(
        page_kernel,
        [
            pltpu.VMEM((mine, HEAD) + pool.shape[2:], BF16),
            pltpu.HBM(tail, BF16),
            pltpu.HBM(rows_shape, BF16),
        ],
        [FAR] * 4,
        [
            pltpu.SMEM(table.shape, jnp.int32),
            pltpu.SMEM(lens.shape, jnp.int32),
            pltpu.VMEM(tail, BF16),
            pltpu.VMEM(rows_shape, BF16),
            pltpu.SemaphoreType.DMA((mine, 3)),
            pltpu.SemaphoreType.DMA((mine, 3)),
            pltpu.SemaphoreType.DMA((2,)),
            pltpu.SemaphoreType.DMA((rows_shape[0] + 1,)),
        ],
        outs=[VM, FAR, FAR],
    )(in_hbm(table), in_hbm(lens), in_hbm(pool), in_hbm(weight))


def attention_kernel(
    lens, sel, arrived, fresh, start, far, out, middle, cache, qs, os, sc, ef, sems, one
):
    count, rest, _, wide = cache.shape
    requests = range(count)

    def middle_of(j):
        return pltpu.make_async_copy(far.at[j, pl.ds(0, MIDDLE)], middle.at[j], one.at[j])

    for j in requests:
        middle_of(j).start()

    def copy_of(j):
        return pltpu.make_async_copy(far.at[j, pl.ds(MIDDLE, rest)], cache.at[j], sems.at[j])

    for j in requests:

        @pl.when(lens[j] > HEAD + MIDDLE)
        def _(j=j):
            copy_of(j).start()

    peers, rows, _ = arrived.shape
    heads = wide // HD
    group = 2 * heads
    inv_scale = 1.0 / math.sqrt(HD)
    picks = sel[...]
    masks = [[picks[:, 1 + k : 2 + k] == float(e) for e in range(EXPERTS)] for k in range(2)]
    for h in range(heads):
        values = [arrived[e * heads + h].astype(F32) for e in range(EXPERTS)]
        for k in range(2):
            total = jnp.where(masks[k][0], values[0], 0.0)
            for e in range(1, EXPERTS):
                total = total + jnp.where(masks[k][e], values[e], 0.0)
            qs[k * heads + h] = total
    ef[...] = jnp.zeros_like(ef)
    ef[0 : 2 * rows] = fresh[...]
    extra = ef[...]
    big = (2 * group, wide)
    block_row = lax.broadcasted_iota(jnp.int32, big, 0) % heads
    diagonal = block_row == lax.broadcasted_iota(jnp.int32, big, 1) // HD
    e_col = lax.broadcasted_iota(jnp.int32, (2 * group, HD), 1)
    e_row = lax.broadcasted_iota(jnp.int32, (2 * group, HD), 0)

    starts = (0, HEAD, HEAD + MIDDLE)

    def rows_of(j, part):
        if part == 0:
            return start[j].reshape(2 * HEAD, wide)
        if part == 1:
            return middle[j].reshape(2 * MIDDLE, wide)
        return cache[j].reshape(2 * rest, wide)

    def masked_scores(q, j, part):
        s = dot_rows(q, rows_of(j, part)) * inv_scale
        column = lax.broadcasted_iota(jnp.int32, s.shape, 1)
        return jnp.where(
            (column % 2 == 0) & (column < 2 * (lens[j] - starts[part])), s, MASKED
        )

    def highest(s):
        return jnp.max(s, axis=1, keepdims=True)

    def added(p):
        return jnp.sum(p, axis=1, keepdims=True)

    def onto_values(p, distance=1):
        return pltpu.roll(p, distance, 1).astype(BF16)

    longer = [jnp.where(lens[j] > starts[2], 1, 0) for j in requests]
    queries, extras, firsts, seconds, tops = [], [], [], [], []
    for j in requests:
        q = jnp.concatenate([qs[:, 2 * j, :], qs[:, 2 * j + 1, :]], axis=0)
        q = jnp.where(diagonal, jnp.concatenate([q] * heads, axis=1), 0.0).astype(BF16)
        live = (e_col == 2 * j) | ((e_col == 2 * j + 1) & (e_row >= group))
        queries.append(q)
        extras.append(jnp.where(live, dot_rows(q, extra) * inv_scale, MASKED))
        firsts.append(masked_scores(q, j, 0))
    for j in requests:
        middle_of(j).wait()
    for j in requests:
        seconds.append(masked_scores(queries[j], j, 1))
        top = jnp.maximum(highest(extras[j]), highest(firsts[j]))
        tops.append(jnp.maximum(top, highest(seconds[j])))

    for j in requests:

        def score(_, top, j=j):
            copy_of(j).wait()
            s = masked_scores(queries[j], j, 2)
            sc[j] = s
            return jnp.maximum(top, highest(s))

        tops[j] = lax.fori_loop(0, longer[j], score, tops[j])

    extras = [jnp.exp(extras[j] - tops[j]) for j in requests]
    firsts = [jnp.exp(firsts[j] - tops[j]) for j in requests]
    seconds = [jnp.exp(seconds[j] - tops[j]) for j in requests]
    sums = [added(extras[j]) + added(firsts[j]) + added(seconds[j]) for j in requests]
    mixed = [
        dot(onto_values(extras[j], rows), extra)
        + dot(onto_values(firsts[j]), rows_of(j, 0))
        + dot(onto_values(seconds[j]), rows_of(j, 1))
        for j in requests
    ]
    for j in requests:

        def gather(_, state, j=j):
            p = jnp.exp(sc[j] - tops[j])
            return state[0] + added(p), state[1] + dot(onto_values(p), rows_of(j, 2))

        sums[j], mixed[j] = lax.fori_loop(0, longer[j], gather, (sums[j], mixed[j]))

    for j in requests:
        kept = jnp.where(diagonal, mixed[j], 0.0)
        o = kept[:, :HD]
        for h in range(1, heads):
            o = o + kept[:, h * HD : (h + 1) * HD]
        o = o / sums[j]
        os[:, 2 * j, :] = o[:group]
        os[:, 2 * j + 1, :] = o[group:]
    for h in range(heads):
        one, two = os[h], os[heads + h]
        for e in range(EXPERTS):
            value = jnp.where(masks[0][e], one, 0.0) + jnp.where(masks[1][e], two, 0.0)
            out[e * heads + h] = value.astype(BF16)


def attention_call(lens, sel, arrived, fresh, start, cache):
    rows, wide = arrived.shape[1], cache.shape[-1]
    mine = cache.shape[0]
    rest = cache.shape[1] - MIDDLE
    pairs = 2 * wide // HD
    return call(
        attention_kernel,
        shape_of(arrived.shape),
        [SM, VM, VM, VM, VM, FAR],
        [
            pltpu.VMEM((mine, MIDDLE) + cache.shape[2:], BF16),
            pltpu.VMEM((mine, rest) + cache.shape[2:], BF16),
            pltpu.VMEM((pairs, rows, HD), F32),
            pltpu.VMEM((pairs, rows, HD), F32),
            pltpu.VMEM((mine, 2 * pairs, 2 * rest), F32),
            pltpu.VMEM((HD, wide), BF16),
            pltpu.SemaphoreType.DMA((mine,)),
            pltpu.SemaphoreType.DMA((mine,)),
        ],
        16,
    )(lens, sel, arrived, fresh, in_vmem(start), in_hbm(cache))


def columns_of(z, core, quarter):
    return pl.ds(pl.multiple_of((2 * z + core) * quarter, quarter), quarter)


def answers_of(notes, returned):
    peers, rows, wide = returned.shape
    values = returned[...].reshape(peers * rows, wide)
    return lax.dot_general(
        order_of(notes[...]), values, (((0,), (0,)), ((), ())), preferred_element_type=F32
    ).astype(BF16)


def own_part(a, weight, out):
    peers, halves, rows, quarter = out.shape
    core = lax.axis_index("rep") % 2
    for z in range(halves):
        part = dot(a, weight[0, :, columns_of(z, core, quarter)])
        out[:, z] = part.reshape(peers, rows, quarter)


def other_part(a, weight, part, out):
    peers, halves, rows, quarter = out.shape
    for z in range(halves):
        more = dot(a, weight[z]).reshape(peers, rows, quarter)
        out[:, z] = (part[:, z] + more).astype(BF16)


def project_kernel(notes, returned, weight, out):
    own_part(answers_of(notes, returned), weight, out)


def finish_project_kernel(notes, returned, weight, part, out):
    other_part(answers_of(notes, returned), weight, part, out)


def part_kernel(units, weight, out):
    own_part(units[...], weight, out)


def place_kernel(*refs):
    pieces, out = refs[:-1], refs[-1]
    rep = lax.axis_index("rep")
    count, _, width = out.shape
    quarter = width // len(pieces)
    for m, piece in enumerate(pieces):
        place = pl.multiple_of((rep ^ m) * quarter, quarter)
        out[:, :, pl.ds(place, quarter)] = piece[...].reshape(count, 2, quarter)


def raw_products(block, side, gains, wg, wu):
    peers, halves, rows, quarter = block.shape
    total = peers * rows
    squares = jnp.zeros((total, 1), F32)
    gate = jnp.zeros((total, wg.shape[1]), F32)
    up = jnp.zeros((total, wg.shape[1]), F32)
    for z in range(halves):
        where = columns_of(z, side, quarter)
        v = block[:, z].reshape(total, quarter).astype(F32)
        squares = squares + jnp.sum(v * v, axis=1, keepdims=True)
        v = (v * gains[1:2, where]).astype(BF16)
        gate = gate + dot_rows(v, wg[0, :, where])
        up = up + dot_rows(v, wu[0, :, where])
    return squares, gate, up


def near_kernel(near, gains, wg, wu, squares, gate, up):
    core = lax.axis_index("rep") % 2
    a, b, c = raw_products(near, core, gains, wg, wu)
    squares[...] = jnp.broadcast_to(a, squares.shape)
    gate[...] = b
    up[...] = c


def expert_kernel(far, gains, wg, wu, wd, near_squares, near_gate, near_up, units, theirs):
    peers, halves, rows, quarter = far.shape
    core = lax.axis_index("rep") % 2
    squares, gate, up = raw_products(far, 1 - core, gains, wg, wu)
    squares = squares + near_squares[:, :1]
    scaling = lax.rsqrt(squares / (2 * halves * quarter) + EPSILON)
    gate = (gate + near_gate[...]) * scaling
    up = (up + near_up[...]) * scaling
    a = (gate / (1.0 + jnp.exp(-gate)) * up).astype(BF16)
    units[...] = a
    for z in range(halves):
        part = dot(a, wd[0, :, columns_of(z, 1 - core, quarter)])
        theirs[:, z] = part.astype(BF16).reshape(peers, rows, quarter)


def shards(
    tokens,
    norm_gains,
    w_kv,
    w_query,
    w_out,
    w_gate,
    w_up,
    w_down,
    kv_pages,
    page_table,
    cache_len,
    route_ids,
    route_gates,
    new_slot,
):
    req_count = lax.axis_size("req")
    rep_count = lax.axis_size("rep")
    mine, _, width = tokens.shape
    rows = 2 * mine
    total = rows * req_count
    half = width // 2
    quarter = width // rep_count
    wide = kv_pages.shape[-1]
    rep = lax.axis_index("rep")
    swap = [(p, p ^ 1) for p in range(rep_count)]
    wide_groups = [
        [r * rep_count + 2 * z + c for r in range(req_count) for z in range(rep_count // 2)]
        for c in range(2)
    ]
    peers = req_count * rep_count // 2
    split = (req_count, rep_count // 2, rows, quarter)

    def spread_req(value):
        return lax.all_to_all(value, "req", split_axis=0, concat_axis=0, tiled=True)

    def spread_wide(value):
        return lax.all_to_all(
            value,
            ("req", "rep"),
            split_axis=0,
            concat_axis=0,
            tiled=True,
            axis_index_groups=wide_groups,
        )

    def other_core(value):
        return lax.ppermute(value, "rep", swap)

    inputs = tokens.reshape(rows, width)
    ids = route_ids.transpose(0, 2, 1, 3).reshape(rows, 2, 2)
    gates = route_gates.astype(F32).transpose(0, 2, 1, 3).reshape(rows, 2, 2)
    experts_row = jnp.arange(EXPERTS, dtype=jnp.int32)
    shares = jnp.sum(jnp.where(ids[..., None] == experts_row, gates[..., None], 0.0), axis=2)
    shares = shares.transpose(1, 2, 0)[..., None]
    shares = [shares[0], shares[1]]
    kept = lax.dynamic_slice_in_dim(inputs, rep * quarter, quarter, 1).astype(F32)

    routes = route_ids.transpose(1, 2, 3, 0)
    message = call(
        message_kernel,
        shape_of((req_count, rows, half + HD)),
        [FAR] * 4,
        [
            pltpu.SMEM(new_slot.shape, jnp.int32),
            pltpu.SMEM(routes.shape, jnp.int32),
            pltpu.VMEM(tokens.shape, BF16),
            pltpu.VMEM(norm_gains.shape, F32),
            pltpu.SemaphoreType.DMA((4,)),
        ],
    )(in_hbm(new_slot), in_hbm(routes), in_hbm(tokens), in_hbm(norm_gains))
    near = spread_req(message)
    start, cache, picked = pages_call(page_table, cache_len, kv_pages, w_out, quarter)
    near, start, cache, picked, shares, kept = lax.optimization_barrier(
        (near, start, cache, picked, shares, kept)
    )
    far = other_core(near)
    wq, begun = call(
        near_query_kernel,
        [pltpu.VMEM(w_query.shape, BF16), shape_of((total, HD), F32)],
        [VM, FAR],
        [pltpu.SemaphoreType.DMA],
    )(near, in_hbm(w_query))
    ordered, notes = call(
        query_kernel, [shape_of((req_count, rows, HD)), shape_of((total, HD))], [VM] * 4
    )(near, far, in_vmem(wq), begun)
    arrived = spread_req(ordered)
    sel, fresh = call(
        own_kernel,
        [shape_of((rows, HD), F32), shape_of((2 * rows, wide))],
        [VM, VM, FAR],
        [pltpu.VMEM(w_kv.shape, BF16), pltpu.SemaphoreType.DMA((8,))],
    )(near, far, in_hbm(w_kv))
    back = attention_call(cache_len, sel, arrived, fresh, start, cache)
    returned = spread_req(back)
    returned, picked = lax.optimization_barrier((returned, picked))
    returned_x, out_x = other_core(returned), other_core(picked)
    part = call(project_kernel, shape_of(split, F32), [VM] * 3)(notes, returned, w_out)
    summed = call(finish_project_kernel, shape_of(split), [VM] * 4)(
        notes, returned_x, out_x, part
    )

    def reduce_wide(summed, share):
        got = spread_wide(summed.reshape(peers, rows, quarter))
        got = got.reshape(EXPERTS, peers // EXPERTS, rows, quarter).astype(F32)
        return jnp.sum(jnp.sum(got, axis=1) * share, axis=0)

    hidden = kept + reduce_wide(summed, shares[0])
    copies = jnp.broadcast_to(hidden.astype(BF16)[None], (peers, rows, quarter))
    block = spread_wide(copies)
    far = other_core(block).reshape(split)
    wg, wu = w_gate.transpose(0, 2, 1), w_up.transpose(0, 2, 1)
    units_dev = w_down.shape[1]
    squares, gate, up = call(
        near_kernel,
        [shape_of((total, HD), F32)] + [shape_of((total, units_dev), F32)] * 2,
        [VM] * 4,
    )(block.reshape(split), norm_gains, wg, wu)
    units, theirs = call(
        expert_kernel, [shape_of((total, units_dev)), shape_of(split)], [VM] * 8
    )(far, norm_gains, wg, wu, w_down, squares, gate, up)
    theirs = other_core(theirs)
    part = call(part_kernel, shape_of(split, F32), [VM] * 2)(units, w_down)
    feed = reduce_wide((part + theirs.astype(F32)).astype(BF16), shares[1])
    piece = (hidden + feed).astype(BF16)
    pieces = [piece] + [
        lax.ppermute(piece, "rep", [(p, p ^ m) for p in range(rep_count)])
        for m in range(1, rep_count)
    ]
    return call(place_kernel, shape_of((mine, 2, width)), [VM] * rep_count)(*pieces)


def solution(mesh):
    in_specs = (
        P("req", None, None),
        P(),
        P(None, None, "rep"),
        P("req", None, "rep"),
        P("req", "rep", None),
        P("req", None, "rep"),
        P("req", None, "rep"),
        P("req", "rep", None),
        P("req", None, None, "rep"),
        P("req", None),
        P("req"),
        P("req", None, None, None),
        P("req", None, None, None),
        P("req"),
    )
    out_specs = P("req", None, None)
    return jax.shard_map(shards, mesh=mesh, in_specs=in_specs, out_specs=out_specs, check_vma=False)
```

```python
import functools
import math

import jax
import jax.numpy as jnp
from jax import lax
from jax.experimental import pallas as pl
from jax.experimental.pallas import tpu as pltpu
from jax.sharding import PartitionSpec as P

HD = 128
EXPERTS = 8
SPAN = 256
EPSILON = 1e-06
MASKED = -1e30
F32 = jnp.float32
BF16 = jnp.bfloat16
VM = pl.BlockSpec(memory_space=pltpu.VMEM)
SM = pl.BlockSpec(memory_space=pltpu.SMEM)
FAR = pl.BlockSpec(memory_space=pltpu.HBM)
ROWS_BY_ROWS = (((1,), (1,)), ((), ()))


def dot(a, b):
    return jnp.dot(a, b, preferred_element_type=F32)


def dot_rows(a, b):
    return lax.dot_general(a, b, ROWS_BY_ROWS, preferred_element_type=F32)


def call(body, out, ins, scratch=(), limit=12, outs=None):
    many = isinstance(out, (list, tuple))
    return pl.pallas_call(
        body,
        out_shape=out,
        in_specs=ins,
        out_specs=outs or ([VM] * len(out) if many else VM),
        scratch_shapes=scratch,
        compiler_params=pltpu.CompilerParams(vmem_limit_bytes=limit << 20),
    )


def in_hbm(value):
    return pltpu.with_memory_space_constraint(value, pltpu.HBM)


def in_vmem(value):
    return pltpu.with_memory_space_constraint(value, pltpu.VMEM)


def shape_of(shape, dtype=BF16):
    return jax.ShapeDtypeStruct(shape, dtype)


def message_kernel(slots_far, ids_far, tokens_far, gains_far, out, slots, ids, tokens, gains, sems):
    pairs = ((slots_far, slots), (ids_far, ids), (tokens_far, tokens), (gains_far, gains))
    copies = [pltpu.make_async_copy(a, b, sems.at[i]) for i, (a, b) in enumerate(pairs)]
    for copy in copies:
        copy.start()
    for copy in copies:
        copy.wait()
    count, _, width = tokens.shape
    rows = 2 * count
    half = width // 2
    rank, core = lax.axis_index("req"), lax.axis_index("rep") % 2
    x = tokens[...].reshape(rows, width).astype(F32)
    scaling = lax.rsqrt(jnp.mean(x * x, axis=1, keepdims=True) + EPSILON)
    normed = (x * scaling * gains[0:1]).astype(BF16)
    out[0, :, :half] = jnp.where(core == 0, normed[:, :half], normed[:, half:])
    row = lax.broadcasted_iota(jnp.int32, (rows, HD), 0)
    lane = lax.broadcasted_iota(jnp.int32, (rows, HD), 1)
    notes = jnp.zeros((rows, HD), jnp.int32)
    for j in range(count):
        for s in range(2):
            here = row == 2 * j + s
            source = 2 * (rank * count + j) if s == 0 else 2 * slots[j] + 1
            notes = jnp.where(here & (lane == 0), source, notes)
            for k in range(2):
                notes = jnp.where(here & (lane == 1 + k), ids[0, s, k, j], notes)
    out[0, :, half:] = notes.astype(F32).astype(BF16)
    message = out[0]
    for r in range(1, out.shape[0]):
        out[r] = message


def order_of(notes):
    source = notes[:, :1]
    column = lax.broadcasted_iota(jnp.int32, (notes.shape[0], notes.shape[0]), 1)
    return (source.astype(jnp.int32) == column).astype(BF16)


def near_query_kernel(near, wq_far, wq, out, sem):
    load = pltpu.make_async_copy(wq_far, wq, sem)
    load.start()
    peers, rows, wide = near.shape
    half = wide - HD
    core = lax.axis_index("rep") % 2
    a = near[:, :, :half].reshape(peers * rows, half)
    load.wait()
    out[...] = dot(a, wq[0, pl.ds(pl.multiple_of(core * half, half), half)])


def query_kernel(near, far, wq, begun, out, notes):
    peers, rows, wide = near.shape
    half = wide - HD
    core = lax.axis_index("rep") % 2
    b = far[:, :, :half].reshape(peers * rows, half)
    q = begun[...] + dot(b, wq[0, pl.ds(pl.multiple_of((1 - core) * half, half), half)])
    marks = near[:, :, half:].reshape(peers * rows, HD)
    notes[...] = marks
    out[...] = dot(order_of(marks), q.astype(BF16)).astype(BF16).reshape(out.shape)


def own_kernel(near, far, wkv_far, sel, fresh, wkv, sems):
    pieces = sems.shape[0]
    size = wkv.shape[0] // pieces
    copies = [
        pltpu.make_async_copy(wkv_far.at[pl.ds(i * size, size)], wkv.at[pl.ds(i * size, size)], sems.at[i])
        for i in range(pieces)
    ]
    for copy in copies:
        copy.start()
    peers, rows, wide = near.shape
    half = wide - HD
    rank, core = lax.axis_index("req"), lax.axis_index("rep") % 2
    source = near[rank][:, half : half + 1]
    column = lax.broadcasted_iota(jnp.int32, (rows, peers * rows), 1)
    order = (source.astype(jnp.int32) == column).astype(BF16)
    a = dot(order, near[...].reshape(peers * rows, wide))
    b = dot(order, far[:, :, :half].reshape(peers * rows, half)).astype(BF16)
    sel[...] = a[:, half:]
    a = a[:, :half].astype(BF16)
    parts = (jnp.where(core == 0, a, b), jnp.where(core == 0, b, a))
    spans = half // HD
    chunks = [part[:, c * HD : (c + 1) * HD] for part in parts for c in range(spans)]
    twice = (HD, 2 * HD)
    feature = lax.broadcasted_iota(jnp.int32, twice, 1) // 2
    doubling = (lax.broadcasted_iota(jnp.int32, twice, 0) == feature).astype(BF16)
    doubled = dot(jnp.concatenate(chunks, axis=0), doubling)
    even = lax.broadcasted_iota(jnp.int32, (rows, 2 * HD), 1) % 2 == 0
    total = jnp.zeros(fresh.shape, F32)
    for c in range(2 * spans):
        if c * HD % size == 0:
            copies[c * HD // size].wait()
        v = doubled[c * rows : (c + 1) * rows]
        v = jnp.concatenate([jnp.where(even, v, 0.0), jnp.where(even, 0.0, v)], axis=0)
        w = wkv[c * HD : (c + 1) * HD].reshape(2 * HD, fresh.shape[1])
        total = total + dot(v.astype(BF16), w)
    fresh[...] = total.astype(BF16)


def page_kernel(
    table_far, lens_far, pool, weight, start, out, picked_far, table, lens, staged, picked, sems, back, small, pick
):
    halves, _, quarter = picked.shape
    side = 1 - lax.axis_index("rep") % 2
    picks = [
        pltpu.make_async_copy(weight.at[0, :, columns_of(z, side, quarter)], picked.at[z], pick.at[z])
        for z in range(halves)
    ]
    for copy in picks:
        copy.start()
    first = pltpu.make_async_copy(table_far, table, small.at[0])
    second = pltpu.make_async_copy(lens_far, lens, small.at[1])
    first.start()
    second.start()
    first.wait()
    second.wait()
    count = out.shape[0]
    page = pool.shape[1]
    chunks = 1 + out.shape[1] // SPAN

    def each(act):
        for c in range(chunks):
            for j in range(count):
                if c < 2:
                    act(j, c)
                else:
                    pl.when(lens[j] > 2 * SPAN)(functools.partial(act, j, c))

    def block_of(j, c):
        return start.at[j] if c == 0 else staged.at[j, pl.ds((c - 1) * SPAN, SPAN)]

    def read(j, c):
        block = block_of(j, c)
        for p in range(SPAN // page):
            pltpu.make_async_copy(
                pool.at[table[j, c * (SPAN // page) + p]],
                block.at[pl.ds(p * page, page)],
                sems.at[j, c],
            ).start()

    def write(j, c):
        place = out.at[j, pl.ds((c - 1) * SPAN, SPAN)]
        return pltpu.make_async_copy(block_of(j, c), place, back.at[j, c])

    def forward(j, c):
        block = block_of(j, c)
        pltpu.make_async_copy(block, block, sems.at[j, c]).wait()
        if c:
            write(j, c).start()

    def finish(j, c):
        if c:
            write(j, c).wait()

    each(read)
    for copy in picks:
        copy.wait()
    send = pltpu.make_async_copy(picked, picked_far, pick.at[halves])
    send.start()
    each(forward)
    each(finish)
    send.wait()


def pages_call(table, lens, pool, weight, quarter):
    mine, pages = table.shape
    length = pages * pool.shape[1]
    tail = (mine, length - SPAN) + pool.shape[2:]
    rows_shape = (weight.shape[2] // (2 * quarter), weight.shape[1], quarter)
    return call(
        page_kernel,
        [
            pltpu.VMEM((mine, SPAN) + pool.shape[2:], BF16),
            pltpu.HBM(tail, BF16),
            pltpu.HBM(rows_shape, BF16),
        ],
        [FAR] * 4,
        [
            pltpu.SMEM(table.shape, jnp.int32),
            pltpu.SMEM(lens.shape, jnp.int32),
            pltpu.VMEM(tail, BF16),
            pltpu.VMEM(rows_shape, BF16),
            pltpu.SemaphoreType.DMA((mine, length // SPAN)),
            pltpu.SemaphoreType.DMA((mine, length // SPAN)),
            pltpu.SemaphoreType.DMA((2,)),
            pltpu.SemaphoreType.DMA((rows_shape[0] + 1,)),
        ],
        outs=[VM, FAR, FAR],
    )(in_hbm(table), in_hbm(lens), in_hbm(pool), in_hbm(weight))


def attention_kernel(lens, sel, arrived, fresh, start, far, out, cache, qs, os, sc, ef, sems):
    count, tail, _, wide = cache.shape
    requests = range(count)
    spans = (pl.ds(0, SPAN), pl.ds(SPAN, tail - SPAN))

    def copy_of(j, part):
        span = spans[part]
        return pltpu.make_async_copy(far.at[j, span], cache.at[j, span], sems.at[j, part])

    for j in requests:
        copy_of(j, 0).start()
    for j in requests:

        @pl.when(lens[j] > 2 * SPAN)
        def _(j=j):
            copy_of(j, 1).start()

    peers, rows, _ = arrived.shape
    heads = wide // HD
    group = 2 * heads
    inv_scale = 1.0 / math.sqrt(HD)
    picks = sel[...]
    masks = [[picks[:, 1 + k : 2 + k] == float(e) for e in range(EXPERTS)] for k in range(2)]
    for h in range(heads):
        values = [arrived[e * heads + h].astype(F32) for e in range(EXPERTS)]
        for k in range(2):
            total = jnp.where(masks[k][0], values[0], 0.0)
            for e in range(1, EXPERTS):
                total = total + jnp.where(masks[k][e], values[e], 0.0)
            qs[k * heads + h] = total
    ef[...] = jnp.zeros_like(ef)
    ef[0 : 2 * rows] = fresh[...]
    extra = ef[...]
    big = (2 * group, wide)
    block_row = lax.broadcasted_iota(jnp.int32, big, 0) % heads
    diagonal = block_row == lax.broadcasted_iota(jnp.int32, big, 1) // HD
    e_col = lax.broadcasted_iota(jnp.int32, (2 * group, HD), 1)
    e_row = lax.broadcasted_iota(jnp.int32, (2 * group, HD), 0)

    def rows_of(j, part):
        if part == 0:
            return start[j].reshape(2 * SPAN, wide)
        if part == 1:
            return cache[j, :SPAN].reshape(2 * SPAN, wide)
        return cache[j, SPAN:].reshape(2 * (tail - SPAN), wide)

    def masked_scores(q, j, part):
        s = dot_rows(q, rows_of(j, part)) * inv_scale
        column = lax.broadcasted_iota(jnp.int32, s.shape, 1)
        return jnp.where(
            (column % 2 == 0) & (column < 2 * (lens[j] - part * SPAN)), s, MASKED
        )

    def highest(s):
        return jnp.max(s, axis=1, keepdims=True)

    def added(p):
        return jnp.sum(p, axis=1, keepdims=True)

    def onto_values(p, distance=1):
        return pltpu.roll(p, distance, 1).astype(BF16)

    longer = [jnp.where(lens[j] > 2 * SPAN, 1, 0) for j in requests]
    queries, extras, firsts, seconds, tops = [], [], [], [], []
    for j in requests:
        q = jnp.concatenate([qs[:, 2 * j, :], qs[:, 2 * j + 1, :]], axis=0)
        q = jnp.where(diagonal, jnp.concatenate([q] * heads, axis=1), 0.0).astype(BF16)
        live = (e_col == 2 * j) | ((e_col == 2 * j + 1) & (e_row >= group))
        queries.append(q)
        extras.append(jnp.where(live, dot_rows(q, extra) * inv_scale, MASKED))
        firsts.append(masked_scores(q, j, 0))
    for j in requests:
        copy_of(j, 0).wait()
    for j in requests:
        seconds.append(masked_scores(queries[j], j, 1))
        top = jnp.maximum(highest(extras[j]), highest(firsts[j]))
        tops.append(jnp.maximum(top, highest(seconds[j])))

    for j in requests:

        def score(_, top, j=j):
            copy_of(j, 1).wait()
            s = masked_scores(queries[j], j, 2)
            sc[j] = s
            return jnp.maximum(top, highest(s))

        tops[j] = lax.fori_loop(0, longer[j], score, tops[j])

    extras = [jnp.exp(extras[j] - tops[j]) for j in requests]
    firsts = [jnp.exp(firsts[j] - tops[j]) for j in requests]
    seconds = [jnp.exp(seconds[j] - tops[j]) for j in requests]
    sums = [added(extras[j]) + added(firsts[j]) + added(seconds[j]) for j in requests]
    mixed = [
        dot(onto_values(extras[j], rows), extra)
        + dot(onto_values(firsts[j]), rows_of(j, 0))
        + dot(onto_values(seconds[j]), rows_of(j, 1))
        for j in requests
    ]
    for j in requests:

        def gather(_, state, j=j):
            p = jnp.exp(sc[j] - tops[j])
            return state[0] + added(p), state[1] + dot(onto_values(p), rows_of(j, 2))

        sums[j], mixed[j] = lax.fori_loop(0, longer[j], gather, (sums[j], mixed[j]))

    for j in requests:
        kept = jnp.where(diagonal, mixed[j], 0.0)
        o = kept[:, :HD]
        for h in range(1, heads):
            o = o + kept[:, h * HD : (h + 1) * HD]
        o = o / sums[j]
        os[:, 2 * j, :] = o[:group]
        os[:, 2 * j + 1, :] = o[group:]
    for h in range(heads):
        one, two = os[h], os[heads + h]
        for e in range(EXPERTS):
            value = jnp.where(masks[0][e], one, 0.0) + jnp.where(masks[1][e], two, 0.0)
            out[e * heads + h] = value.astype(BF16)


def attention_call(lens, sel, arrived, fresh, start, cache):
    rows, wide = arrived.shape[1], cache.shape[-1]
    mine, tail = cache.shape[:2]
    pairs = 2 * wide // HD
    return call(
        attention_kernel,
        shape_of(arrived.shape),
        [SM, VM, VM, VM, VM, FAR],
        [
            pltpu.VMEM(cache.shape, BF16),
            pltpu.VMEM((pairs, rows, HD), F32),
            pltpu.VMEM((pairs, rows, HD), F32),
            pltpu.VMEM((mine, 2 * pairs, 2 * (tail - SPAN)), F32),
            pltpu.VMEM((HD, wide), BF16),
            pltpu.SemaphoreType.DMA((mine, 2)),
        ],
        16,
    )(lens, sel, arrived, fresh, in_vmem(start), in_hbm(cache))


def columns_of(z, core, quarter):
    return pl.ds(pl.multiple_of((2 * z + core) * quarter, quarter), quarter)


def answers_of(notes, returned):
    peers, rows, wide = returned.shape
    values = returned[...].reshape(peers * rows, wide)
    return lax.dot_general(
        order_of(notes[...]), values, (((0,), (0,)), ((), ())), preferred_element_type=F32
    ).astype(BF16)


def own_part(a, weight, out):
    peers, halves, rows, quarter = out.shape
    core = lax.axis_index("rep") % 2
    for z in range(halves):
        part = dot(a, weight[0, :, columns_of(z, core, quarter)])
        out[:, z] = part.reshape(peers, rows, quarter)


def other_part(a, weight, part, out):
    peers, halves, rows, quarter = out.shape
    for z in range(halves):
        more = dot(a, weight[z]).reshape(peers, rows, quarter)
        out[:, z] = (part[:, z] + more).astype(BF16)


def project_kernel(notes, returned, weight, out):
    own_part(answers_of(notes, returned), weight, out)


def finish_project_kernel(notes, returned, weight, part, out):
    other_part(answers_of(notes, returned), weight, part, out)


def part_kernel(units, weight, out):
    own_part(units[...], weight, out)


def place_kernel(*refs):
    pieces, out = refs[:-1], refs[-1]
    rep = lax.axis_index("rep")
    count, _, width = out.shape
    quarter = width // len(pieces)
    for m, piece in enumerate(pieces):
        place = pl.multiple_of((rep ^ m) * quarter, quarter)
        out[:, :, pl.ds(place, quarter)] = piece[...].reshape(count, 2, quarter)


def raw_products(block, side, gains, wg, wu):
    peers, halves, rows, quarter = block.shape
    total = peers * rows
    squares = jnp.zeros((total, 1), F32)
    gate = jnp.zeros((total, wg.shape[1]), F32)
    up = jnp.zeros((total, wg.shape[1]), F32)
    for z in range(halves):
        where = columns_of(z, side, quarter)
        v = block[:, z].reshape(total, quarter).astype(F32)
        squares = squares + jnp.sum(v * v, axis=1, keepdims=True)
        v = (v * gains[1:2, where]).astype(BF16)
        gate = gate + dot_rows(v, wg[0, :, where])
        up = up + dot_rows(v, wu[0, :, where])
    return squares, gate, up


def near_kernel(near, gains, wg, wu, squares, gate, up):
    core = lax.axis_index("rep") % 2
    a, b, c = raw_products(near, core, gains, wg, wu)
    squares[...] = jnp.broadcast_to(a, squares.shape)
    gate[...] = b
    up[...] = c


def expert_kernel(far, gains, wg, wu, wd, near_squares, near_gate, near_up, units, theirs):
    peers, halves, rows, quarter = far.shape
    core = lax.axis_index("rep") % 2
    squares, gate, up = raw_products(far, 1 - core, gains, wg, wu)
    squares = squares + near_squares[:, :1]
    scaling = lax.rsqrt(squares / (2 * halves * quarter) + EPSILON)
    gate = (gate + near_gate[...]) * scaling
    up = (up + near_up[...]) * scaling
    a = (gate / (1.0 + jnp.exp(-gate)) * up).astype(BF16)
    units[...] = a
    for z in range(halves):
        part = dot(a, wd[0, :, columns_of(z, 1 - core, quarter)])
        theirs[:, z] = part.astype(BF16).reshape(peers, rows, quarter)


def shards(
    tokens,
    norm_gains,
    w_kv,
    w_query,
    w_out,
    w_gate,
    w_up,
    w_down,
    kv_pages,
    page_table,
    cache_len,
    route_ids,
    route_gates,
    new_slot,
):
    req_count = lax.axis_size("req")
    rep_count = lax.axis_size("rep")
    mine, _, width = tokens.shape
    rows = 2 * mine
    total = rows * req_count
    half = width // 2
    quarter = width // rep_count
    wide = kv_pages.shape[-1]
    rep = lax.axis_index("rep")
    swap = [(p, p ^ 1) for p in range(rep_count)]
    wide_groups = [
        [r * rep_count + 2 * z + c for r in range(req_count) for z in range(rep_count // 2)]
        for c in range(2)
    ]
    peers = req_count * rep_count // 2
    split = (req_count, rep_count // 2, rows, quarter)

    def spread_req(value):
        return lax.all_to_all(value, "req", split_axis=0, concat_axis=0, tiled=True)

    def spread_wide(value):
        return lax.all_to_all(
            value,
            ("req", "rep"),
            split_axis=0,
            concat_axis=0,
            tiled=True,
            axis_index_groups=wide_groups,
        )

    def other_core(value):
        return lax.ppermute(value, "rep", swap)

    inputs = tokens.reshape(rows, width)
    ids = route_ids.transpose(0, 2, 1, 3).reshape(rows, 2, 2)
    gates = route_gates.astype(F32).transpose(0, 2, 1, 3).reshape(rows, 2, 2)
    experts_row = jnp.arange(EXPERTS, dtype=jnp.int32)
    shares = jnp.sum(jnp.where(ids[..., None] == experts_row, gates[..., None], 0.0), axis=2)
    shares = shares.transpose(1, 2, 0)[..., None]
    shares = [shares[0], shares[1]]
    kept = lax.dynamic_slice_in_dim(inputs, rep * quarter, quarter, 1).astype(F32)

    routes = route_ids.transpose(1, 2, 3, 0)
    message = call(
        message_kernel,
        shape_of((req_count, rows, half + HD)),
        [FAR] * 4,
        [
            pltpu.SMEM(new_slot.shape, jnp.int32),
            pltpu.SMEM(routes.shape, jnp.int32),
            pltpu.VMEM(tokens.shape, BF16),
            pltpu.VMEM(norm_gains.shape, F32),
            pltpu.SemaphoreType.DMA((4,)),
        ],
    )(in_hbm(new_slot), in_hbm(routes), in_hbm(tokens), in_hbm(norm_gains))
    near = spread_req(message)
    start, cache, picked = pages_call(page_table, cache_len, kv_pages, w_out, quarter)
    near, start, cache, picked, shares, kept = lax.optimization_barrier(
        (near, start, cache, picked, shares, kept)
    )
    far = other_core(near)
    wq, begun = call(
        near_query_kernel,
        [pltpu.VMEM(w_query.shape, BF16), shape_of((total, HD), F32)],
        [VM, FAR],
        [pltpu.SemaphoreType.DMA],
    )(near, in_hbm(w_query))
    ordered, notes = call(
        query_kernel, [shape_of((req_count, rows, HD)), shape_of((total, HD))], [VM] * 4
    )(near, far, in_vmem(wq), begun)
    arrived = spread_req(ordered)
    sel, fresh = call(
        own_kernel,
        [shape_of((rows, HD), F32), shape_of((2 * rows, wide))],
        [VM, VM, FAR],
        [pltpu.VMEM(w_kv.shape, BF16), pltpu.SemaphoreType.DMA((8,))],
    )(near, far, in_hbm(w_kv))
    back = attention_call(cache_len, sel, arrived, fresh, start, cache)
    returned = spread_req(back)
    returned, picked = lax.optimization_barrier((returned, picked))
    returned_x, out_x = other_core(returned), other_core(picked)
    part = call(project_kernel, shape_of(split, F32), [VM] * 3)(notes, returned, w_out)
    summed = call(finish_project_kernel, shape_of(split), [VM] * 4)(
        notes, returned_x, out_x, part
    )

    def reduce_wide(summed, share):
        got = spread_wide(summed.reshape(peers, rows, quarter))
        got = got.reshape(EXPERTS, peers // EXPERTS, rows, quarter).astype(F32)
        return jnp.sum(jnp.sum(got, axis=1) * share, axis=0)

    hidden = kept + reduce_wide(summed, shares[0])
    copies = jnp.broadcast_to(hidden.astype(BF16)[None], (peers, rows, quarter))
    block = spread_wide(copies)
    far = other_core(block).reshape(split)
    wg, wu = w_gate.transpose(0, 2, 1), w_up.transpose(0, 2, 1)
    units_dev = w_down.shape[1]
    squares, gate, up = call(
        near_kernel,
        [shape_of((total, HD), F32)] + [shape_of((total, units_dev), F32)] * 2,
        [VM] * 4,
    )(block.reshape(split), norm_gains, wg, wu)
    units, theirs = call(
        expert_kernel, [shape_of((total, units_dev)), shape_of(split)], [VM] * 8
    )(far, norm_gains, wg, wu, w_down, squares, gate, up)
    theirs = other_core(theirs)
    part = call(part_kernel, shape_of(split, F32), [VM] * 2)(units, w_down)
    feed = reduce_wide((part + theirs.astype(F32)).astype(BF16), shares[1])
    piece = (hidden + feed).astype(BF16)
    pieces = [piece] + [
        lax.ppermute(piece, "rep", [(p, p ^ m) for p in range(rep_count)])
        for m in range(1, rep_count)
    ]
    return call(place_kernel, shape_of((mine, 2, width)), [VM] * rep_count)(*pieces)


def solution(mesh):
    in_specs = (
        P("req", None, None),
        P(),
        P(None, None, "rep"),
        P("req", None, "rep"),
        P("req", "rep", None),
        P("req", None, "rep"),
        P("req", None, "rep"),
        P("req", "rep", None),
        P("req", None, None, "rep"),
        P("req", None),
        P("req"),
        P("req", None, None, None),
        P("req", None, None, None),
        P("req"),
    )
    out_specs = P("req", None, None)
    return jax.shard_map(shards, mesh=mesh, in_specs=in_specs, out_specs=out_specs, check_vma=False)
```
